32 devices in a mesh: section: 2 (over core), ctx: 4 (over y, x), tensor: 4 (over z).
Axes of the slice: x: 2, y: 2, z: 4, core: 2. Of those that a mesh axis runs over, the one named last changes fastest.
Arguments:
- x_in: bfloat16 [2, 512, 2048], P(None, 'ctx'), may hold values from -6 to 6
- cotangent: float32 [2, 512, 2048], P(None, 'ctx'), may hold values from -6 to 6
- block_pos: int32 [2, 8], replicated, may hold values from 0 to 7, each once within a row
- norm1_gain: bfloat16 [2, 2048], P('section', 'ctx'), may hold values from 0.5 to 1.5
- norm1_bias: bfloat16 [2, 2048], P('section', 'ctx'), may hold values from -3 to 3
- norm2_gain: bfloat16 [2, 2048], P('section', 'ctx'), may hold values from 0.5 to 1.5
- norm2_bias: bfloat16 [2, 2048], P('section', 'ctx'), may hold values from -3 to 3
- qkv_weight: bfloat16 [2, 2048, 3, 8, 256], P('section', 'ctx', None, 'tensor'), may hold values from -0.125 to 0.125
- qkv_bias: bfloat16 [2, 3, 8, 256], P('section', None, 'tensor', 'ctx'), may hold values from -3 to 3
- dense_weight: bfloat16 [2, 8, 256, 2048], P('section', 'tensor', None, 'ctx'), may hold values from -1 to 1
- dense_bias: bfloat16 [2, 2048], P('section', 'ctx'), may hold values from -3 to 3
- fc1_weight: bfloat16 [2, 2048, 8192], P('section', 'ctx', 'tensor'), may hold values from -0.125 to 0.125
- fc1_bias: bfloat16 [2, 4, 2048], P('section', 'tensor', 'ctx'), may hold values from -3 to 3
- fc2_weight: bfloat16 [2, 8192, 2048], P('section', 'tensor', 'ctx'), may hold values from -0.0625 to 0.0625
- fc2_bias: bfloat16 [2, 2048], P('section', 'ctx'), may hold values from -3 to 3
Outputs:
- boundary: float32 [2, 2, 512, 2048], P('section', None, 'ctx', 'tensor')
- grad_norm1_gain: float32 [2, 2048], P('section', 'ctx')
- grad_norm1_bias: float32 [2, 2048], P('section', 'ctx')
- grad_norm2_gain: float32 [2, 2048], P('section', 'ctx')
- grad_norm2_bias: float32 [2, 2048], P('section', 'ctx')
- grad_qkv_weight: float32 [2, 2048, 3, 8, 256], P('section', 'ctx', None, 'tensor')
- grad_qkv_bias: float32 [2, 3, 8, 256], P('section', None, 'tensor', 'ctx')
- grad_dense_weight: float32 [2, 8, 256, 2048], P('section', 'tensor', None, 'ctx')
- grad_dense_bias: float32 [2, 2048], P('section', 'ctx')
- grad_fc1_weight: float32 [2, 2048, 8192], P('section', 'ctx', 'tensor')
- grad_fc1_bias: float32 [2, 4, 2048], P('section', 'tensor', 'ctx')
- grad_fc2_weight: float32 [2, 8192, 2048], P('section', 'tensor', 'ctx')
- grad_fc2_bias: float32 [2, 2048], P('section', 'ctx')
The draws below stay inside these ranges and needn't reach their ends.
Inputs may be any that keep to these rules, and one draw needn't show every extreme that they name: Each row is a permutation: slot block j of micro-batch m holds the tokens at positions block_pos[m, j] * 64 to block_pos[m, j] * 64 + 63 of its sequence.
All inputs are finite; a program needn't handle non-finite values.
Results may differ from the reference program's by a relative error of at most 0.024.
Values may be sent and summed in bfloat16 or wider, within the bound.
No kernel may reach another device: no remote copies, remote signals or barrier semaphores. Data moves between devices by JAX's collectives and lax.ppermute only.
A program may use at most 320 MiB of HBM per device.

```python
import math
import jax
import jax.numpy as jnp
from jax import lax

D = 2048
HEADS = 8
HD = 256
ROT = 64
FF = 8192
MB = 2
LAYERS = 2
LEN = 512
BLK = 64
NBLK = 8
N_TENSOR = 4


def steps_of(stream_key, shape, pieces, least, largest):
    factor_of, own = 1.0, jax.random.fold_in(stream_key, 6)
    for dim, blocks in pieces:
        steps = jnp.exp(jax.random.uniform(jax.random.fold_in(own, dim), (blocks,), jnp.float32, least / len(pieces), largest / len(pieces)))
        factor_of = factor_of * jnp.repeat(steps, shape[dim] // blocks).reshape([-1 if axis == dim else 1 for axis in range(len(shape))])
    return factor_of


def gaussian(stream_key, extent, spread, limit, cuts=(), kind=jnp.bfloat16):
    drawn = jax.random.normal(stream_key, extent, jnp.float32) * spread
    if len(cuts) > 0:
        drawn = steps_of(stream_key, extent, cuts, -0.22, 0.18) * drawn
    return jnp.clip(drawn, min=-limit, max=limit).astype(kind)


def setup_inputs(seed: int = 0) -> dict:
    keys = jax.random.split(jax.random.key(seed), 16)
    return {
        "x_in": gaussian(keys[0], (MB, LEN, D), 1.0, 6.0, ((1, 4),)),
        "cotangent": gaussian(keys[1], (MB, LEN, D), 1.0, 6.0, ((1, 4),), jnp.float32),
        "block_pos": jax.vmap(lambda own: jax.random.permutation(own, NBLK))(jax.random.split(keys[2], MB)).reshape((MB, NBLK)).astype(jnp.int32),
        "norm1_gain": jnp.clip(1.0 + 0.1 * jax.random.normal(keys[3], (LAYERS, D), jnp.float32), 0.5, 1.5).astype(jnp.bfloat16),
        "norm1_bias": gaussian(keys[4], (LAYERS, D), 0.5, 3.0, ((0, 2), (1, 4))),
        "norm2_gain": jnp.clip(1.0 + 0.1 * jax.random.normal(keys[5], (LAYERS, D), jnp.float32), 0.5, 1.5).astype(jnp.bfloat16),
        "norm2_bias": gaussian(keys[6], (LAYERS, D), 0.5, 3.0, ((0, 2), (1, 4))),
        "qkv_weight": gaussian(keys[7], (LAYERS, D, 3, HEADS, HD), D ** -0.5, 0.125, ((0, 2), (1, 4), (3, 4))),
        "qkv_bias": gaussian(keys[8], (LAYERS, 3, HEADS, HD), 0.5, 3.0, ((0, 2), (2, 4), (3, 4))),
        "dense_weight": gaussian(keys[9], (LAYERS, HEADS, HD, D), (max(HEADS * HD // 64, 1)) ** -0.5, 1.0, ((0, 2), (1, 4), (3, 4))),
        "dense_bias": gaussian(keys[10], (LAYERS, D), 0.5, 3.0, ((0, 2), (1, 4))),
        "fc1_weight": gaussian(keys[11], (LAYERS, D, FF), D ** -0.5, 0.125, ((0, 2), (1, 4), (2, 4))),
        "fc1_bias": gaussian(keys[12], (LAYERS, N_TENSOR, FF // N_TENSOR), 0.5, 3.0, ((0, 2), (1, 4), (2, 4))),
        "fc2_weight": gaussian(keys[13], (LAYERS, FF, D), FF ** -0.5, 0.0625, ((0, 2), (1, 4), (2, 4))),
        "fc2_bias": gaussian(keys[14], (LAYERS, D), 0.5, 3.0, ((0, 2), (1, 4))),
    }


EPS = 1e-05
MASKED_SCORE = -1e+30

def round_trip(to_round):
    return lax.optimization_barrier(to_round.astype(jnp.bfloat16)).astype(jnp.float32)

def slot_positions(order_row):
    offsets = jnp.arange(BLK, dtype=jnp.int32)
    return (order_row[:, None] * BLK + offsets[None, :]).reshape(LEN).astype(jnp.int32)

def rotary_tables(positions):
    halfway = ROT // 2
    inverse = 10000.0 ** (-(jnp.arange(halfway, dtype=jnp.float32) * 2.0 / ROT))
    angles = positions.astype(jnp.float32)[:, None] * inverse[None, :]
    angles = jnp.concatenate([angles, angles], axis=-1)
    return (jnp.cos(angles), jnp.sin(angles))

def rotate_heads(tensor_in, cosine, sine_table):
    halfway = ROT // 2
    leading = tensor_in[..., :ROT]
    turned = jnp.concatenate([-leading[..., halfway:], leading[..., :halfway]], axis=-1)
    rotated = leading * cosine[:, None, :] + turned * sine_table[:, None, :]
    return jnp.concatenate([rotated, tensor_in[..., ROT:]], axis=-1)

def unrotate_heads(grad_in, cosine, sine_table):
    halfway = ROT // 2
    leading = grad_in[..., :ROT]
    scaled = leading * sine_table[:, None, :]
    turned = jnp.concatenate([scaled[..., halfway:], -scaled[..., :halfway]], axis=-1)
    return jnp.concatenate([leading * cosine[:, None, :] + turned, grad_in[..., ROT:]], axis=-1)

def norm_stats(hidden):
    centre = hidden - lax.optimization_barrier(jnp.mean(hidden, axis=-1, keepdims=True))
    inv_std = lax.rsqrt(lax.optimization_barrier(jnp.mean(centre * centre, axis=-1, keepdims=True)) + EPS)
    return (centre * inv_std, inv_std)

def norm_grad(upstream, normed, inv_std):
    return inv_std * (upstream - lax.optimization_barrier(jnp.mean(upstream, axis=-1, keepdims=True)) - normed * lax.optimization_barrier(jnp.mean(upstream * normed, axis=-1, keepdims=True)))

def gelu_slope(pre_act):
    return 0.5 * (1.0 + lax.erf(pre_act * 0.7071067811865476)) + pre_act * jnp.exp(-0.5 * pre_act * pre_act) * 0.3989422804014327

def attend_forward(queries, keys_rot, values, positions):
    scaling = HD ** (-0.5)
    block_rows = math.gcd(LEN, 512)
    block_count = LEN // block_rows
    keys_wide = keys_rot.astype(jnp.float32)
    values_wide = values.astype(jnp.float32)

    def one_block(inputs):
        query_part, part_pos = inputs
        scores = jnp.einsum('qhd,khd->hqk', query_part.astype(jnp.float32), keys_wide) * scaling
        allowed = (part_pos[:, None] >= positions[None, :])[None]
        scores = jnp.where(allowed, scores, MASKED_SCORE)
        row_max = lax.optimization_barrier(jnp.max(scores, axis=-1, keepdims=True))
        exp_scores = jnp.where(allowed, jnp.exp(scores - row_max), 0.0)
        row_total = lax.optimization_barrier(jnp.sum(exp_scores, axis=-1, keepdims=True))
        weighted = jnp.einsum('hqk,khd->hqd', round_trip(exp_scores), values_wide)
        output = jnp.transpose(weighted / row_total, (1, 0, 2)).astype(jnp.bfloat16)
        return (output, (row_max + jnp.log(row_total))[..., 0])
    results, log_parts = lax.map(one_block, (queries.reshape(block_count, block_rows, HEADS, HD), positions.reshape(block_count, block_rows)))
    return (results.reshape(LEN, HEADS, HD), jnp.transpose(log_parts, (1, 0, 2)).reshape(HEADS, LEN))

def attend_backward(queries, keys_rot, values, positions, grad_attn, attn_out, log_totals):
    scaling = HD ** (-0.5)
    block_rows = math.gcd(LEN, 512)
    block_count = LEN // block_rows
    keys_wide = keys_rot.astype(jnp.float32)
    values_wide = values.astype(jnp.float32)
    row_dot = lax.optimization_barrier(jnp.sum(grad_attn.astype(jnp.float32) * attn_out.astype(jnp.float32), axis=-1))
    log_blocks = jnp.transpose(log_totals.reshape(HEADS, block_count, block_rows), (1, 0, 2))
    dot_blocks = jnp.transpose(row_dot.reshape(block_count, block_rows, HEADS), (0, 2, 1))

    def one_block(running, inputs):
        query_part, part_pos, grad_part, log_part, dot_part = inputs
        query_wide = query_part.astype(jnp.float32)
        grad_wide = grad_part.astype(jnp.float32)
        scores = jnp.einsum('qhd,khd->hqk', query_wide, keys_wide) * scaling
        allowed = (part_pos[:, None] >= positions[None, :])[None]
        scores = jnp.where(allowed, scores, MASKED_SCORE)
        probability = jnp.where(allowed, jnp.exp(scores - log_part[..., None]), 0.0)
        grad_v = running[1] + jnp.einsum('hqk,qhd->khd', round_trip(probability), grad_wide)
        d_prob = jnp.einsum('qhd,khd->hqk', grad_wide, values_wide)
        d_score = round_trip(probability * (d_prob - dot_part[..., None]))
        grad_q = jnp.einsum('hqk,khd->qhd', d_score, keys_wide) * scaling
        grad_k = running[0] + jnp.einsum('hqk,qhd->khd', d_score, query_wide) * scaling
        return ((grad_k, grad_v), grad_q)
    zero_grads = jnp.zeros((LEN, HEADS, HD), jnp.float32)
    (grad_k, grad_v), grad_q = lax.scan(one_block, (zero_grads, zero_grads), (queries.reshape(block_count, block_rows, HEADS, HD), positions.reshape(block_count, block_rows), grad_attn.reshape(block_count, block_rows, HEADS, HD), log_blocks, dot_blocks))
    return (grad_q.reshape(LEN, HEADS, HD), grad_k, grad_v)

def layer_forward(hidden, params, positions):
    norm1_gain, norm1_bias, norm2_gain, norm2_bias, qkv_weight, qkv_bias, dense_weight, dense_bias, fc1_weight, fc1_bias, fc2_weight, fc2_bias = params
    normed, inv_std = norm_stats(hidden)
    attn_in = (normed * norm1_gain.astype(jnp.float32) + norm1_bias.astype(jnp.float32)).astype(jnp.bfloat16)
    mlp_in = (normed * norm2_gain.astype(jnp.float32) + norm2_bias.astype(jnp.float32)).astype(jnp.bfloat16)
    mixed_qkv = jnp.dot(attn_in, qkv_weight.reshape(D, 3 * HEADS * HD), preferred_element_type=jnp.float32)
    mixed_qkv = mixed_qkv.reshape(LEN, 3, HEADS, HD) + qkv_bias.astype(jnp.float32)
    cosine, sine_table = rotary_tables(positions)
    queries = rotate_heads(mixed_qkv[:, 0], cosine, sine_table).astype(jnp.bfloat16)
    keys_rot = rotate_heads(mixed_qkv[:, 1], cosine, sine_table).astype(jnp.bfloat16)
    values = mixed_qkv[:, 2].astype(jnp.bfloat16)
    attn_out, log_totals = attend_forward(queries, keys_rot, values, positions)
    attn_part = jnp.dot(attn_out.reshape(LEN, HEADS * HD), dense_weight.reshape(HEADS * HD, D), preferred_element_type=jnp.float32)
    pre_act = jnp.dot(mlp_in, fc1_weight, preferred_element_type=jnp.float32) + fc1_bias.reshape(FF).astype(jnp.float32)
    activated = jax.nn.gelu(pre_act, approximate=False).astype(jnp.bfloat16)
    mlp_part = jnp.dot(activated, fc2_weight, preferred_element_type=jnp.float32)
    result = hidden + (attn_part + mlp_part) + dense_bias.astype(jnp.float32) + fc2_bias.astype(jnp.float32)
    saved = (normed, inv_std, attn_in, mlp_in, queries, keys_rot, values, attn_out, log_totals, pre_act, activated)
    return (result, saved)

def layer_backward(upstream, params, saved, positions):
    norm1_gain, norm1_bias, norm2_gain, norm2_bias, qkv_weight, qkv_bias, dense_weight, dense_bias, fc1_weight, fc1_bias, fc2_weight, fc2_bias = params
    normed, inv_std, attn_in, mlp_in, queries, keys_rot, values, attn_out, log_totals, pre_act, activated = saved
    upstream_b = upstream.astype(jnp.bfloat16)
    token_sum = lax.optimization_barrier(jnp.sum(upstream, axis=0))
    g_down = jnp.dot(activated.T, upstream_b, preferred_element_type=jnp.float32)
    d_pre = jnp.dot(upstream_b, fc2_weight.T, preferred_element_type=jnp.float32) * gelu_slope(pre_act)
    d_pre_b = d_pre.astype(jnp.bfloat16)
    g_up = jnp.dot(mlp_in.T, d_pre_b, preferred_element_type=jnp.float32)
    g_up_bias = lax.optimization_barrier(jnp.sum(d_pre, axis=0))
    d_mlp_in = jnp.dot(d_pre_b, fc1_weight.T, preferred_element_type=jnp.float32)
    grad_attn = jnp.dot(upstream_b, dense_weight.reshape(HEADS * HD, D).T, preferred_element_type=jnp.float32)
    grad_attn = grad_attn.reshape(LEN, HEADS, HD).astype(jnp.bfloat16)
    g_dense = jnp.dot(attn_out.reshape(LEN, HEADS * HD).T, upstream_b, preferred_element_type=jnp.float32).reshape(HEADS, HD, D)
    grad_q, grad_k, grad_v = attend_backward(queries, keys_rot, values, positions, grad_attn, attn_out, log_totals)
    cosine, sine_table = rotary_tables(positions)
    d_qkv = jnp.stack([unrotate_heads(grad_q, cosine, sine_table), unrotate_heads(grad_k, cosine, sine_table), grad_v], axis=1)
    g_qkv_bias = lax.optimization_barrier(jnp.sum(d_qkv, axis=0))
    d_qkv_b = d_qkv.astype(jnp.bfloat16).reshape(LEN, 3 * HEADS * HD)
    g_qkv = jnp.dot(attn_in.T, d_qkv_b, preferred_element_type=jnp.float32).reshape(D, 3, HEADS, HD)
    d_attn_in = jnp.dot(d_qkv_b, qkv_weight.reshape(D, 3 * HEADS * HD).T, preferred_element_type=jnp.float32)
    g_gain_one = lax.optimization_barrier(jnp.sum(d_attn_in * normed, axis=0))
    g_shift_one = lax.optimization_barrier(jnp.sum(d_attn_in, axis=0))
    g_gain_two = lax.optimization_barrier(jnp.sum(d_mlp_in * normed, axis=0))
    g_shift_two = lax.optimization_barrier(jnp.sum(d_mlp_in, axis=0))
    combined = d_attn_in * norm1_gain.astype(jnp.float32) + d_mlp_in * norm2_gain.astype(jnp.float32)
    grad_x = upstream + norm_grad(combined, normed, inv_std)
    grads = (g_gain_one, g_shift_one, g_gain_two, g_shift_two, g_qkv, g_qkv_bias, g_dense, token_sum, g_up, g_up_bias, g_down, token_sum)
    return (grad_x, grads)

def reference(x_in, cotangent, block_pos, norm1_gain, norm1_bias, norm2_gain, norm2_bias, qkv_weight, qkv_bias, dense_weight, dense_bias, fc1_weight, fc1_bias, fc2_weight, fc2_bias):
    stacks = (norm1_gain, norm1_bias, norm2_gain, norm2_bias, qkv_weight, qkv_bias, dense_weight, dense_bias, fc1_weight, fc1_bias, fc2_weight, fc2_bias)
    layer_params = [tuple((stacked[layer_index] for stacked in stacks)) for layer_index in range(LAYERS)]
    grad_sums = [None] * LAYERS
    input_grads = []
    block_outputs = []
    for micro_index in range(MB):
        positions = slot_positions(block_pos[micro_index])
        hidden = x_in[micro_index].astype(jnp.float32)
        kept_states = []
        result = hidden
        for layer_index in range(LAYERS):
            result, saved = layer_forward(hidden, layer_params[layer_index], positions)
            kept_states.append(saved)
            hidden = round_trip(result)
        block_outputs.append(result)
        upstream = cotangent[micro_index]
        grad_x = upstream
        for layer_index in reversed(range(LAYERS)):
            grad_x, grads = layer_backward(upstream, layer_params[layer_index], kept_states[layer_index], positions)
            if grad_sums[layer_index] is None:
                grad_sums[layer_index] = grads
            else:
                grad_sums[layer_index] = tuple((first_term + second_term for first_term, second_term in zip(grad_sums[layer_index], grads)))
            upstream = round_trip(grad_x)
        input_grads.append(grad_x)
    boundary = jnp.stack([jnp.stack(input_grads), jnp.stack(block_outputs)])
    stacked_grads = [jnp.stack([grad_sums[layer_index][position] for layer_index in range(LAYERS)]) for position in range(12)]
    return (boundary, stacked_grads[0], stacked_grads[1], stacked_grads[2], stacked_grads[3], stacked_grads[4], stacked_grads[5], stacked_grads[6], stacked_grads[7], stacked_grads[8], stacked_grads[9].reshape(LAYERS, N_TENSOR, FF // N_TENSOR), stacked_grads[10], stacked_grads[11])
```

```python
from functools import partial

import jax
import jax.numpy as jnp
from jax import lax
from jax.sharding import PartitionSpec as P

ROT = 64
EPS = 1e-05
MASKED_SCORE = -1e30
BF = jnp.bfloat16
F32 = jnp.float32


def dot(a, b, dims=((1,), (0,))):
    return lax.dot_general(a, b, (dims, ((), ())), preferred_element_type=F32)


def swap(v, axis, distance):
    size = lax.axis_size(axis)
    return lax.ppermute(v, axis, [(i, i ^ distance) for i in range(size)])


def rotary_tables(positions):
    inverse = 10000.0 ** (-(jnp.arange(ROT // 2, dtype=F32) * 2.0 / ROT))
    angles = positions.astype(F32)[:, None] * inverse[None, :]
    angles = jnp.concatenate([angles, angles], axis=-1)
    return (jnp.cos(angles), jnp.sin(angles))


def rotate(z, cosine, sine):
    half = ROT // 2
    lead = z[:, :ROT]
    turned = jnp.concatenate([-lead[:, half:], lead[:, :half]], axis=-1)
    return jnp.concatenate([lead * cosine + turned * sine, z[:, ROT:]], axis=-1)


def unrotate(g, cosine, sine):
    half = ROT // 2
    lead = g[:, :ROT]
    scaled = lead * sine
    turned = jnp.concatenate([scaled[:, half:], -scaled[:, :half]], axis=-1)
    return jnp.concatenate([lead * cosine + turned, g[:, ROT:]], axis=-1)


class Place:
    def __init__(self):
        self.k = lax.axis_index("section")
        self.c = lax.axis_index("ctx")
        self.t = lax.axis_index("tensor")
        self.n = lax.axis_size("ctx")
        self.nt = lax.axis_size("tensor")
        self.m = self.n // 2
        self.bits = self.m.bit_length() - 1
        self.y = self.c // self.m
        self.cl = self.c % self.m

    def over_k(self, v):
        return swap(v, "section", 1)

    def over_y(self, v):
        return swap(v, "ctx", self.m)

    def over_x(self, v, bit):
        return swap(v, "ctx", 1 << bit)

    def over_z(self, v, distance):
        return swap(v, "tensor", distance)

    def reduce_rows(self, v):
        cur = v
        for bit in reversed(range(self.bits)):
            half = cur.shape[0] // 2
            got = self.over_x(cur[half:].astype(BF), bit)
            cur = cur[:half].astype(F32) + got.astype(F32)
        return cur[0].astype(F32)

    def sum_rows(self, v):
        cur = v
        for bit in range(self.bits):
            got = self.over_x(cur.astype(BF), bit)
            shape = got.shape
            got = got.reshape(shape[0] >> (bit + 1), 2, 1 << bit, *shape[1:])
            got = jnp.concatenate([got[:, 1:], got[:, :1]], axis=1).reshape(shape)
            cur = cur.astype(F32) + got.astype(F32)
        return cur

    def gather_rows(self, v):
        cur = v[None]
        for bit in range(self.bits):
            cur = jnp.concatenate([cur, self.over_x(cur, bit)], axis=0)
        return cur.reshape(-1, v.shape[-1])

    def reduce_tensor(self, v):
        got = self.over_k(v[:, :, 1])
        cur = v[:, :, 0].astype(F32) + got.astype(F32)
        sent = cur.astype(BF)
        total = cur[:, 0]
        for s in range(1, self.nt):
            total = total + self.over_z(sent[:, s], s).astype(F32)
        return total

    def gather_tensor(self, v):
        parts = [v] + [self.over_z(v, s) for s in range(1, self.nt)]
        mine = jnp.stack(parts, axis=1)
        other = self.over_k(mine)
        return jnp.stack([mine, other], axis=2).reshape(-1, v.shape[-1])


def merge_stats(place, mean, spread, count):
    for bit in range(place.bits):
        got = place.over_x(jnp.stack([mean, spread]), bit)
        shape = mean.shape
        if mean.ndim == 2:
            pairs = got.reshape(2, shape[0] >> (bit + 1), 2, 1 << bit, shape[1])
            pairs = jnp.concatenate([pairs[:, :, 1:], pairs[:, :, :1]], axis=2)
            got = pairs.reshape(2, *shape)
        delta = got[0] - mean
        spread = spread + got[1] + delta * delta * (count * 0.5)
        mean = 0.5 * (mean + got[0])
        count = count * 2
    return mean, spread, count


def norm_stats(place, h):
    rows, width = h.shape
    wide = h.astype(F32)
    mean = jnp.mean(wide, axis=-1)
    centre = wide - mean[:, None]
    spread = jnp.sum(centre * centre, axis=-1)
    shape = (place.m, rows // place.m)
    mean, spread, count = merge_stats(place, mean.reshape(shape), spread.reshape(shape), float(width))
    inv = lax.rsqrt(spread / count + EPS)
    return mean.reshape(rows, 1), inv.reshape(rows, 1)


def layer_forward(place, h, w, small, tables):
    w_qkv, w_out, w_up, w_down = w
    rows = h.shape[0]
    m = place.m
    own = rows // m
    hd = w_out[0].shape[0]
    cosine, sine, pos = tables
    mean, inv = norm_stats(place, h)
    normed = (h.astype(F32) - mean) * inv
    attn_in = (normed * small["g1"] + small["b1"]).astype(BF)
    mlp_in = (normed * small["g2"] + small["b2"]).astype(BF)
    mixed = dot(attn_in, w_qkv).astype(BF).reshape(m, own, 3 * hd)
    hidden = dot(mlp_in, w_up).astype(BF).reshape(m, own, -1)
    kv = place.sum_rows(mixed[..., hd:]).reshape(rows, 2 * hd) + small["qkv_bias"][hd:]
    q = place.reduce_rows(mixed[..., :hd]) + small["qkv_bias"][:hd]
    queries = rotate(q, cosine[:own], sine[:own]).astype(BF)
    keys = rotate(kv[:, :hd], cosine, sine).astype(BF)
    values = kv[:, hd:].astype(BF)
    scores = dot(queries, keys, ((1,), (1,))) * (hd**-0.5)
    allowed = pos[:own, None] >= pos[None, :]
    scores = jnp.where(allowed, scores, MASKED_SCORE)
    top = jnp.max(scores, axis=-1, keepdims=True)
    exps = jnp.where(allowed, jnp.exp(scores - top), 0.0)
    total = jnp.sum(exps, axis=-1, keepdims=True)
    attn_out = (dot(exps.astype(BF), values) / total).astype(BF)
    probs = exps / total
    pre = place.reduce_rows(hidden) + small["fc1_bias"]
    cdf = 0.5 * (1.0 + lax.erf(pre * 0.7071067811865476))
    act = (pre * cdf).astype(BF)
    slope = cdf + pre * jnp.exp(-0.5 * pre * pre) * 0.3989422804014327
    attn_all = place.gather_rows(attn_out)
    act_all = place.gather_rows(act)
    part = jnp.concatenate(
        [dot(attn_all, w_out[j]) + dot(act_all, w_down[j]) for j in range(2)], axis=1
    ).astype(BF)
    branch = place.reduce_tensor(part.reshape(m, place.nt, 2, -1, part.shape[-1]))
    h_own = h.reshape(m, place.nt, 2, -1, h.shape[-1])[:, 0, 0].astype(F32)
    out = h_own + branch + small["out_bias"]
    saved = (h, mean, inv, attn_in, mlp_in, queries, keys, values, probs, attn_out, attn_all, act_all, slope)
    return out, saved


def layer_backward(place, grad, w, small, tables, saved):
    w_qkv, w_out, w_up, w_down = w
    h, mean, inv, attn_in, mlp_in, queries, keys, values, probs, attn_out, attn_all, act_all, slope = saved
    rows = h.shape[0]
    m = place.m
    own = rows // m
    hd = w_out[0].shape[0]
    width = h.shape[1] // 2
    scaling = hd**-0.5
    cosine, sine, pos = tables
    halves = (grad[:, :width], grad[:, width:])
    d_attn = sum(dot(halves[j], w_out[j], ((1,), (1,))) for j in range(2)).astype(BF)
    d_act = sum(dot(halves[j], w_down[j], ((1,), (1,))) for j in range(2)).astype(BF)
    grad_attn = place.reduce_rows(d_attn.reshape(m, own, hd)).astype(BF)
    row_dot = jnp.sum(grad_attn.astype(F32) * attn_out.astype(F32), axis=-1, keepdims=True)
    d_prob = dot(grad_attn, values, ((1,), (1,)))
    d_score = (probs * (d_prob - row_dot)).astype(BF)
    dq = unrotate(dot(d_score, keys) * scaling, cosine[:own], sine[:own]).astype(BF)
    dk = unrotate(dot(d_score, queries, ((0,), (0,))) * scaling, cosine, sine).astype(BF)
    dv = dot(probs.astype(BF), grad_attn, ((0,), (0,))).astype(BF)
    dkv = place.sum_rows(jnp.concatenate([dk, dv], axis=1).reshape(m, own, 2 * hd)).astype(BF)
    d_qkv = jnp.concatenate([place.gather_rows(dq), dkv.reshape(rows, 2 * hd)], axis=1)
    d_pre = (place.reduce_rows(d_act.reshape(m, own, -1)) * slope).astype(BF)
    d_pre_all = place.gather_rows(d_pre)
    d_mlp_in = dot(d_pre_all, w_up, ((1,), (1,)))
    d_attn_in = dot(d_qkv, w_qkv, ((1,), (1,)))
    normed = (h.astype(F32) - mean) * inv
    combined = (d_attn_in * small["g1"] + d_mlp_in * small["g2"]).astype(BF)
    gains = jnp.stack(
        [
            jnp.sum(d_attn_in * normed, axis=0),
            jnp.sum(d_attn_in, axis=0),
            jnp.sum(d_mlp_in * normed, axis=0),
            jnp.sum(d_mlp_in, axis=0),
            jnp.sum(grad.astype(F32), axis=0),
        ]
    )
    biases = jnp.concatenate(
        [jnp.sum(d_qkv.astype(F32), axis=0), jnp.sum(d_pre_all.astype(F32), axis=0)]
    )
    comb = place.reduce_tensor(combined.reshape(m, place.nt, 2, -1, combined.shape[-1]))
    pick = lambda v: v.reshape(m, place.nt, 2, -1, v.shape[-1])[:, 0, 0]
    own_normed = pick(normed)
    sums = jnp.stack([jnp.sum(comb, axis=-1), jnp.sum(comb * own_normed, axis=-1)])
    for bit in range(place.bits):
        got = place.over_x(sums, bit)
        shape = got.shape
        got = got.reshape(2, shape[1] >> (bit + 1), 2, 1 << bit, shape[2])
        got = jnp.concatenate([got[:, :, 1:], got[:, :, :1]], axis=2).reshape(shape)
        sums = sums + got
    sums = sums / (comb.shape[-1] * m)
    grad_in = pick(grad).astype(F32) + pick(inv) * (
        comb - sums[0][..., None] - own_normed * sums[1][..., None]
    )

    def both(make):
        mine, other = make(0), make(1).astype(BF)
        return mine + place.over_y(other).astype(F32)

    cut = lambda v, j: v[:, j * width : (j + 1) * width]
    g_down = both(lambda j: dot(act_all, halves[j], ((0,), (0,))))
    g_out = both(lambda j: dot(attn_all, halves[j], ((0,), (0,))))
    g_up = both(lambda j: dot(cut(mlp_in, j), d_pre_all, ((0,), (0,))))
    g_qkv = both(lambda j: dot(cut(attn_in, j), d_qkv, ((0,), (0,))))
    return grad_in, (g_qkv, g_out, g_up, g_down), gains, biases


def spread_tokens(place, v, index):
    _, tokens, width = v.shape
    n, m = place.n, place.m
    half = tokens // 2
    rows = lax.dynamic_slice_in_dim(v.astype(BF), place.k * half, half, axis=1)
    rows = rows.reshape(2, half, 2, m, width // n)
    rows = jnp.stack([rows[0], jnp.flip(rows[1], axis=1)])
    rows = jnp.transpose(rows, (0, 3, 1, 2, 4)).reshape(n, half, 2 * width // n)
    got = lax.all_to_all(rows, "ctx", 0, 0)
    both = jnp.stack([got, place.over_k(got)])
    block = tokens // place.nt
    blocks = both.reshape(-1, block, 2 * width // n)
    return jnp.take(blocks, index, axis=0, mode="clip").reshape(-1, 2 * width // n)


def deliver(place, out, grad_in):
    is_first = place.k == 0
    n, m, nt = place.n, place.m, place.nt
    mine = jnp.where(is_first, grad_in, out).astype(BF)
    other = jnp.where(is_first, out, grad_in).astype(BF)
    got = place.over_k(other)
    low = jnp.where(is_first, mine, got)
    high = jnp.where(is_first, got, mine)
    block = mine.shape[1]
    width = mine.shape[2] // 2
    pieces = jnp.stack([low, high], axis=1).reshape(m, 2 * block, 2, width)
    quarter = m // 2
    t0, t1 = place.t % 2, place.t // 2
    top, rest = place.cl // quarter, place.cl % quarter
    arrived = {}
    for a in range(m):
        dest_cl = (t0 * quarter + rest) ^ a
        rel = dest_cl ^ place.cl
        chosen = lax.dynamic_index_in_dim(pieces, rel, axis=0, keepdims=False)
        for b in range(2):
            pairs = []
            for c in range(n):
                for t in range(nt):
                    y, cl = c // m, c % m
                    s0, s1 = t % 2, t // 2
                    dc = ((s0 * quarter + cl % quarter) ^ a) * 2 + s1
                    dt = (y ^ b) * 2 + cl // quarter
                    pairs.append((c * nt + t, dc * nt + dt))
            arrived[a, b] = lax.ppermute(chosen[:, b], ("ctx", "tensor"), pairs)
    own_cl, own_x = place.c // 2, place.c % 2
    j, _ = place.t // 2, place.t % 2
    stacked = jnp.stack([jnp.stack([arrived[a, b] for b in range(2)]) for a in range(m)])
    result = []
    for micro in range(2):
        halves = []
        for s0 in range(2):
            columns = []
            for r in range(quarter):
                a = own_cl ^ (s0 * quarter + r)
                b = j ^ micro
                columns.append(lax.dynamic_slice(stacked, (a, b, 0, 0), (1, 1, 2 * block, width))[0, 0])
            halves.append(jnp.concatenate(columns, axis=1))
        result.append(jnp.concatenate(halves, axis=0))
    return jnp.stack(result)[None].astype(F32)


def body(
    x_in,
    cotangent,
    block_pos,
    norm1_gain,
    norm1_bias,
    norm2_gain,
    norm2_bias,
    qkv_weight,
    qkv_bias,
    dense_weight,
    dense_bias,
    fc1_weight,
    fc1_bias,
    fc2_weight,
    fc2_bias,
):
    place = Place()
    k, n, m, nt = place.k, place.n, place.m, place.nt
    is_first = k == 0
    tokens = x_in.shape[1]
    seq = tokens * n
    block = tokens // nt
    piece = fc1_weight.shape[1]
    hd = dense_weight.shape[2]
    ff = fc1_weight.shape[2]

    stacks = (
        jnp.transpose(qkv_weight[0], (2, 0, 1, 3)).reshape(2, piece, 3 * hd),
        dense_weight[0],
        jnp.transpose(fc1_weight[0].reshape(piece, 2, ff // 2), (1, 0, 2)),
        fc2_weight[0].reshape(2, ff // 2, piece),
    )
    keep = [lax.dynamic_index_in_dim(s, k, 0, keepdims=False) for s in stacks]
    send = [lax.dynamic_index_in_dim(s, 1 - k, 0, keepdims=False) for s in stacks]
    got = [place.over_k(s) for s in send]
    layers = []
    for layer in range(2):
        mine = [jnp.where(k == layer, a, b) for a, b in zip(keep, got)]
        theirs = [place.over_y(s) for s in mine]
        layers.append(
            (
                jnp.concatenate([mine[0], theirs[0]], axis=0),
                (mine[1], theirs[1]),
                jnp.concatenate([mine[2], theirs[2]], axis=0),
                (mine[3], theirs[3]),
            )
        )

    vector = jnp.concatenate(
        [
            norm1_gain[0],
            norm1_bias[0],
            norm2_gain[0],
            norm2_bias[0],
            dense_bias[0],
            fc2_bias[0],
            qkv_bias.reshape(-1),
            fc1_bias.reshape(-1),
        ]
    )
    everything = lax.all_gather(vector, ("section", "ctx"), axis=0).reshape(2, n, -1).astype(F32)
    pair = [
        lax.dynamic_index_in_dim(everything, place.c, 1, keepdims=False),
        lax.dynamic_index_in_dim(everything, place.c ^ m, 1, keepdims=False),
    ]
    smalls = []
    for layer in range(2):
        rows = [jnp.concatenate([p[layer, i * piece : (i + 1) * piece] for p in pair]) for i in range(6)]
        rest = everything[layer, :, 6 * piece :]
        size = 6 * (hd // n)
        qkv_b = rest[:, :size].reshape(n, 3, 2, hd // n)
        qkv_b = jnp.transpose(qkv_b, (2, 1, 0, 3)).reshape(2, 3 * hd)
        fc1_b = rest[:, size:].reshape(2, ff // 2)
        smalls.append(
            {
                "g1": rows[0],
                "b1": rows[1],
                "g2": rows[2],
                "b2": rows[3],
                "out_bias": rows[4] + rows[5],
                "qkv_bias": lax.dynamic_index_in_dim(qkv_b, k, 0, keepdims=False),
                "fc1_bias": lax.dynamic_index_in_dim(fc1_b, k, 0, keepdims=False),
            }
        )

    code = (place.cl * nt + place.t) * 2 + k
    count = seq // block
    absolute = jnp.arange(count, dtype=jnp.int32) ^ code
    half_rows = nt // 2
    source = absolute // nt
    part = (absolute // half_rows) % 2
    index = ((part ^ k) * n + source) * half_rows + absolute % half_rows
    slot = (absolute[:, None] * block + jnp.arange(block, dtype=jnp.int32)[None]).reshape(-1)
    per_block = seq // block_pos.shape[1]
    order = lax.dynamic_index_in_dim(block_pos, place.y, 0, keepdims=False)
    hit = (slot // per_block)[:, None] == jnp.arange(block_pos.shape[1], dtype=jnp.int32)[None]
    pos = jnp.sum(jnp.where(hit, order[None], 0), axis=1) * per_block + slot % per_block
    tables = rotary_tables(pos) + (pos,)

    h = spread_tokens(place, x_in, index)
    grad = spread_tokens(place, cotangent, index)
    saved = []
    for layer in range(2):
        out, kept = layer_forward(place, h, layers[layer], smalls[layer], tables)
        saved.append(kept)
        if layer == 0:
            h = place.gather_tensor(out.astype(BF))
    results = [None, None]
    for layer in (1, 0):
        grad_in, weights, gains, biases = layer_backward(
            place, grad, layers[layer], smalls[layer], tables, saved[layer]
        )
        results[layer] = (weights, gains, biases)
        if layer == 1:
            grad = place.gather_tensor(grad_in.astype(BF))

    boundary = deliver(place, out, grad_in)

    finals = []
    for i in range(4):
        first, second = results[0][0][i], results[1][0][i]
        to_second = lax.ppermute(second.astype(BF), "section", [(0, 1)])
        to_first = lax.ppermute(first.astype(BF), "section", [(1, 0)])
        mine = jnp.where(is_first, first, second)
        other = jnp.where(is_first, to_first, to_second).astype(F32)
        finals.append((jnp.where(is_first, mine, other), jnp.where(is_first, other, mine)))
    g_qkv = jnp.stack([v.reshape(piece, 3, hd) for v in finals[0]], axis=2)[None]
    g_out = jnp.stack(finals[1])[None]
    g_up = jnp.concatenate(finals[2], axis=1)[None]
    g_down = jnp.concatenate(finals[3], axis=0)[None]

    def flat(layer):
        _, gains, biases = results[layer]
        return gains.reshape(5, 2, piece), biases

    packed = [jnp.concatenate([flat(layer)[0][:, 1].reshape(-1), flat(layer)[1]]) for layer in range(2)]
    packed = place.over_y(jnp.stack(packed))
    sums = []
    for layer in range(2):
        gains, biases = flat(layer)
        sums.append(jnp.concatenate([gains[:, 0].reshape(-1), biases]) + packed[layer])
    mine = jnp.where(is_first, sums[0], sums[1])
    other = place.over_k(jnp.where(is_first, sums[1], sums[0]))
    norms = mine[: 4 * piece] + other[: 4 * piece]
    total = norms
    for s in range(1, nt):
        total = total + place.over_z(norms, s)
    total = total.reshape(4, 1, piece)
    token_sum = mine[4 * piece : 5 * piece][None]
    tail_mine, tail_other = mine[5 * piece :], other[5 * piece :]
    low = jnp.where(is_first, tail_mine, tail_other)
    high = jnp.where(is_first, tail_other, tail_mine)
    tails = jnp.stack([low, high])
    qkv_b = jnp.transpose(tails[:, : 3 * hd].reshape(2, 3, hd), (1, 0, 2))
    qkv_b = lax.dynamic_slice_in_dim(qkv_b, place.c * (hd // n), hd // n, axis=2)[None]
    fc1_b = lax.dynamic_slice_in_dim(tails[:, 3 * hd :].reshape(-1), place.c * (ff // n), ff // n)[None, None]
    return (
        boundary,
        total[0],
        total[1],
        total[2],
        total[3],
        g_qkv,
        qkv_b,
        g_out,
        token_sum,
        g_up,
        fc1_b,
        g_down,
        token_sum,
    )


def solution(mesh):
    in_specs = (
        P(None, "ctx", None),
        P(None, "ctx", None),
        P(),
        P("section", "ctx"),
        P("section", "ctx"),
        P("section", "ctx"),
        P("section", "ctx"),
        P("section", "ctx", None, "tensor", None),
        P("section", None, "tensor", "ctx"),
        P("section", "tensor", None, "ctx"),
        P("section", "ctx"),
        P("section", "ctx", "tensor"),
        P("section", "tensor", "ctx"),
        P("section", "tensor", "ctx"),
        P("section", "ctx"),
    )
    out_specs = (
        P("section", None, "ctx", "tensor"),
        P("section", "ctx"),
        P("section", "ctx"),
        P("section", "ctx"),
        P("section", "ctx"),
        P("section", "ctx", None, "tensor", None),
        P("section", None, "tensor", "ctx"),
        P("section", "tensor", None, "ctx"),
        P("section", "ctx"),
        P("section", "ctx", "tensor"),
        P("section", "tensor", "ctx"),
        P("section", "tensor", "ctx"),
        P("section", "ctx"),
    )
    return jax.shard_map(body, mesh=mesh, in_specs=in_specs, out_specs=out_specs, check_vma=False)
```

```python
import jax
import jax.numpy as jnp
from jax import lax
from jax.experimental import pallas as pl
from jax.experimental.pallas import tpu as pltpu
from jax.sharding import PartitionSpec as P


ROT = 64
EPS = 1e-05
MASKED_SCORE = -1e30
BF = jnp.bfloat16
F32 = jnp.float32

CTX, TENSOR, SECTION = "ctx", "tensor", "section"


def dot(a, b, dims=((1,), (0,))):
    return lax.dot_general(a, b, (dims, ((), ())), preferred_element_type=F32)


def swap(v, axis, distance):
    size = lax.axis_size(axis)
    return lax.ppermute(v, axis, [(i, i ^ distance) for i in range(size)])


def rotary_tables(positions):
    inverse = 10000.0 ** (-(jnp.arange(ROT // 2, dtype=F32) * 2.0 / ROT))
    angles = positions.astype(F32)[:, None] * inverse[None, :]
    angles = jnp.concatenate([angles, angles], axis=-1)
    return (jnp.cos(angles), jnp.sin(angles))


def rotate(z, cosine, sine):
    half = ROT // 2
    lead = z[:, :ROT]
    turned = jnp.concatenate([-lead[:, half:], lead[:, :half]], axis=-1)
    return jnp.concatenate([lead * cosine + turned * sine, z[:, ROT:]], axis=-1)


def unrotate(g, cosine, sine):
    half = ROT // 2
    lead = g[:, :ROT]
    scaled = lead * sine
    turned = jnp.concatenate([scaled[:, half:], -scaled[:, :half]], axis=-1)
    return jnp.concatenate([lead * cosine + turned, g[:, ROT:]], axis=-1)


class Place:
    def __init__(self):
        self.k = lax.axis_index(SECTION)
        self.c = lax.axis_index(CTX)
        self.t = lax.axis_index(TENSOR)
        self.n = lax.axis_size(CTX)
        self.nt = lax.axis_size(TENSOR)
        self.m = self.n // 2
        self.bits = self.m.bit_length() - 1
        self.y = self.c // self.m
        self.cl = self.c % self.m

    def over_k(self, v):
        return swap(v, SECTION, 1)

    def over_y(self, v):
        return swap(v, CTX, self.m)

    def over_x(self, v, bit):
        return swap(v, CTX, 1 << bit)

    def over_z(self, v, distance):
        return swap(v, TENSOR, distance)

    def reduce_rows(self, v):
        cur = v
        for bit in reversed(range(self.bits)):
            half = cur.shape[0] // 2
            got = self.over_x(cur[half:].astype(BF), bit)
            cur = cur[:half].astype(F32) + got.astype(F32)
        return cur[0].astype(F32)

    def sum_rows(self, v):
        cur = v
        for bit in range(self.bits):
            got = self.over_x(cur.astype(BF), bit)
            shape = got.shape
            got = got.reshape(shape[0] >> (bit + 1), 2, 1 << bit, *shape[1:])
            got = jnp.concatenate([got[:, 1:], got[:, :1]], axis=1).reshape(shape)
            cur = cur.astype(F32) + got.astype(F32)
        return cur

    def gather_rows(self, v):
        cur = v[None]
        for bit in range(self.bits):
            cur = jnp.concatenate([cur, self.over_x(cur, bit)], axis=0)
        return cur.reshape(-1, v.shape[-1])

    def reduce_tensor(self, v):
        got = self.over_k(v[:, :, 1])
        cur = v[:, :, 0].astype(F32) + got.astype(F32)
        sent = cur.astype(BF)
        total = cur[:, 0]
        for s in range(1, self.nt):
            total = total + self.over_z(sent[:, s], s).astype(F32)
        return total

    def gather_tensor(self, v):
        parts = [v] + [self.over_z(v, s) for s in range(1, self.nt)]
        mine = jnp.stack(parts, axis=1)
        other = self.over_k(mine)
        return jnp.stack([mine, other], axis=2).reshape(-1, v.shape[-1])


def merge_stats(place, mean, spread, count):
    for bit in range(place.bits):
        got = place.over_x(jnp.stack([mean, spread]), bit)
        shape = mean.shape
        if mean.ndim == 2:
            pairs = got.reshape(2, shape[0] >> (bit + 1), 2, 1 << bit, shape[1])
            pairs = jnp.concatenate([pairs[:, :, 1:], pairs[:, :, :1]], axis=2)
            got = pairs.reshape(2, *shape)
        delta = got[0] - mean
        spread = spread + got[1] + delta * delta * (count * 0.5)
        mean = 0.5 * (mean + got[0])
        count = count * 2
    return mean, spread, count


def norm_stats(place, h):
    rows, width = h.shape
    wide = h.astype(F32)
    mean = jnp.mean(wide, axis=-1)
    centre = wide - mean[:, None]
    spread = jnp.sum(centre * centre, axis=-1)
    shape = (place.m, rows // place.m)
    mean, spread, count = merge_stats(place, mean.reshape(shape), spread.reshape(shape), float(width))
    inv = lax.rsqrt(spread / count + EPS)
    return mean.reshape(rows, 1), inv.reshape(rows, 1)


def layer_forward(place, h, w, small, tables):
    w_qkv, w_out, w_up, w_down = w
    rows = h.shape[0]
    m = place.m
    own = rows // m
    hd = w_out[0].shape[0]
    cosine, sine, pos = tables
    mean, inv = norm_stats(place, h)
    normed = (h.astype(F32) - mean) * inv
    attn_in = (normed * small["g1"] + small["b1"]).astype(BF)
    mlp_in = (normed * small["g2"] + small["b2"]).astype(BF)
    mixed = dot(attn_in, w_qkv).astype(BF).reshape(m, own, 3 * hd)
    hidden = dot(mlp_in, w_up).astype(BF).reshape(m, own, -1)
    kv = place.sum_rows(mixed[..., hd:]).reshape(rows, 2 * hd) + small["qkv_bias"][hd:]
    q = place.reduce_rows(mixed[..., :hd]) + small["qkv_bias"][:hd]
    queries = rotate(q, cosine[:own], sine[:own]).astype(BF)
    keys = rotate(kv[:, :hd], cosine, sine).astype(BF)
    values = kv[:, hd:].astype(BF)
    scores = dot(queries, keys, ((1,), (1,))) * (hd**-0.5)
    allowed = pos[:own, None] >= pos[None, :]
    scores = jnp.where(allowed, scores, MASKED_SCORE)
    top = jnp.max(scores, axis=-1, keepdims=True)
    exps = jnp.where(allowed, jnp.exp(scores - top), 0.0)
    total = jnp.sum(exps, axis=-1, keepdims=True)
    attn_out = (dot(exps.astype(BF), values) / total).astype(BF)
    probs = exps / total
    pre = place.reduce_rows(hidden) + small["fc1_bias"]
    cdf = 0.5 * (1.0 + lax.erf(pre * 0.7071067811865476))
    act = (pre * cdf).astype(BF)
    slope = cdf + pre * jnp.exp(-0.5 * pre * pre) * 0.3989422804014327
    attn_all = place.gather_rows(attn_out)
    act_all = place.gather_rows(act)
    part = jnp.concatenate(
        [dot(attn_all, w_out[j]) + dot(act_all, w_down[j]) for j in range(2)], axis=1
    ).astype(BF)
    branch = place.reduce_tensor(part.reshape(m, place.nt, 2, -1, part.shape[-1]))
    h_own = h.reshape(m, place.nt, 2, -1, h.shape[-1])[:, 0, 0].astype(F32)
    out = h_own + branch + small["out_bias"]
    saved = (h, mean, inv, attn_in, mlp_in, queries, keys, values, probs, attn_out, attn_all, act_all, slope)
    return out, saved


def layer_backward(place, grad, w, small, tables, saved):
    w_qkv, w_out, w_up, w_down = w
    h, mean, inv, attn_in, mlp_in, queries, keys, values, probs, attn_out, attn_all, act_all, slope = saved
    rows = h.shape[0]
    m = place.m
    own = rows // m
    hd = w_out[0].shape[0]
    width = h.shape[1] // 2
    scaling = hd**-0.5
    cosine, sine, _ = tables
    halves = (grad[:, :width], grad[:, width:])
    d_attn = sum(dot(halves[j], w_out[j], ((1,), (1,))) for j in range(2)).astype(BF)
    d_act = sum(dot(halves[j], w_down[j], ((1,), (1,))) for j in range(2)).astype(BF)
    grad_attn = place.reduce_rows(d_attn.reshape(m, own, hd)).astype(BF)
    row_dot = jnp.sum(grad_attn.astype(F32) * attn_out.astype(F32), axis=-1, keepdims=True)
    d_prob = dot(grad_attn, values, ((1,), (1,)))
    d_score = (probs * (d_prob - row_dot)).astype(BF)
    dq = unrotate(dot(d_score, keys) * scaling, cosine[:own], sine[:own]).astype(BF)
    dk = unrotate(dot(d_score, queries, ((0,), (0,))) * scaling, cosine, sine).astype(BF)
    dv = dot(probs.astype(BF), grad_attn, ((0,), (0,))).astype(BF)
    dkv = place.sum_rows(jnp.concatenate([dk, dv], axis=1).reshape(m, own, 2 * hd)).astype(BF)
    d_qkv = jnp.concatenate([place.gather_rows(dq), dkv.reshape(rows, 2 * hd)], axis=1)
    d_pre = (place.reduce_rows(d_act.reshape(m, own, -1)) * slope).astype(BF)
    d_pre_all = place.gather_rows(d_pre)
    d_mlp_in = dot(d_pre_all, w_up, ((1,), (1,)))
    d_attn_in = dot(d_qkv, w_qkv, ((1,), (1,)))
    normed = (h.astype(F32) - mean) * inv
    combined = (d_attn_in * small["g1"] + d_mlp_in * small["g2"]).astype(BF)
    gains = jnp.stack(
        [
            jnp.sum(d_attn_in * normed, axis=0),
            jnp.sum(d_attn_in, axis=0),
            jnp.sum(d_mlp_in * normed, axis=0),
            jnp.sum(d_mlp_in, axis=0),
            jnp.sum(grad.astype(F32), axis=0),
        ]
    )
    biases = jnp.concatenate(
        [jnp.sum(d_qkv.astype(F32), axis=0), jnp.sum(d_pre_all.astype(F32), axis=0)]
    )
    comb = place.reduce_tensor(combined.reshape(m, place.nt, 2, -1, combined.shape[-1]))
    pick = lambda v: v.reshape(m, place.nt, 2, -1, v.shape[-1])[:, 0, 0]
    own_normed = pick(normed)
    sums = jnp.stack([jnp.sum(comb, axis=-1), jnp.sum(comb * own_normed, axis=-1)])
    for bit in range(place.bits):
        got = place.over_x(sums, bit)
        shape = got.shape
        got = got.reshape(2, shape[1] >> (bit + 1), 2, 1 << bit, shape[2])
        got = jnp.concatenate([got[:, :, 1:], got[:, :, :1]], axis=2).reshape(shape)
        sums = sums + got
    sums = sums / (comb.shape[-1] * m)
    grad_in = pick(grad).astype(F32) + pick(inv) * (
        comb - sums[0][..., None] - own_normed * sums[1][..., None]
    )

    def both(make):
        mine, other = make(0), make(1).astype(BF)
        return mine + place.over_y(other).astype(F32)

    cut = lambda v, j: v[:, j * width : (j + 1) * width]
    g_down = both(lambda j: dot(act_all, halves[j], ((0,), (0,))))
    g_out = both(lambda j: dot(attn_all, halves[j], ((0,), (0,))))
    g_up = both(lambda j: dot(cut(mlp_in, j), d_pre_all, ((0,), (0,))))
    g_qkv = both(lambda j: dot(cut(attn_in, j), d_qkv, ((0,), (0,))))
    return grad_in, (g_qkv, g_out, g_up, g_down), gains, biases


def spread_tokens(place, v, index):
    _, tokens, width = v.shape
    n, m = place.n, place.m
    half = tokens // 2
    rows = lax.dynamic_slice_in_dim(v.astype(BF), place.k * half, half, axis=1)
    rows = rows.reshape(2, half, 2, m, width // n)
    rows = jnp.stack([rows[0], jnp.flip(rows[1], axis=1)])
    rows = jnp.transpose(rows, (0, 3, 1, 2, 4)).reshape(n, half, 2 * width // n)
    got = lax.all_to_all(rows, CTX, 0, 0)
    both = jnp.stack([got, place.over_k(got)])
    block = tokens // place.nt
    blocks = both.reshape(-1, block, 2 * width // n)
    return jnp.take(blocks, index, axis=0, mode="clip").reshape(-1, 2 * width // n)


def deliver(place, out, grad_in):
    is_first = place.k == 0
    n, m, nt = place.n, place.m, place.nt
    mine = jnp.where(is_first, grad_in, out).astype(BF)
    other = jnp.where(is_first, out, grad_in).astype(BF)
    got = place.over_k(other)
    low = jnp.where(is_first, mine, got)
    high = jnp.where(is_first, got, mine)
    block = mine.shape[1]
    width = mine.shape[2] // 2
    pieces = jnp.stack([low, high], axis=1).reshape(m, 2 * block, 2, width)
    quarter = m // 2
    t0 = place.t % 2
    rest = place.cl % quarter
    arrived = {}
    for a in range(m):
        dest_cl = (t0 * quarter + rest) ^ a
        rel = dest_cl ^ place.cl
        chosen = lax.dynamic_index_in_dim(pieces, rel, axis=0, keepdims=False)
        for b in range(2):
            pairs = []
            for c in range(n):
                for t in range(nt):
                    y, cl = c // m, c % m
                    s0, s1 = t % 2, t // 2
                    dc = ((s0 * quarter + cl % quarter) ^ a) * 2 + s1
                    dt = (y ^ b) * 2 + cl // quarter
                    pairs.append((c * nt + t, dc * nt + dt))
            arrived[a, b] = lax.ppermute(chosen[:, b], (CTX, TENSOR), pairs)
    own_cl = place.c // 2
    j = place.t // 2
    stacked = jnp.stack([jnp.stack([arrived[a, b] for b in range(2)]) for a in range(m)])
    result = []
    for micro in range(2):
        halves = []
        for s0 in range(2):
            columns = []
            for r in range(quarter):
                a = own_cl ^ (s0 * quarter + r)
                b = j ^ micro
                columns.append(lax.dynamic_slice(stacked, (a, b, 0, 0), (1, 1, 2 * block, width))[0, 0])
            halves.append(jnp.concatenate(columns, axis=1))
        result.append(jnp.concatenate(halves, axis=0))
    return jnp.stack(result)[None].astype(F32)


def body_any(
    x_in,
    cotangent,
    block_pos,
    norm1_gain,
    norm1_bias,
    norm2_gain,
    norm2_bias,
    qkv_weight,
    qkv_bias,
    dense_weight,
    dense_bias,
    fc1_weight,
    fc1_bias,
    fc2_weight,
    fc2_bias,
):
    place = Place()
    k, n, m, nt = place.k, place.n, place.m, place.nt
    is_first = k == 0
    tokens = x_in.shape[1]
    seq = tokens * n
    block = tokens // nt
    piece = fc1_weight.shape[1]
    hd = dense_weight.shape[2]
    ff = fc1_weight.shape[2]

    stacks = (
        jnp.transpose(qkv_weight[0], (2, 0, 1, 3)).reshape(2, piece, 3 * hd),
        dense_weight[0],
        jnp.transpose(fc1_weight[0].reshape(piece, 2, ff // 2), (1, 0, 2)),
        fc2_weight[0].reshape(2, ff // 2, piece),
    )
    keep = [lax.dynamic_index_in_dim(s, k, 0, keepdims=False) for s in stacks]
    send = [lax.dynamic_index_in_dim(s, 1 - k, 0, keepdims=False) for s in stacks]
    got = [place.over_k(s) for s in send]
    layers = []
    for layer in range(2):
        mine = [jnp.where(k == layer, a, b) for a, b in zip(keep, got)]
        theirs = [place.over_y(s) for s in mine]
        layers.append(
            (
                jnp.concatenate([mine[0], theirs[0]], axis=0),
                (mine[1], theirs[1]),
                jnp.concatenate([mine[2], theirs[2]], axis=0),
                (mine[3], theirs[3]),
            )
        )

    vector = jnp.concatenate(
        [
            norm1_gain[0],
            norm1_bias[0],
            norm2_gain[0],
            norm2_bias[0],
            dense_bias[0],
            fc2_bias[0],
            qkv_bias.reshape(-1),
            fc1_bias.reshape(-1),
        ]
    )
    everything = lax.all_gather(vector, (SECTION, CTX), axis=0).reshape(2, n, -1).astype(F32)
    pair = [
        lax.dynamic_index_in_dim(everything, place.c, 1, keepdims=False),
        lax.dynamic_index_in_dim(everything, place.c ^ m, 1, keepdims=False),
    ]
    smalls = []
    for layer in range(2):
        rows = [jnp.concatenate([p[layer, i * piece : (i + 1) * piece] for p in pair]) for i in range(6)]
        rest = everything[layer, :, 6 * piece :]
        size = 6 * (hd // n)
        qkv_b = rest[:, :size].reshape(n, 3, 2, hd // n)
        qkv_b = jnp.transpose(qkv_b, (2, 1, 0, 3)).reshape(2, 3 * hd)
        fc1_b = rest[:, size:].reshape(2, ff // 2)
        smalls.append(
            {
                "g1": rows[0],
                "b1": rows[1],
                "g2": rows[2],
                "b2": rows[3],
                "out_bias": rows[4] + rows[5],
                "qkv_bias": lax.dynamic_index_in_dim(qkv_b, k, 0, keepdims=False),
                "fc1_bias": lax.dynamic_index_in_dim(fc1_b, k, 0, keepdims=False),
            }
        )

    code = (place.cl * nt + place.t) * 2 + k
    count = seq // block
    absolute = jnp.arange(count, dtype=jnp.int32) ^ code
    half_rows = nt // 2
    source = absolute // nt
    part = (absolute // half_rows) % 2
    index = ((part ^ k) * n + source) * half_rows + absolute % half_rows
    slot = (absolute[:, None] * block + jnp.arange(block, dtype=jnp.int32)[None]).reshape(-1)
    per_block = seq // block_pos.shape[1]
    order = lax.dynamic_index_in_dim(block_pos, place.y, 0, keepdims=False)
    hit = (slot // per_block)[:, None] == jnp.arange(block_pos.shape[1], dtype=jnp.int32)[None]
    pos = jnp.sum(jnp.where(hit, order[None], 0), axis=1) * per_block + slot % per_block
    tables = rotary_tables(pos) + (pos,)

    h = spread_tokens(place, x_in, index)
    grad = spread_tokens(place, cotangent, index)
    saved = []
    for layer in range(2):
        out, kept = layer_forward(place, h, layers[layer], smalls[layer], tables)
        saved.append(kept)
        if layer == 0:
            h = place.gather_tensor(out.astype(BF))
    results = [None, None]
    for layer in (1, 0):
        grad_in, weights, gains, biases = layer_backward(
            place, grad, layers[layer], smalls[layer], tables, saved[layer]
        )
        results[layer] = (weights, gains, biases)
        if layer == 1:
            grad = place.gather_tensor(grad_in.astype(BF))

    boundary = deliver(place, out, grad_in)

    finals = []
    for i in range(4):
        first, second = results[0][0][i], results[1][0][i]
        to_second = lax.ppermute(second.astype(BF), SECTION, [(0, 1)])
        to_first = lax.ppermute(first.astype(BF), SECTION, [(1, 0)])
        mine = jnp.where(is_first, first, second)
        other = jnp.where(is_first, to_first, to_second).astype(F32)
        finals.append((jnp.where(is_first, mine, other), jnp.where(is_first, other, mine)))
    g_qkv = jnp.stack([v.reshape(piece, 3, hd) for v in finals[0]], axis=2)[None]
    g_out = jnp.stack(finals[1])[None]
    g_up = jnp.concatenate(finals[2], axis=1)[None]
    g_down = jnp.concatenate(finals[3], axis=0)[None]

    def flat(layer):
        _, gains, biases = results[layer]
        return gains.reshape(5, 2, piece), biases

    packed = [jnp.concatenate([flat(layer)[0][:, 1].reshape(-1), flat(layer)[1]]) for layer in range(2)]
    packed = place.over_y(jnp.stack(packed))
    sums = []
    for layer in range(2):
        gains, biases = flat(layer)
        sums.append(jnp.concatenate([gains[:, 0].reshape(-1), biases]) + packed[layer])
    mine = jnp.where(is_first, sums[0], sums[1])
    other = place.over_k(jnp.where(is_first, sums[1], sums[0]))
    norms = mine[: 4 * piece] + other[: 4 * piece]
    total = norms
    for s in range(1, nt):
        total = total + place.over_z(norms, s)
    total = total.reshape(4, 1, piece)
    token_sum = mine[4 * piece : 5 * piece][None]
    tail_mine, tail_other = mine[5 * piece :], other[5 * piece :]
    low = jnp.where(is_first, tail_mine, tail_other)
    high = jnp.where(is_first, tail_other, tail_mine)
    tails = jnp.stack([low, high])
    qkv_b = jnp.transpose(tails[:, : 3 * hd].reshape(2, 3, hd), (1, 0, 2))
    qkv_b = lax.dynamic_slice_in_dim(qkv_b, place.c * (hd // n), hd // n, axis=2)[None]
    fc1_b = lax.dynamic_slice_in_dim(tails[:, 3 * hd :].reshape(-1), place.c * (ff // n), ff // n)[None, None]
    return (
        boundary,
        total[0],
        total[1],
        total[2],
        total[3],
        g_qkv,
        qkv_b,
        g_out,
        token_sum,
        g_up,
        fc1_b,
        g_down,
        token_sum,
    )


SHIFT = ROT // 2


def run(kernel, outs, args, flops=0, grid=None, in_specs=None, out_specs=None, scratch=(), scalars=0, vmem=None):
    moved = sum(a.size * a.dtype.itemsize for a in args) + sum(
        int(jnp.dtype(o.dtype).itemsize) * o.size for o in outs
    )
    params = {"vmem_limit_bytes": (vmem or 40) << 20}
    extra = {}
    if in_specs is not None:
        extra["in_specs"], extra["out_specs"] = in_specs, out_specs
    spec = pltpu.PrefetchScalarGridSpec(
        num_scalar_prefetch=scalars, grid=grid or (), scratch_shapes=list(scratch), **extra
    ) if (grid or scalars or scratch) else None
    keywords = {"grid_spec": spec} if spec is not None else {}
    return pl.pallas_call(
        kernel,
        out_shape=outs,
        compiler_params=pltpu.CompilerParams(**params),
        cost_estimate=pl.CostEstimate(flops=flops, bytes_accessed=moved, transcendentals=0),
        **keywords,
    )(*args)


def scalar(*values):
    return jnp.stack([v.astype(jnp.int32) for v in values])


def shape(dims, dtype=BF):
    return jax.ShapeDtypeStruct(dims, dtype)


def as_row(*columns):
    rows = columns[0].shape[0]
    lane = lax.broadcasted_iota(jnp.int32, (rows, 128), 1)
    packed = jnp.zeros((rows, 128), F32)
    for i, column in enumerate(columns):
        packed = jnp.where(lane == i, column, packed)
    return packed.T[:8]


def as_columns(rows):
    wide = jnp.concatenate([rows, jnp.zeros((120, rows.shape[1]), F32)], axis=0)
    return wide.T


def row_stats(h_ref, stat_ref):
    wide = h_ref[...].astype(F32)
    mean = jnp.mean(wide, axis=-1, keepdims=True)
    centre = wide - mean
    spread = jnp.sum(centre * centre, axis=-1, keepdims=True)
    stat_ref[...] = as_row(mean, spread)


def assemble_kernel(with_stats, *refs):
    pieces, h_ref = refs[:8], refs[8]
    block = pieces[0].shape[0] // 2
    for s in range(4):
        for u in range(2):
            piece = pieces[s * 2 + u]
            for r in range(2):
                start = r * 8 * block + s * 2 * block + u * block
                h_ref[start : start + block, :] = piece[r * block : (r + 1) * block, :]
    if with_stats:
        row_stats(h_ref, refs[9])


def assemble(pieces, with_stats):
    rows, width = pieces[0].shape
    outs = [shape((8 * rows, width))]
    if with_stats:
        outs.append(shape((8, 8 * rows), F32))

    def kernel(*refs):
        assemble_kernel(with_stats, *refs)

    return run(kernel, outs, pieces)


EXTRA = 16


def pack_tokens(place, v, vector):
    _, tokens, full = v.shape
    half = tokens // 2
    width = full // 4
    extra = EXTRA if vector is not None else 0

    def kernel(at, v_ref, *refs):
        k, c = at[0], at[1]
        outs = refs[-4:]
        rows = pl.ds(pl.multiple_of(k * half, half), half)
        for d in range(4):
            there = c ^ d
            micro = there // 2
            first = pl.ds(pl.multiple_of(there * width, width), width)
            second = pl.ds(pl.multiple_of((there ^ 2) * width, width), width)
            outs[d][:half, :width] = v_ref[micro, rows, first].astype(BF)
            outs[d][:half, width:] = v_ref[micro, rows, second].astype(BF)
            if extra:
                outs[d][half:, :width] = refs[0][...]
                outs[d][half:, width:] = jnp.zeros((extra, width), BF)

    return run(
        kernel,
        [shape((half + extra, 2 * width))] * 4,
        [scalar(place.k, place.c), v] + ([vector] if extra else []),
        scalars=1,
    )


def send_tokens(place, v, vector):
    parts = pack_tokens(place, v, vector)
    got = [parts[0]]
    for d in (1, 2, 3):
        got.append(swap(parts[d], CTX, d))
    out = []
    for g in got:
        out += [g, place.over_k(g)]
    return out


def unpack_tokens(place, pieces, with_stats):
    extra = EXTRA if with_stats else 0
    stride, width = pieces[0].shape
    half = stride - extra
    block = half // 2
    rows = 8 * half
    piece = width // 2

    def kernel(at, *refs):
        got, h_ref, flat = refs[:8], refs[8], refs[-1]
        k, c, t = at[0], at[1], at[2]
        for i in range(8):
            flat[i * stride : (i + 1) * stride, :] = got[i][...]
        code = ((c % 2) * 4 + t) * 2 + k
        for j in range(16):
            a = code ^ j
            d = (a // 4) ^ c
            u = ((a // 2) % 2) ^ k
            start = (d * 2 + u) * stride + (a % 2) * block
            h_ref[j * block : (j + 1) * block, :] = flat[pl.ds(pl.multiple_of(start, 16), block), :]
        if with_stats:
            row_stats(h_ref, refs[9])
            for layer in range(2):
                for d in range(4):
                    start = (d * 2 + (k ^ layer)) * stride + half
                    lines = flat[pl.ds(pl.multiple_of(start, 16), extra), :piece].astype(F32)
                    refs[11][layer, d, :, :] = lines
                    if d % 2 == 0:
                        refs[10][layer, :, (d // 2) * piece : (d // 2 + 1) * piece] = lines

    outs = [shape((rows, width))]
    if with_stats:
        outs += [shape((8, rows), F32), shape((2, extra, width), F32), shape((2, 4, extra, piece), F32)]
    return run(
        kernel,
        outs,
        [scalar(place.k, place.c, place.t), *pieces],
        scalars=1,
        scratch=[pltpu.VMEM((8 * stride, width), BF)],
    )


def norm_inputs(h, stat, stat_x, vec):
    rows, width = h.shape
    own = rows // 2

    def kernel(h_ref, stat_ref, stat_x_ref, vec_ref, attn_ref, mlp_ref, cols_ref):
        there = stat_x_ref[...]
        there = jnp.concatenate([there[:, own:], there[:, :own]], axis=1)
        here = stat_ref[...]
        delta = there[0:1] - here[0:1]
        mean = here[0:1] + 0.5 * delta
        spread = here[1:2] + there[1:2] + delta * delta * (width * 0.5)
        inv = lax.rsqrt(spread / (2 * width) + EPS)
        columns = as_columns(jnp.concatenate([mean, inv, jnp.zeros((6, rows), F32)], axis=0))
        cols_ref[...] = columns
        vec = vec_ref[...]
        for r in range(0, rows, 64):
            part = slice(r, r + 64)
            normed = (h_ref[part, :].astype(F32) - columns[part, 0:1]) * columns[part, 1:2]
            attn_ref[part, :] = (normed * vec[0:1] + vec[1:2]).astype(BF)
            mlp_ref[part, :] = (normed * vec[2:3] + vec[3:4]).astype(BF)

    return run(
        kernel,
        [shape((rows, width)), shape((rows, width)), shape((rows, 128), F32)],
        [h, stat, stat_x, vec],
    )


def product_qkv(attn_in, w_qkv):
    rows, width = attn_in.shape
    own, piece = rows // 2, width // 2
    hd = w_qkv[0].shape[1] // 3

    def kernel(a_ref, w0, w1, q_ref, send_ref):
        first, second = a_ref[:, :piece], a_ref[:, piece:]
        kv = dot(first, w0[:, hd:]) + dot(second, w1[:, hd:])
        send_ref[:, : 2 * hd] = kv.astype(BF)
        q = dot(first, w0[:, :hd]) + dot(second, w1[:, :hd])
        q_ref[...] = q[:own].astype(BF)
        send_ref[:own, 2 * hd :] = q[own:, :128].astype(BF)
        send_ref[own:, 2 * hd :] = q[own:, 128:].astype(BF)

    return run(
        kernel,
        [shape((own, hd)), shape((rows, 2 * hd + 128))],
        [attn_in, *w_qkv],
        flops=6 * rows * width * hd,
    )


def product_up(mlp_in, w_up):
    rows, width = mlp_in.shape
    own, piece = rows // 2, width // 2
    ff = w_up[0].shape[1]

    def kernel(m_ref, w0, w1, own_ref, send_ref):
        for r, ref in ((slice(own, rows), send_ref), (slice(0, own), own_ref)):
            ref[...] = (dot(m_ref[r, :piece], w0[...]) + dot(m_ref[r, piece:], w1[...])).astype(BF)

    return run(kernel, [shape((own, ff))] * 2, [mlp_in, *w_up], flops=2 * rows * width * ff)


def unfold(ref, hd):
    own = ref.shape[0] // 2
    return jnp.concatenate([ref[:own, 2 * hd :], ref[own:, 2 * hd :]], axis=1)


def turn_in(z, tables, inverse):
    cosine, low, high = tables
    lead = z[:, :128]
    left = pltpu.roll(lead, 128 - SHIFT, axis=1)
    right = pltpu.roll(lead, SHIFT, axis=1)
    mixed = left * low + right * high
    lead = lead * cosine - mixed if inverse else lead * cosine + mixed
    return jnp.concatenate([lead, z[:, 128:]], axis=1)


def attention(q_own, kv_own, kv_got, bias, tables, pos_row):
    rows = kv_own.shape[0]
    own, hd = q_own.shape
    scaling = hd**-0.5

    def kernel(qo, kvo, kvg, b_ref, cos_ref, low_ref, high_ref, pos_ref, q_ref, k_ref, v_ref, p_ref, o_ref):
        b = b_ref[0:1, :]
        tab = (cos_ref[...], low_ref[...], high_ref[...])
        q = qo[...].astype(F32) + unfold(kvg, hd).astype(F32) + b[:, :hd]
        q = turn_in(q, tuple(a[:own] for a in tab), False).astype(BF)
        kv = jnp.concatenate(
            [
                kvo[:own, : 2 * hd].astype(F32) + kvg[own:, : 2 * hd].astype(F32),
                kvo[own:, : 2 * hd].astype(F32) + kvg[:own, : 2 * hd].astype(F32),
            ],
            axis=0,
        ) + b[:, hd:]
        k = turn_in(kv[:, :hd], tab, False).astype(BF)
        v = kv[:, hd:].astype(BF)
        q_ref[...], k_ref[...], v_ref[...] = q, k, v
        pos = pos_ref[...]
        column = as_columns(pos)[:own, 0:1]
        scores = dot(q, k, ((1,), (1,))) * scaling
        allowed = column >= pos[0:1, :]
        scores = jnp.where(allowed, scores, MASKED_SCORE)
        top = jnp.max(scores, axis=-1, keepdims=True)
        exps = jnp.where(allowed, jnp.exp(scores - top), 0.0)
        total = jnp.sum(exps, axis=-1, keepdims=True)
        o_ref[...] = (dot(exps.astype(BF), v) / total).astype(BF)
        p_ref[...] = exps / total

    return run(
        kernel,
        [shape((own, hd)), shape((rows, hd)), shape((rows, hd)), shape((own, rows), F32), shape((own, hd))],
        [q_own, kv_own, kv_got, bias, *tables, pos_row],
        flops=4 * own * rows * hd,
    )


def split_rows(ref_keep, ref_send, value, r, block):
    for s in range(4):
        at = (r * 4 + s) * block
        ref_keep[at : at + block, :] = value[2 * s * block : (2 * s + 1) * block].astype(BF)
        ref_send[at : at + block, :] = value[(2 * s + 1) * block : (2 * s + 2) * block].astype(BF)


def second_products(acts, attns, w_cat):
    own, ff = acts[0].shape
    hd = attns[0].shape[1]
    piece = w_cat[0].shape[1]
    block = own // 8

    def kernel(a0, a1, t0, t1, w0, w1, keep_ref, send_ref):
        for r, (a, t) in enumerate(((a0, t0), (a1, t1))):
            for j, w in enumerate((w0, w1)):
                columns = pl.ds(j * piece, piece)
                value = dot(a[...], w[:ff, :]) + dot(t[...], w[ff:, :])
                split_rows(keep_ref.at[:, columns], send_ref.at[:, columns], value, r, block)

    return run(
        kernel,
        [shape((own, 2 * piece))] * 2,
        [*acts, *attns, *w_cat],
        flops=8 * own * piece * (ff + hd),
    )


def cut_tensor(keep, got):
    rows, width = keep.shape
    block = rows // 8

    def kernel(keep_ref, got_ref, own_ref, *sends):
        for r in range(2):
            for s in range(4):
                at = slice((r * 4 + s) * block, (r * 4 + s + 1) * block)
                value = keep_ref[at, :].astype(F32) + got_ref[at, :].astype(F32)
                to = slice(r * block, (r + 1) * block)
                if s == 0:
                    own_ref[to, :] = value
                else:
                    sends[s - 1][to, :] = value.astype(BF)

    small = shape((2 * block, width))
    return run(kernel, [shape((2 * block, width), F32), small, small, small], [keep, got])


def sum_tensor(place, keep, send):
    got = place.over_k(send)
    own, *sends = cut_tensor(keep, got)
    parts = []
    for s, v in enumerate(sends):
        parts.append(place.over_z(v, s + 1))
    return own, parts


def spread_tensor(place, v):
    got = [v]
    for s in (1, 2, 3):
        got.append(place.over_z(v, s))
    out = []
    for g in got:
        out += [g, place.over_k(g)]
    return out


def own_rows(ref, block):
    half = ref.shape[0] // 2
    return jnp.concatenate([ref[:block, :], ref[half : half + block, :]], axis=0)


def residual(own, parts, h, vec, dtype):
    rows, width = own.shape
    block = rows // 2

    def kernel(own_ref, p1, p2, p3, h_ref, vec_ref, out_ref):
        total = own_ref[...] + p1[...].astype(F32) + p2[...].astype(F32) + p3[...].astype(F32)
        out_ref[...] = (own_rows(h_ref, block).astype(F32) + total + vec_ref[4:5, :] + vec_ref[5:6, :]).astype(dtype)

    return run(kernel, [shape((rows, width), dtype)], [own, *parts, h, vec])[0]


def first_grads(grad, w_cat, hd):
    rows, width = grad.shape
    own, piece = rows // 2, width // 2
    total = w_cat[0].shape[0]
    last = ((1,), (1,))

    def kernel(g_ref, w0, w1, own_ref, send_ref):
        for lines, at in ((slice(total - hd, total), slice(0, hd)), (slice(0, total - hd), slice(hd, total))):
            value = dot(g_ref[:, :piece], w0[lines, :], last) + dot(g_ref[:, piece:], w1[lines, :], last)
            own_ref[:, at] = value[:own].astype(BF)
            send_ref[:, at] = value[own:].astype(BF)

    return run(kernel, [shape((own, total))] * 2, [grad, *w_cat], flops=2 * rows * width * total)


def attention_grads(d_own, d_got, attn_out, probs, queries, keys, values, tables):
    own, hd = queries.shape
    rows = keys.shape[0]
    scaling = hd**-0.5

    def kernel(do, dg, o_ref, p_ref, q_ref, k_ref, v_ref, cos_ref, low_ref, high_ref, out_ref):
        grad = (do[...].astype(F32) + dg[...].astype(F32)).astype(BF)
        row_dot = jnp.sum(grad.astype(F32) * o_ref[...].astype(F32), axis=-1, keepdims=True)
        d_prob = dot(grad, v_ref[...], ((1,), (1,)))
        probs = p_ref[...]
        d_score = (probs * (d_prob - row_dot)).astype(BF)
        tab = (cos_ref[...], low_ref[...], high_ref[...])
        dq = dot(d_score, k_ref[...]) * scaling
        dq = turn_in(dq, tuple(a[:own] for a in tab), True).astype(BF)
        out_ref[:own, 2 * hd :] = dq[:, :128]
        out_ref[own:, 2 * hd :] = dq[:, 128:]
        dk = dot(d_score, q_ref[...], ((0,), (0,))) * scaling
        out_ref[:, :hd] = turn_in(dk, tab, True).astype(BF)
        out_ref[:, hd : 2 * hd] = dot(probs.astype(BF), grad, ((0,), (0,))).astype(BF)

    part = pl.BlockSpec((own, hd), lambda i: (0, 0))
    args = [d_own, d_got, attn_out, probs, queries, keys, values, *tables]
    return run(
        kernel,
        [shape((rows, 2 * hd + 128))],
        args,
        flops=8 * own * rows * hd,
        grid=(1,),
        in_specs=[part, part] + [pl.BlockSpec(a.shape, lambda i: (0, 0)) for a in args[2:]],
        out_specs=[pl.BlockSpec((rows, 2 * hd + 128), lambda i: (0, 0))],
    )[0]


def second_grads(pres, dkv_own, dkv_got, w_qkv, w_up, h, cols, grad, vec):
    rows, width = h.shape
    own = rows // 2
    piece = width // 2
    block = own // 8
    hd, ff = w_qkv[0].shape[1] // 3, pres[0].shape[1]
    last = ((1,), (1,))

    def kernel(p0, p1, kvo, kvg, wq0, wq1, wu0, wu1, h_ref, c_ref, g_ref, vec_ref, *refs):
        keep_ref, send_ref, gain_ref, bq_ref, bf_ref, dqkv_ref = refs
        fill_qkv(dqkv_ref, kvo, kvg, hd)
        zero = jnp.zeros((3, width), F32)
        sums = [[jnp.zeros((1, piece), F32) for _ in range(5)] for _ in range(2)]
        for r in range(2):
            at = slice(r * own, (r + 1) * own)
            p = (p0, p1)[r][...]
            qkv = dqkv_ref[at, :]
            for j in range(2):
                cut = slice(j * piece, (j + 1) * piece)
                d_mlp = dot(p, (wu0, wu1)[j][...], last)
                d_attn = dot(qkv, (wq0, wq1)[j][...], last)
                normed = (h_ref[at, cut].astype(F32) - c_ref[at, 0:1]) * c_ref[at, 1:2]
                both = d_attn * vec_ref[0:1, cut] + d_mlp * vec_ref[2:3, cut]
                split_rows(keep_ref.at[:, pl.ds(j * piece, piece)], send_ref.at[:, pl.ds(j * piece, piece)], both, r, block)
                add = (d_attn * normed, d_attn, d_mlp * normed, d_mlp, g_ref[at, cut].astype(F32))
                for i, v in enumerate(add):
                    sums[j][i] = sums[j][i] + jnp.sum(v, axis=0, keepdims=True)
        gain_ref[...] = jnp.concatenate(
            [jnp.concatenate([sums[0][i], sums[1][i]], axis=1) for i in range(5)] + [zero], axis=0
        )
        bq = jnp.sum(dqkv_ref[...].astype(F32), axis=0, keepdims=True)
        bf = jnp.sum(p0[...].astype(F32), axis=0, keepdims=True) + jnp.sum(p1[...].astype(F32), axis=0, keepdims=True)
        bq_ref[...] = jnp.broadcast_to(bq, (8, 3 * hd))
        bf_ref[...] = jnp.broadcast_to(bf, (8, ff))

    return run(
        kernel,
        [
            shape((own, width)),
            shape((own, width)),
            shape((8, width), F32),
            shape((8, 3 * hd), F32),
            shape((8, ff), F32),
        ],
        [*pres, dkv_own, dkv_got, *w_qkv, *w_up, h, cols, grad, vec],
        flops=2 * rows * width * (3 * hd + ff),
        scratch=[pltpu.VMEM((rows, 3 * hd), BF)],
    )


def own_stats(own, parts, h, cols):
    rows, width = own.shape
    block = rows // 2

    def kernel(own_ref, p1, p2, p3, h_ref, c_ref, comb_ref, sums_ref):
        comb = own_ref[...] + p1[...].astype(F32) + p2[...].astype(F32) + p3[...].astype(F32)
        comb_ref[...] = comb
        c = own_rows(c_ref, block)
        normed = (own_rows(h_ref, block).astype(F32) - c[:, 0:1]) * c[:, 1:2]
        lane = lax.broadcasted_iota(jnp.int32, (rows, 128), 1)
        first = jnp.sum(comb, axis=-1, keepdims=True)
        second = jnp.sum(comb * normed, axis=-1, keepdims=True)
        sums_ref[...] = jnp.where(lane == 0, first, second)

    return run(kernel, [shape((rows, width), F32), shape((rows, 128), F32)], [own, *parts, h, cols])


def input_grad(comb, sums, got, h, cols, grad):
    rows, width = comb.shape
    block = rows // 2

    def kernel(comb_ref, s_ref, g_ref, h_ref, c_ref, grad_ref, out_ref):
        c = own_rows(c_ref, block)
        normed = (own_rows(h_ref, block).astype(F32) - c[:, 0:1]) * c[:, 1:2]
        there = g_ref[...]
        total = (s_ref[...] + jnp.concatenate([there[block:], there[:block]], axis=0)) / (2 * width)
        change = comb_ref[...] - total[:, 0:1] - normed * total[:, 1:2]
        out_ref[...] = (own_rows(grad_ref, block).astype(F32) + c[:, 1:2] * change).astype(BF)

    return run(kernel, [shape((rows, width))], [comb, sums, got, h, cols, grad])[0]


def grads_cat(acts, attns, grad):
    own, ff = acts[0].shape
    hd = attns[0].shape[1]
    width = grad.shape[1]
    piece = width // 2
    first = ((0,), (0,))

    def kernel(a0, a1, t0, t1, g_ref, own_ref, send_ref):
        for lines, left in ((slice(0, ff), (a0, a1)), (slice(ff, ff + hd), (t0, t1))):
            for j, ref in ((1, send_ref), (0, own_ref)):
                cut = slice(j * piece, (j + 1) * piece)
                value = dot(left[0][...], g_ref[:own, cut], first) + dot(left[1][...], g_ref[own:, cut], first)
                ref[lines, :] = value.astype(BF)

    return run(
        kernel,
        [shape((ff + hd, piece))] * 2,
        [*acts, *attns, grad],
        flops=4 * own * width * (ff + hd),
    )


def grads_up(mlp_in, pres):
    rows, width = mlp_in.shape
    own, piece = rows // 2, width // 2
    ff = pres[0].shape[1]
    first = ((0,), (0,))

    def kernel(m_ref, p0, p1, own_ref, send_ref):
        for j, ref in ((1, send_ref), (0, own_ref)):
            cut = slice(j * piece, (j + 1) * piece)
            value = dot(m_ref[:own, cut], p0[...], first) + dot(m_ref[own:, cut], p1[...], first)
            ref[...] = value.astype(BF)

    return run(kernel, [shape((piece, ff))] * 2, [mlp_in, *pres], flops=2 * rows * width * ff)


def fill_qkv(out_ref, own_ref, got_ref, hd):
    half = out_ref.shape[0] // 2
    for r in range(2):
        at = slice(r * half, (r + 1) * half)
        cross = slice((1 - r) * half, (2 - r) * half)
        out_ref[at, :hd] = unfold((own_ref, got_ref)[r], hd)
        both = own_ref[at, : 2 * hd].astype(F32) + got_ref[cross, : 2 * hd].astype(F32)
        out_ref[at, hd:] = both.astype(BF)


def grads_qkv(attn_in, dkvq_own, dkvq_got, hd):
    rows, width = attn_in.shape
    piece = width // 2

    def kernel(a_ref, do_ref, dg_ref, own_ref, send_ref, full):
        fill_qkv(full, do_ref, dg_ref, hd)
        for j, ref in ((1, send_ref), (0, own_ref)):
            value = dot(a_ref[:, j * piece : (j + 1) * piece], full[...], ((0,), (0,)))
            ref[...] = value.astype(BF)

    return run(
        kernel,
        [shape((piece, 3 * hd))] * 2,
        [attn_in, dkvq_own, dkvq_got],
        flops=6 * rows * width * hd,
        scratch=[pltpu.VMEM((rows, 3 * hd), BF)],
    )


def prepare_up(place, fc1):
    piece, full = fc1.shape
    part = piece // 4

    def kernel(at, in_ref, out_ref):
        out_ref[...] = in_ref[...]

    return run(
        kernel,
        [shape((piece, full // 2))],
        [scalar(place.k), fc1],
        grid=(4,),
        scalars=1,
        in_specs=[pl.BlockSpec((part, full // 2), lambda i, at: (i, 1 - at[0]))],
        out_specs=[pl.BlockSpec((part, full // 2), lambda i, at: (i, 0))],
    )[0]


def pick_up(place, fc1, got, layer):
    piece, full = fc1.shape
    part = piece // 4

    def kernel(at, own_ref, got_ref, out_ref):
        @pl.when(at[0] == layer)
        def _():
            out_ref[...] = own_ref[...]

        @pl.when(at[0] != layer)
        def _():
            out_ref[...] = got_ref[...]

    return run(
        kernel,
        [shape((piece, full // 2))],
        [scalar(place.k), fc1, got],
        grid=(4,),
        scalars=1,
        in_specs=[
            pl.BlockSpec((part, full // 2), lambda i, at: (jnp.where(at[0] == layer, i, 0), layer)),
            pl.BlockSpec((part, full // 2), lambda i, at: (jnp.where(at[0] == layer, 0, i), 0)),
        ],
        out_specs=[pl.BlockSpec((part, full // 2), lambda i, at: (i, 0))],
    )[0]


def pick_qkv(place, keep, got, layer):
    piece, width = keep.shape
    part = piece // 4

    def kernel(at, own_ref, got_ref, out_ref):
        @pl.when(at[0] == layer)
        def _():
            out_ref[...] = own_ref[...]

        @pl.when(at[0] != layer)
        def _():
            out_ref[...] = got_ref[...]

    return run(
        kernel,
        [shape((piece, width))],
        [scalar(place.k), keep, got],
        grid=(4,),
        scalars=1,
        in_specs=[
            pl.BlockSpec((part, width), lambda i, at: (jnp.where(at[0] == layer, i, 0), 0)),
            pl.BlockSpec((part, width), lambda i, at: (jnp.where(at[0] == layer, 0, i), 0)),
        ],
        out_specs=[pl.BlockSpec((part, width), lambda i, at: (i, 0))],
    )[0]


def prepare_cat(place, fc2, dense):
    full, piece = fc2.shape
    ff, hd = full // 2, dense.shape[0] // 2
    tiles = ff // hd

    def kernel(at, down_ref, out_w_ref, out_ref):
        @pl.when(pl.program_id(0) < tiles)
        def _():
            out_ref[...] = down_ref[...]

        @pl.when(pl.program_id(0) >= tiles)
        def _():
            out_ref[...] = out_w_ref[...]

    return run(
        kernel,
        [shape((ff + hd, piece))],
        [scalar(place.k), fc2, dense],
        grid=(tiles + 1,),
        scalars=1,
        in_specs=[
            pl.BlockSpec((hd, piece), lambda i, at: ((1 - at[0]) * tiles + jnp.minimum(i, tiles - 1), 0)),
            pl.BlockSpec((hd, piece), lambda i, at: (1 - at[0], 0)),
        ],
        out_specs=[pl.BlockSpec((hd, piece), lambda i, at: (i, 0))],
    )[0]


def pick_cat(place, fc2, dense, got, layer):
    full, piece = fc2.shape
    ff, hd = full // 2, dense.shape[0] // 2
    tiles = ff // hd

    def kernel(at, down_ref, out_w_ref, got_ref, out_ref):
        own, i = at[0] == layer, pl.program_id(0)

        @pl.when(own & (i < tiles))
        def _():
            out_ref[...] = down_ref[...]

        @pl.when(own & (i >= tiles))
        def _():
            out_ref[...] = out_w_ref[...]

        @pl.when(at[0] != layer)
        def _():
            out_ref[...] = got_ref[...]

    return run(
        kernel,
        [shape((ff + hd, piece))],
        [scalar(place.k), fc2, dense, got],
        grid=(tiles + 1,),
        scalars=1,
        in_specs=[
            pl.BlockSpec(
                (hd, piece),
                lambda i, at: (layer * tiles + jnp.where(at[0] == layer, jnp.minimum(i, tiles - 1), 0), 0),
            ),
            pl.BlockSpec((hd, piece), lambda i, at: (layer, 0)),
            pl.BlockSpec((hd, piece), lambda i, at: (jnp.where(at[0] == layer, 0, i), 0)),
        ],
        out_specs=[pl.BlockSpec((hd, piece), lambda i, at: (i, 0))],
    )[0]


def sum_for_owner(place, ours, theirs):
    rows, width = ours[0].shape
    part = 256
    steps = rows // part

    def kernel(at, o0, o1, y0, y1, out_ref):
        for layer, (o, y) in enumerate(((o0, y0), (o1, y1))):
            @pl.when(at[0] != layer)
            def _():
                out_ref[...] = (o[...].astype(F32) + y[...].astype(F32)).astype(BF)

    def block(layer):
        return pl.BlockSpec((part, width), lambda i, at: (jnp.where(at[0] != layer, i, 0), 0))

    return run(
        kernel,
        [shape((rows, width))],
        [scalar(place.k), *ours, *theirs],
        grid=(steps,),
        scalars=1,
        in_specs=[block(0), block(1)] * 2,
        out_specs=[pl.BlockSpec((part, width), lambda i, at: (i, 0))],
    )[0]


def finish(place, ours, theirs, arrived, by_row, start, half_shape):
    rows, width = half_shape
    steps = 4 if rows >= 512 else 1
    part = rows // steps
    first = start // part if by_row else start // width

    def kernel(at, o0, o1, y0, y1, d_ref, out_ref):
        k = at[0]

        def put(half, value):
            if by_row:
                out_ref[half, :, :] = value
            else:
                out_ref[:, half * width : (half + 1) * width] = value

        for layer, (o, y) in enumerate(((o0, y0), (o1, y1))):
            @pl.when(k == layer)
            def _():
                put(layer, o[...].astype(F32) + y[...].astype(F32))
                put(1 - layer, d_ref[...].astype(F32))

    def block(layer):
        chosen = lambda i, at: i if layer is None else jnp.where(at[0] == layer, i, 0)
        if by_row:
            return pl.BlockSpec((part, width), lambda i, at: (first + chosen(i, at), 0))
        return pl.BlockSpec((part, width), lambda i, at: (chosen(i, at), first))

    if by_row:
        out = shape((2, rows, width), F32)
        out_spec = pl.BlockSpec((2, part, width), lambda i, at: (0, i, 0))
    else:
        out = shape((rows, 2 * width), F32)
        out_spec = pl.BlockSpec((part, 2 * width), lambda i, at: (i, 0))
    return run(
        kernel,
        [out],
        [scalar(place.k), *ours, *theirs, arrived],
        grid=(steps,),
        scalars=1,
        in_specs=[block(0), block(1), block(0), block(1), block(None)],
        out_specs=[out_spec],
    )[0]


def finish_qkv(place, ours, theirs, arrived):
    rows, width = ours[0].shape
    steps = 4
    part = rows // steps
    lines = 2 * width // 128

    def kernel(at, o0, o1, y0, y1, d_ref, out_ref):
        k = at[0]
        for layer, (o, y) in enumerate(((o0, y0), (o1, y1))):
            @pl.when(k == layer)
            def _():
                for chunk in range(width // 128):
                    cut = slice(chunk * 128, (chunk + 1) * 128)
                    mine = o[:, cut].astype(F32) + y[:, cut].astype(F32)
                    out_ref[pl.ds(2 * chunk + layer, part, stride=lines), :] = mine
                    other = d_ref[:, cut].astype(F32)
                    out_ref[pl.ds(2 * chunk + 1 - layer, part, stride=lines), :] = other

    def block(layer):
        chosen = lambda i, at: i if layer is None else jnp.where(at[0] == layer, i, 0)
        return pl.BlockSpec((part, width), lambda i, at: (chosen(i, at), 0))

    out = run(
        kernel,
        [shape((rows * lines, 128), F32)],
        [scalar(place.k), *ours, *theirs, arrived],
        grid=(steps,),
        scalars=1,
        in_specs=[block(0), block(1), block(0), block(1), block(None)],
        out_specs=[pl.BlockSpec((part * lines, 128), lambda i, at: (i, 0))],
    )[0]
    hd = width // 3
    out = out.reshape(rows, 3, hd // 128, 2, 128)
    return jnp.transpose(out, (0, 1, 3, 2, 4)).reshape(1, rows, 3, 2, hd)


def split_heads(place, qkv_weight):
    piece, _, _, hd = qkv_weight.shape
    lines = qkv_weight.reshape(piece, 3, 2, hd // 128, 128)
    lines = jnp.transpose(lines, (0, 1, 3, 2, 4)).reshape(-1, 128)
    count = 6 * hd // 128

    def kernel(at, in_ref, keep_ref, send_ref, wide):
        wide[...] = in_ref[...].astype(F32)
        for chunk in range(count // 2):
            columns = pl.ds(chunk * 128, 128)
            keep_ref[:, columns] = wide[pl.ds(2 * chunk + at[0], piece, stride=count), :].astype(BF)
            send_ref[:, columns] = wide[pl.ds(2 * chunk + 1 - at[0], piece, stride=count), :].astype(BF)

    return run(
        kernel,
        [shape((piece, 3 * hd))] * 2,
        [scalar(place.k), lines],
        scalars=1,
        scratch=[pltpu.VMEM(lines.shape, F32)],
    )


def body_two(
    x_in,
    cotangent,
    block_pos,
    norm1_gain,
    norm1_bias,
    norm2_gain,
    norm2_bias,
    qkv_weight,
    qkv_bias,
    dense_weight,
    dense_bias,
    fc1_weight,
    fc1_bias,
    fc2_weight,
    fc2_bias,
):
    place = Place()
    k, n, nt = place.k, place.n, place.nt
    is_first = k == 0
    tokens = x_in.shape[1]
    seq = tokens * n
    block = tokens // nt
    piece = fc1_weight.shape[1]
    width = 2 * piece
    hd = dense_weight.shape[2]
    ff = fc1_weight.shape[2] // 2

    def x_swap(v):
        return place.over_x(v, 0)

    def y_swap(v):
        return place.over_y(v)

    heads_bias = jnp.pad(qkv_bias.reshape(1, -1), ((0, 0), (0, piece - qkv_bias.size)))
    rows = [norm1_gain, norm1_bias, norm2_gain, norm2_bias, dense_bias, fc2_bias, fc1_bias[0], heads_bias]
    vector = jnp.concatenate(rows + [jnp.zeros_like(heads_bias)] * (EXTRA - len(rows)), axis=0)
    x_pieces = send_tokens(place, x_in, vector)

    fc1, fc2 = fc1_weight[0], fc2_weight[0]
    dense = dense_weight.reshape(2 * hd, piece)

    def k_swap(v):
        return place.over_k(v)

    up_send = prepare_up(place, fc1)
    up_got = k_swap(up_send)
    head_keep, head_send = split_heads(place, qkv_weight[0])
    head_got = k_swap(head_send)
    cat_send = prepare_cat(place, fc2, dense)
    cat_got = k_swap(cat_send)
    layers = []
    for layer in range(2):
        mine_q = pick_qkv(place, head_keep, head_got, layer)
        mine_u = pick_up(place, fc1, up_got, layer)
        mine_c = pick_cat(place, fc2, dense, cat_got, layer)
        layers.append(((mine_q, y_swap(mine_q)), (mine_u, y_swap(mine_u)), (mine_c, y_swap(mine_c))))

    code = (place.cl * nt + place.t) * 2 + k
    absolute = jnp.arange(seq // block, dtype=jnp.int32) ^ code
    slot = (absolute[:, None] * block + jnp.arange(block, dtype=jnp.int32)[None]).reshape(-1)
    per_block = seq // block_pos.shape[1]
    order = jnp.where(place.y == 0, block_pos[0], block_pos[1])
    hit = (slot // per_block)[:, None] == jnp.arange(block_pos.shape[1], dtype=jnp.int32)[None]
    pos = jnp.sum(jnp.where(hit, order[None], 0), axis=1) * per_block + slot % per_block
    pos_row = jnp.broadcast_to(pos.astype(F32)[None], (8, seq))
    cosine, sine = rotary_tables(pos)
    blank = jnp.zeros((seq, 128 - ROT), F32)
    empty = jnp.zeros((seq, SHIFT), F32)
    tables = (
        jnp.concatenate([cosine, blank + 1.0], axis=1),
        jnp.concatenate([-sine[:, :SHIFT], empty, blank], axis=1),
        jnp.concatenate([empty, sine[:, SHIFT:], blank], axis=1),
    )

    h, stat, vecs, lines = unpack_tokens(place, x_pieces, True)
    by_place = jnp.take(lines[:, :, 6:8], jnp.arange(n, dtype=jnp.int32) ^ place.c, axis=1, mode="clip")
    qkv_biases, fc1_biases = [], []
    for layer in range(2):
        fc1_b = by_place[layer, :, 0].reshape(2, ff)
        qkv_b = by_place[layer, :, 1, : qkv_bias.size].reshape(n, 3, 2, hd // n)
        qkv_b = jnp.where(is_first, qkv_b[:, :, 0], qkv_b[:, :, 1])
        qkv_b = jnp.transpose(qkv_b, (1, 0, 2)).reshape(1, 3 * hd)
        qkv_biases.append(jnp.broadcast_to(qkv_b, (8, 3 * hd)))
        fc1_biases.append(jnp.where(is_first, fc1_b[0], fc1_b[1]))

    cot_pieces = send_tokens(place, cotangent, None)
    saved = []
    for layer in range(2):
        w_qkv, w_up, w_cat = layers[layer]
        stat_x = x_swap(stat)
        attn_in, mlp_in, cols = norm_inputs(h, stat, stat_x, vecs[layer])
        q_own, kvq = product_qkv(attn_in, w_qkv)
        f_own, f_send = product_up(mlp_in, w_up)
        kvq_got, f_got = x_swap(kvq), x_swap(f_send)
        queries, keys, values, probs, attn_out = attention(
            q_own, kvq, kvq_got, qkv_biases[layer], tables, pos_row
        )
        pre = f_own.astype(F32) + f_got.astype(F32) + fc1_biases[layer]
        cdf = 0.5 * (1.0 + lax.erf(pre * 0.7071067811865476))
        act = (pre * cdf).astype(BF)
        slope = cdf + pre * jnp.exp(-0.5 * pre * pre) * 0.3989422804014327
        acts = (act, x_swap(act))
        attns = (attn_out, x_swap(attn_out))
        keep, send = second_products(acts, attns, w_cat)
        own, parts = sum_tensor(place, keep, send)
        out = residual(own, parts, h, vecs[layer], BF)
        saved.append((h, cols, attn_in, mlp_in, queries, keys, values, probs, attn_out, attns, acts, slope))
        if layer == 0:
            pieces = spread_tensor(place, out)
            h, stat = assemble(pieces, True)
    grad = unpack_tokens(place, cot_pieces, False)[0]

    results = [None, None]
    for layer in (1, 0):
        w_qkv, w_up, w_cat = layers[layer]
        h, cols, attn_in, mlp_in, queries, keys, values, probs, attn_out, attns, acts, slope = saved[layer]
        ta_own, ta_send = first_grads(grad, w_cat, hd)
        ta_got = x_swap(ta_send)
        dkvq = attention_grads(ta_own, ta_got, attn_out, probs, queries, keys, values, tables)
        dkvq_got = x_swap(dkvq)
        d_pre = ((ta_own[:, hd:].astype(F32) + ta_got[:, hd:].astype(F32)) * slope).astype(BF)
        pres = (d_pre, x_swap(d_pre))
        keep, send, gains, bias_q, bias_f = second_grads(pres, dkvq, dkvq_got, w_qkv, w_up, h, cols, grad, vecs[layer])
        own, parts = sum_tensor(place, keep, send)
        comb, sums = own_stats(own, parts, h, cols)
        sums_got = x_swap(sums)
        grad_in = input_grad(comb, sums, sums_got, h, cols, grad)
        cat_own, cat_out = grads_cat(acts, attns, grad)
        up_own, up_out = grads_up(mlp_in, pres)
        qkv_own, qkv_out = grads_qkv(attn_in, dkvq, dkvq_got, hd)
        results[layer] = (
            (cat_own, y_swap(cat_out)),
            (up_own, y_swap(up_out)),
            (qkv_own, y_swap(qkv_out)),
            gains,
            bias_q[:1],
            bias_f[:1],
        )
        if layer == 1:
            pieces = spread_tensor(place, grad_in)
            grad = assemble(pieces, False)[0]

    boundary = deliver(place, out.reshape(2, block, width), grad_in.reshape(2, block, width))

    def to_owner(which):
        ours = [results[layer][which][0] for layer in range(2)]
        theirs = [results[layer][which][1] for layer in range(2)]
        sent = sum_for_owner(place, ours, theirs)
        return ours, theirs, k_swap(sent)

    cat, up, heads = to_owner(0), to_owner(1), to_owner(2)
    g_down = finish(place, *cat, True, 0, (ff, piece)).reshape(1, 2 * ff, piece)
    g_out = finish(place, *cat, True, ff, (hd, piece)).reshape(1, 2, hd, piece)
    g_up = finish(place, *up, False, 0, (piece, ff))[None]
    g_qkv = finish_qkv(place, *heads)

    norms = jnp.concatenate([results[layer][3] for layer in range(2)], axis=0)
    total = norms
    for s in range(1, nt):
        total = total + place.over_z(norms, s)
    rows_used = jnp.arange(16, dtype=jnp.int32)[:, None] % 8
    norms = jnp.where(rows_used == 4, norms, total)
    ends = [jnp.concatenate([results[layer][4], results[layer][5]], axis=1) for layer in range(2)]
    ours = jnp.concatenate([jnp.where(is_first, norms[:8], norms[8:]).reshape(1, -1), jnp.where(is_first, *ends)], axis=1)
    theirs = jnp.concatenate([jnp.where(is_first, norms[8:], norms[:8]).reshape(1, -1), jnp.where(is_first, *ends[::-1])], axis=1)
    got = k_swap(theirs)
    joined = jnp.concatenate([ours[:, : 8 * width] + got[:, : 8 * width], ours[:, 8 * width :], got[:, 8 * width :]], axis=1)
    joined = joined.reshape(1, -1)
    across = y_swap(joined)
    gain_mine = joined[0, : 8 * width].reshape(8, 2, piece)[:5, 0]
    gain_got = across[0, : 8 * width].reshape(8, 2, piece)[:5, 1]
    gains = gain_mine + gain_got
    total = gains[:4].reshape(4, 1, piece)
    token_sum = 0.5 * gains[4:5]
    ends = (joined[0, 8 * width :] + across[0, 8 * width :]).reshape(2, -1)
    tails = jnp.where(is_first, ends, jnp.flip(ends, axis=0))
    qkv_b = jnp.transpose(tails[:, : 3 * hd].reshape(2, 3, hd), (1, 0, 2))
    qkv_b = lax.dynamic_slice_in_dim(qkv_b, place.c * (hd // n), hd // n, axis=2)[None]
    fc1_b = lax.dynamic_slice_in_dim(tails[:, 3 * hd :].reshape(-1), place.c * (2 * ff // n), 2 * ff // n)[None, None]
    return (
        boundary,
        total[0],
        total[1],
        total[2],
        total[3],
        g_qkv,
        qkv_b,
        g_out,
        token_sum,
        g_up,
        fc1_b,
        g_down,
        token_sum,
    )


def body(*args):
    two = lax.axis_size(CTX) == 4 and lax.axis_size(TENSOR) == 4
    if not two:
        return body_any(*args)
    return body_two(*args)


def solution(mesh):
    in_specs = (
        P(None, CTX, None),
        P(None, CTX, None),
        P(),
        P(SECTION, CTX),
        P(SECTION, CTX),
        P(SECTION, CTX),
        P(SECTION, CTX),
        P(SECTION, CTX, None, TENSOR, None),
        P(SECTION, None, TENSOR, CTX),
        P(SECTION, TENSOR, None, CTX),
        P(SECTION, CTX),
        P(SECTION, CTX, TENSOR),
        P(SECTION, TENSOR, CTX),
        P(SECTION, TENSOR, CTX),
        P(SECTION, CTX),
    )
    out_specs = (
        P(SECTION, None, CTX, TENSOR),
        P(SECTION, CTX),
        P(SECTION, CTX),
        P(SECTION, CTX),
        P(SECTION, CTX),
        P(SECTION, CTX, None, TENSOR, None),
        P(SECTION, None, TENSOR, CTX),
        P(SECTION, TENSOR, None, CTX),
        P(SECTION, CTX),
        P(SECTION, CTX, TENSOR),
        P(SECTION, TENSOR, CTX),
        P(SECTION, TENSOR, CTX),
        P(SECTION, CTX),
    )
    return jax.shard_map(body, mesh=mesh, in_specs=in_specs, out_specs=out_specs, check_vma=False)
```

```python
import jax
import jax.numpy as jnp
from jax import lax
from jax.experimental import pallas as pl
from jax.experimental.pallas import tpu as pltpu
from jax.sharding import PartitionSpec as P


ROT = 64
EPS = 1e-05
MASKED_SCORE = -1e30
BF = jnp.bfloat16
F32 = jnp.float32

CTX, TENSOR, SECTION = "ctx", "tensor", "section"


def dot(a, b, dims=((1,), (0,))):
    return lax.dot_general(a, b, (dims, ((), ())), preferred_element_type=F32)


def swap(v, axis, distance):
    size = lax.axis_size(axis)
    return lax.ppermute(v, axis, [(i, i ^ distance) for i in range(size)])


def rotary_tables(positions):
    inverse = 10000.0 ** (-(jnp.arange(ROT // 2, dtype=F32) * 2.0 / ROT))
    angles = positions.astype(F32)[:, None] * inverse[None, :]
    angles = jnp.concatenate([angles, angles], axis=-1)
    return (jnp.cos(angles), jnp.sin(angles))


def rotate(z, cosine, sine):
    half = ROT // 2
    lead = z[:, :ROT]
    turned = jnp.concatenate([-lead[:, half:], lead[:, :half]], axis=-1)
    return jnp.concatenate([lead * cosine + turned * sine, z[:, ROT:]], axis=-1)


def unrotate(g, cosine, sine):
    half = ROT // 2
    lead = g[:, :ROT]
    scaled = lead * sine
    turned = jnp.concatenate([scaled[:, half:], -scaled[:, :half]], axis=-1)
    return jnp.concatenate([lead * cosine + turned, g[:, ROT:]], axis=-1)


class Place:
    def __init__(self):
        self.k = lax.axis_index(SECTION)
        self.c = lax.axis_index(CTX)
        self.t = lax.axis_index(TENSOR)
        self.n = lax.axis_size(CTX)
        self.nt = lax.axis_size(TENSOR)
        self.m = self.n // 2
        self.bits = self.m.bit_length() - 1
        self.y = self.c // self.m
        self.cl = self.c % self.m

    def over_k(self, v):
        return swap(v, SECTION, 1)

    def over_y(self, v):
        return swap(v, CTX, self.m)

    def over_x(self, v, bit):
        return swap(v, CTX, 1 << bit)

    def over_z(self, v, distance):
        return swap(v, TENSOR, distance)

    def reduce_rows(self, v):
        cur = v
        for bit in reversed(range(self.bits)):
            half = cur.shape[0] // 2
            got = self.over_x(cur[half:].astype(BF), bit)
            cur = cur[:half].astype(F32) + got.astype(F32)
        return cur[0].astype(F32)

    def sum_rows(self, v):
        cur = v
        for bit in range(self.bits):
            got = self.over_x(cur.astype(BF), bit)
            shape = got.shape
            got = got.reshape(shape[0] >> (bit + 1), 2, 1 << bit, *shape[1:])
            got = jnp.concatenate([got[:, 1:], got[:, :1]], axis=1).reshape(shape)
            cur = cur.astype(F32) + got.astype(F32)
        return cur

    def gather_rows(self, v):
        cur = v[None]
        for bit in range(self.bits):
            cur = jnp.concatenate([cur, self.over_x(cur, bit)], axis=0)
        return cur.reshape(-1, v.shape[-1])

    def reduce_tensor(self, v):
        got = self.over_k(v[:, :, 1])
        cur = v[:, :, 0].astype(F32) + got.astype(F32)
        sent = cur.astype(BF)
        total = cur[:, 0]
        for s in range(1, self.nt):
            total = total + self.over_z(sent[:, s], s).astype(F32)
        return total

    def gather_tensor(self, v):
        parts = [v] + [self.over_z(v, s) for s in range(1, self.nt)]
        mine = jnp.stack(parts, axis=1)
        other = self.over_k(mine)
        return jnp.stack([mine, other], axis=2).reshape(-1, v.shape[-1])


def merge_stats(place, mean, spread, count):
    for bit in range(place.bits):
        got = place.over_x(jnp.stack([mean, spread]), bit)
        shape = mean.shape
        if mean.ndim == 2:
            pairs = got.reshape(2, shape[0] >> (bit + 1), 2, 1 << bit, shape[1])
            pairs = jnp.concatenate([pairs[:, :, 1:], pairs[:, :, :1]], axis=2)
            got = pairs.reshape(2, *shape)
        delta = got[0] - mean
        spread = spread + got[1] + delta * delta * (count * 0.5)
        mean = 0.5 * (mean + got[0])
        count = count * 2
    return mean, spread, count


def norm_stats(place, h):
    rows, width = h.shape
    wide = h.astype(F32)
    mean = jnp.mean(wide, axis=-1)
    centre = wide - mean[:, None]
    spread = jnp.sum(centre * centre, axis=-1)
    shape = (place.m, rows // place.m)
    mean, spread, count = merge_stats(place, mean.reshape(shape), spread.reshape(shape), float(width))
    inv = lax.rsqrt(spread / count + EPS)
    return mean.reshape(rows, 1), inv.reshape(rows, 1)


def layer_forward(place, h, w, small, tables):
    w_qkv, w_out, w_up, w_down = w
    rows = h.shape[0]
    m = place.m
    own = rows // m
    hd = w_out[0].shape[0]
    cosine, sine, pos = tables
    mean, inv = norm_stats(place, h)
    normed = (h.astype(F32) - mean) * inv
    attn_in = (normed * small["g1"] + small["b1"]).astype(BF)
    mlp_in = (normed * small["g2"] + small["b2"]).astype(BF)
    mixed = dot(attn_in, w_qkv).astype(BF).reshape(m, own, 3 * hd)
    hidden = dot(mlp_in, w_up).astype(BF).reshape(m, own, -1)
    kv = place.sum_rows(mixed[..., hd:]).reshape(rows, 2 * hd) + small["qkv_bias"][hd:]
    q = place.reduce_rows(mixed[..., :hd]) + small["qkv_bias"][:hd]
    queries = rotate(q, cosine[:own], sine[:own]).astype(BF)
    keys = rotate(kv[:, :hd], cosine, sine).astype(BF)
    values = kv[:, hd:].astype(BF)
    scores = dot(queries, keys, ((1,), (1,))) * (hd**-0.5)
    allowed = pos[:own, None] >= pos[None, :]
    scores = jnp.where(allowed, scores, MASKED_SCORE)
    top = jnp.max(scores, axis=-1, keepdims=True)
    exps = jnp.where(allowed, jnp.exp(scores - top), 0.0)
    total = jnp.sum(exps, axis=-1, keepdims=True)
    attn_out = (dot(exps.astype(BF), values) / total).astype(BF)
    probs = exps / total
    pre = place.reduce_rows(hidden) + small["fc1_bias"]
    cdf = 0.5 * (1.0 + lax.erf(pre * 0.7071067811865476))
    act = (pre * cdf).astype(BF)
    slope = cdf + pre * jnp.exp(-0.5 * pre * pre) * 0.3989422804014327
    attn_all = place.gather_rows(attn_out)
    act_all = place.gather_rows(act)
    part = jnp.concatenate(
        [dot(attn_all, w_out[j]) + dot(act_all, w_down[j]) for j in range(2)], axis=1
    ).astype(BF)
    branch = place.reduce_tensor(part.reshape(m, place.nt, 2, -1, part.shape[-1]))
    h_own = h.reshape(m, place.nt, 2, -1, h.shape[-1])[:, 0, 0].astype(F32)
    out = h_own + branch + small["out_bias"]
    saved = (h, mean, inv, attn_in, mlp_in, queries, keys, values, probs, attn_out, attn_all, act_all, slope)
    return out, saved


def layer_backward(place, grad, w, small, tables, saved):
    w_qkv, w_out, w_up, w_down = w
    h, mean, inv, attn_in, mlp_in, queries, keys, values, probs, attn_out, attn_all, act_all, slope = saved
    rows = h.shape[0]
    m = place.m
    own = rows // m
    hd = w_out[0].shape[0]
    width = h.shape[1] // 2
    scaling = hd**-0.5
    cosine, sine, _ = tables
    halves = (grad[:, :width], grad[:, width:])
    d_attn = sum(dot(halves[j], w_out[j], ((1,), (1,))) for j in range(2)).astype(BF)
    d_act = sum(dot(halves[j], w_down[j], ((1,), (1,))) for j in range(2)).astype(BF)
    grad_attn = place.reduce_rows(d_attn.reshape(m, own, hd)).astype(BF)
    row_dot = jnp.sum(grad_attn.astype(F32) * attn_out.astype(F32), axis=-1, keepdims=True)
    d_prob = dot(grad_attn, values, ((1,), (1,)))
    d_score = (probs * (d_prob - row_dot)).astype(BF)
    dq = unrotate(dot(d_score, keys) * scaling, cosine[:own], sine[:own]).astype(BF)
    dk = unrotate(dot(d_score, queries, ((0,), (0,))) * scaling, cosine, sine).astype(BF)
    dv = dot(probs.astype(BF), grad_attn, ((0,), (0,))).astype(BF)
    dkv = place.sum_rows(jnp.concatenate([dk, dv], axis=1).reshape(m, own, 2 * hd)).astype(BF)
    d_qkv = jnp.concatenate([place.gather_rows(dq), dkv.reshape(rows, 2 * hd)], axis=1)
    d_pre = (place.reduce_rows(d_act.reshape(m, own, -1)) * slope).astype(BF)
    d_pre_all = place.gather_rows(d_pre)
    d_mlp_in = dot(d_pre_all, w_up, ((1,), (1,)))
    d_attn_in = dot(d_qkv, w_qkv, ((1,), (1,)))
    normed = (h.astype(F32) - mean) * inv
    combined = (d_attn_in * small["g1"] + d_mlp_in * small["g2"]).astype(BF)
    gains = jnp.stack(
        [
            jnp.sum(d_attn_in * normed, axis=0),
            jnp.sum(d_attn_in, axis=0),
            jnp.sum(d_mlp_in * normed, axis=0),
            jnp.sum(d_mlp_in, axis=0),
            jnp.sum(grad.astype(F32), axis=0),
        ]
    )
    biases = jnp.concatenate(
        [jnp.sum(d_qkv.astype(F32), axis=0), jnp.sum(d_pre_all.astype(F32), axis=0)]
    )
    comb = place.reduce_tensor(combined.reshape(m, place.nt, 2, -1, combined.shape[-1]))
    pick = lambda v: v.reshape(m, place.nt, 2, -1, v.shape[-1])[:, 0, 0]
    own_normed = pick(normed)
    sums = jnp.stack([jnp.sum(comb, axis=-1), jnp.sum(comb * own_normed, axis=-1)])
    for bit in range(place.bits):
        got = place.over_x(sums, bit)
        shape = got.shape
        got = got.reshape(2, shape[1] >> (bit + 1), 2, 1 << bit, shape[2])
        got = jnp.concatenate([got[:, :, 1:], got[:, :, :1]], axis=2).reshape(shape)
        sums = sums + got
    sums = sums / (comb.shape[-1] * m)
    grad_in = pick(grad).astype(F32) + pick(inv) * (
        comb - sums[0][..., None] - own_normed * sums[1][..., None]
    )

    def both(make):
        mine, other = make(0), make(1).astype(BF)
        return mine + place.over_y(other).astype(F32)

    cut = lambda v, j: v[:, j * width : (j + 1) * width]
    g_down = both(lambda j: dot(act_all, halves[j], ((0,), (0,))))
    g_out = both(lambda j: dot(attn_all, halves[j], ((0,), (0,))))
    g_up = both(lambda j: dot(cut(mlp_in, j), d_pre_all, ((0,), (0,))))
    g_qkv = both(lambda j: dot(cut(attn_in, j), d_qkv, ((0,), (0,))))
    return grad_in, (g_qkv, g_out, g_up, g_down), gains, biases


def spread_tokens(place, v, index):
    _, tokens, width = v.shape
    n, m = place.n, place.m
    half = tokens // 2
    rows = lax.dynamic_slice_in_dim(v.astype(BF), place.k * half, half, axis=1)
    rows = rows.reshape(2, half, 2, m, width // n)
    rows = jnp.stack([rows[0], jnp.flip(rows[1], axis=1)])
    rows = jnp.transpose(rows, (0, 3, 1, 2, 4)).reshape(n, half, 2 * width // n)
    got = lax.all_to_all(rows, CTX, 0, 0)
    both = jnp.stack([got, place.over_k(got)])
    block = tokens // place.nt
    blocks = both.reshape(-1, block, 2 * width // n)
    return jnp.take(blocks, index, axis=0, mode="clip").reshape(-1, 2 * width // n)


def deliver(place, out, grad_in):
    is_first = place.k == 0
    n, m, nt = place.n, place.m, place.nt
    mine = jnp.where(is_first, grad_in, out).astype(BF)
    other = jnp.where(is_first, out, grad_in).astype(BF)
    got = place.over_k(other)
    low = jnp.where(is_first, mine, got)
    high = jnp.where(is_first, got, mine)
    block = mine.shape[1]
    width = mine.shape[2] // 2
    pieces = jnp.stack([low, high], axis=1).reshape(m, 2 * block, 2, width)
    quarter = m // 2
    t0 = place.t % 2
    rest = place.cl % quarter
    arrived = {}
    for a in range(m):
        dest_cl = (t0 * quarter + rest) ^ a
        rel = dest_cl ^ place.cl
        chosen = lax.dynamic_index_in_dim(pieces, rel, axis=0, keepdims=False)
        for b in range(2):
            pairs = []
            for c in range(n):
                for t in range(nt):
                    y, cl = c // m, c % m
                    s0, s1 = t % 2, t // 2
                    dc = ((s0 * quarter + cl % quarter) ^ a) * 2 + s1
                    dt = (y ^ b) * 2 + cl // quarter
                    pairs.append((c * nt + t, dc * nt + dt))
            arrived[a, b] = lax.ppermute(chosen[:, b], (CTX, TENSOR), pairs)
    own_cl = place.c // 2
    j = place.t // 2
    stacked = jnp.stack([jnp.stack([arrived[a, b] for b in range(2)]) for a in range(m)])
    result = []
    for micro in range(2):
        halves = []
        for s0 in range(2):
            columns = []
            for r in range(quarter):
                a = own_cl ^ (s0 * quarter + r)
                b = j ^ micro
                columns.append(lax.dynamic_slice(stacked, (a, b, 0, 0), (1, 1, 2 * block, width))[0, 0])
            halves.append(jnp.concatenate(columns, axis=1))
        result.append(jnp.concatenate(halves, axis=0))
    return jnp.stack(result)[None].astype(F32)


def body_any(
    x_in,
    cotangent,
    block_pos,
    norm1_gain,
    norm1_bias,
    norm2_gain,
    norm2_bias,
    qkv_weight,
    qkv_bias,
    dense_weight,
    dense_bias,
    fc1_weight,
    fc1_bias,
    fc2_weight,
    fc2_bias,
):
    place = Place()
    k, n, m, nt = place.k, place.n, place.m, place.nt
    is_first = k == 0
    tokens = x_in.shape[1]
    seq = tokens * n
    block = tokens // nt
    piece = fc1_weight.shape[1]
    hd = dense_weight.shape[2]
    ff = fc1_weight.shape[2]

    stacks = (
        jnp.transpose(qkv_weight[0], (2, 0, 1, 3)).reshape(2, piece, 3 * hd),
        dense_weight[0],
        jnp.transpose(fc1_weight[0].reshape(piece, 2, ff // 2), (1, 0, 2)),
        fc2_weight[0].reshape(2, ff // 2, piece),
    )
    keep = [lax.dynamic_index_in_dim(s, k, 0, keepdims=False) for s in stacks]
    send = [lax.dynamic_index_in_dim(s, 1 - k, 0, keepdims=False) for s in stacks]
    got = [place.over_k(s) for s in send]
    layers = []
    for layer in range(2):
        mine = [jnp.where(k == layer, a, b) for a, b in zip(keep, got)]
        theirs = [place.over_y(s) for s in mine]
        layers.append(
            (
                jnp.concatenate([mine[0], theirs[0]], axis=0),
                (mine[1], theirs[1]),
                jnp.concatenate([mine[2], theirs[2]], axis=0),
                (mine[3], theirs[3]),
            )
        )

    vector = jnp.concatenate(
        [
            norm1_gain[0],
            norm1_bias[0],
            norm2_gain[0],
            norm2_bias[0],
            dense_bias[0],
            fc2_bias[0],
            qkv_bias.reshape(-1),
            fc1_bias.reshape(-1),
        ]
    )
    everything = lax.all_gather(vector, (SECTION, CTX), axis=0).reshape(2, n, -1).astype(F32)
    pair = [
        lax.dynamic_index_in_dim(everything, place.c, 1, keepdims=False),
        lax.dynamic_index_in_dim(everything, place.c ^ m, 1, keepdims=False),
    ]
    smalls = []
    for layer in range(2):
        rows = [jnp.concatenate([p[layer, i * piece : (i + 1) * piece] for p in pair]) for i in range(6)]
        rest = everything[layer, :, 6 * piece :]
        size = 6 * (hd // n)
        qkv_b = rest[:, :size].reshape(n, 3, 2, hd // n)
        qkv_b = jnp.transpose(qkv_b, (2, 1, 0, 3)).reshape(2, 3 * hd)
        fc1_b = rest[:, size:].reshape(2, ff // 2)
        smalls.append(
            {
                "g1": rows[0],
                "b1": rows[1],
                "g2": rows[2],
                "b2": rows[3],
                "out_bias": rows[4] + rows[5],
                "qkv_bias": lax.dynamic_index_in_dim(qkv_b, k, 0, keepdims=False),
                "fc1_bias": lax.dynamic_index_in_dim(fc1_b, k, 0, keepdims=False),
            }
        )

    code = (place.cl * nt + place.t) * 2 + k
    count = seq // block
    absolute = jnp.arange(count, dtype=jnp.int32) ^ code
    half_rows = nt // 2
    source = absolute // nt
    part = (absolute // half_rows) % 2
    index = ((part ^ k) * n + source) * half_rows + absolute % half_rows
    slot = (absolute[:, None] * block + jnp.arange(block, dtype=jnp.int32)[None]).reshape(-1)
    per_block = seq // block_pos.shape[1]
    order = lax.dynamic_index_in_dim(block_pos, place.y, 0, keepdims=False)
    hit = (slot // per_block)[:, None] == jnp.arange(block_pos.shape[1], dtype=jnp.int32)[None]
    pos = jnp.sum(jnp.where(hit, order[None], 0), axis=1) * per_block + slot % per_block
    tables = rotary_tables(pos) + (pos,)

    h = spread_tokens(place, x_in, index)
    grad = spread_tokens(place, cotangent, index)
    saved = []
    for layer in range(2):
        out, kept = layer_forward(place, h, layers[layer], smalls[layer], tables)
        saved.append(kept)
        if layer == 0:
            h = place.gather_tensor(out.astype(BF))
    results = [None, None]
    for layer in (1, 0):
        grad_in, weights, gains, biases = layer_backward(
            place, grad, layers[layer], smalls[layer], tables, saved[layer]
        )
        results[layer] = (weights, gains, biases)
        if layer == 1:
            grad = place.gather_tensor(grad_in.astype(BF))

    boundary = deliver(place, out, grad_in)

    finals = []
    for i in range(4):
        first, second = results[0][0][i], results[1][0][i]
        to_second = lax.ppermute(second.astype(BF), SECTION, [(0, 1)])
        to_first = lax.ppermute(first.astype(BF), SECTION, [(1, 0)])
        mine = jnp.where(is_first, first, second)
        other = jnp.where(is_first, to_first, to_second).astype(F32)
        finals.append((jnp.where(is_first, mine, other), jnp.where(is_first, other, mine)))
    g_qkv = jnp.stack([v.reshape(piece, 3, hd) for v in finals[0]], axis=2)[None]
    g_out = jnp.stack(finals[1])[None]
    g_up = jnp.concatenate(finals[2], axis=1)[None]
    g_down = jnp.concatenate(finals[3], axis=0)[None]

    def flat(layer):
        _, gains, biases = results[layer]
        return gains.reshape(5, 2, piece), biases

    packed = [jnp.concatenate([flat(layer)[0][:, 1].reshape(-1), flat(layer)[1]]) for layer in range(2)]
    packed = place.over_y(jnp.stack(packed))
    sums = []
    for layer in range(2):
        gains, biases = flat(layer)
        sums.append(jnp.concatenate([gains[:, 0].reshape(-1), biases]) + packed[layer])
    mine = jnp.where(is_first, sums[0], sums[1])
    other = place.over_k(jnp.where(is_first, sums[1], sums[0]))
    norms = mine[: 4 * piece] + other[: 4 * piece]
    total = norms
    for s in range(1, nt):
        total = total + place.over_z(norms, s)
    total = total.reshape(4, 1, piece)
    token_sum = mine[4 * piece : 5 * piece][None]
    tail_mine, tail_other = mine[5 * piece :], other[5 * piece :]
    low = jnp.where(is_first, tail_mine, tail_other)
    high = jnp.where(is_first, tail_other, tail_mine)
    tails = jnp.stack([low, high])
    qkv_b = jnp.transpose(tails[:, : 3 * hd].reshape(2, 3, hd), (1, 0, 2))
    qkv_b = lax.dynamic_slice_in_dim(qkv_b, place.c * (hd // n), hd // n, axis=2)[None]
    fc1_b = lax.dynamic_slice_in_dim(tails[:, 3 * hd :].reshape(-1), place.c * (ff // n), ff // n)[None, None]
    return (
        boundary,
        total[0],
        total[1],
        total[2],
        total[3],
        g_qkv,
        qkv_b,
        g_out,
        token_sum,
        g_up,
        fc1_b,
        g_down,
        token_sum,
    )


SHIFT = ROT // 2


def run(kernel, outs, args, flops=0, grid=None, in_specs=None, out_specs=None, scratch=(), scalars=0, vmem=None):
    moved = sum(a.size * a.dtype.itemsize for a in args) + sum(
        int(jnp.dtype(o.dtype).itemsize) * o.size for o in outs
    )
    params = {"vmem_limit_bytes": (vmem or 40) << 20}
    extra = {}
    if in_specs is not None:
        extra["in_specs"], extra["out_specs"] = in_specs, out_specs
    spec = pltpu.PrefetchScalarGridSpec(
        num_scalar_prefetch=scalars, grid=grid or (), scratch_shapes=list(scratch), **extra
    ) if (grid or scalars or scratch) else None
    keywords = {"grid_spec": spec} if spec is not None else {}
    return pl.pallas_call(
        kernel,
        out_shape=outs,
        compiler_params=pltpu.CompilerParams(**params),
        cost_estimate=pl.CostEstimate(flops=flops, bytes_accessed=moved, transcendentals=0),
        **keywords,
    )(*args)


def scalar(*values):
    return jnp.stack([v.astype(jnp.int32) for v in values])


def shape(dims, dtype=BF):
    return jax.ShapeDtypeStruct(dims, dtype)


def as_row(*columns):
    rows = columns[0].shape[0]
    lane = lax.broadcasted_iota(jnp.int32, (rows, 128), 1)
    packed = jnp.zeros((rows, 128), F32)
    for i, column in enumerate(columns):
        packed = jnp.where(lane == i, column, packed)
    return packed.T[:8]


def as_columns(rows):
    wide = jnp.concatenate([rows, jnp.zeros((120, rows.shape[1]), F32)], axis=0)
    return wide.T


def row_stats(h_ref, stat_ref):
    wide = h_ref[...].astype(F32)
    mean = jnp.mean(wide, axis=-1, keepdims=True)
    centre = wide - mean
    spread = jnp.sum(centre * centre, axis=-1, keepdims=True)
    stat_ref[...] = as_row(mean, spread)


def assemble_kernel(with_stats, *refs):
    pieces, h_ref = refs[:8], refs[8]
    block = pieces[0].shape[0] // 2
    for s in range(4):
        for u in range(2):
            piece = pieces[s * 2 + u]
            for r in range(2):
                start = r * 8 * block + s * 2 * block + u * block
                h_ref[start : start + block, :] = piece[r * block : (r + 1) * block, :]
    if with_stats:
        row_stats(h_ref, refs[9])


def assemble(pieces, with_stats):
    rows, width = pieces[0].shape
    outs = [shape((8 * rows, width))]
    if with_stats:
        outs.append(shape((8, 8 * rows), F32))

    def kernel(*refs):
        assemble_kernel(with_stats, *refs)

    return run(kernel, outs, pieces)


EXTRA = 16


def pack_tokens(place, v, vectors):
    _, tokens, full = v.shape
    half = tokens // 2
    width = full // 4
    extra = EXTRA if vectors else 0
    count = len(vectors)

    def kernel(at, v_ref, *refs):
        k, c = at[0], at[1]
        lines, outs = refs[:count], refs[count : count + 4]
        rows_ref, line_refs, sem = refs[count + 4], refs[count + 5 : -1], refs[-1]
        rows = pl.ds(pl.multiple_of(k * half, half), half)
        copies = [pltpu.make_async_copy(v_ref.at[:, rows, :], rows_ref, sem.at[0])]
        for i in range(count):
            copies.append(pltpu.make_async_copy(lines[i], line_refs[i], sem.at[i + 1]))
        for copy in copies:
            copy.start()
        for copy in copies:
            copy.wait()
        for d in range(4):
            there = c ^ d
            micro = there // 2
            first = pl.ds(pl.multiple_of(there * width, width), width)
            second = pl.ds(pl.multiple_of((there ^ 2) * width, width), width)
            outs[d][:half, :width] = rows_ref[micro, :, first].astype(BF)
            outs[d][:half, width:] = rows_ref[micro, :, second].astype(BF)
            if extra:
                block = [r[...].astype(F32) for r in line_refs]
                block = jnp.concatenate(block + [jnp.zeros((extra - count, width), F32)], axis=0)
                outs[d][half:, :width] = block.astype(BF)
                outs[d][half:, width:] = jnp.zeros((extra, width), BF)

    return run(
        kernel,
        [shape((half + extra, 2 * width))] * 4,
        [scalar(place.k, place.c), v, *vectors],
        scalars=1,
        in_specs=[pl.BlockSpec(memory_space=pl.ANY)] * (1 + count),
        out_specs=[pl.BlockSpec(memory_space=pltpu.VMEM)] * 4,
        scratch=[pltpu.VMEM((2, half, full), v.dtype)]
        + [pltpu.VMEM(a.shape, a.dtype) for a in vectors]
        + [pltpu.SemaphoreType.DMA((1 + count,))],
        grid=(1,),
        vmem=60,
    )


def send_tokens(place, v, vectors):
    parts = pack_tokens(place, v, vectors)
    got = [parts[0]]
    for d in (1, 2, 3):
        got.append(swap(parts[d], CTX, d))
    out = []
    for g in got:
        out += [g, place.over_k(g)]
    return out


def unpack_tokens(place, pieces, with_stats):
    extra = EXTRA if with_stats else 0
    stride, width = pieces[0].shape
    half = stride - extra
    block = half // 2
    rows = 8 * half
    piece = width // 2

    def kernel(at, *refs):
        got, h_ref, flat, sem = refs[:8], refs[8], refs[-2], refs[-1]
        k, c, t = at[0], at[1], at[2]
        copies = [
            pltpu.make_async_copy(got[i], flat.at[pl.ds(i * stride, stride), :], sem.at[i]) for i in range(8)
        ]
        for copy in copies:
            copy.start()
        for copy in copies:
            copy.wait()
        code = ((c % 2) * 4 + t) * 2 + k
        for j in range(16):
            a = code ^ j
            d = (a // 4) ^ c
            u = ((a // 2) % 2) ^ k
            start = (d * 2 + u) * stride + (a % 2) * block
            h_ref[j * block : (j + 1) * block, :] = flat[pl.ds(pl.multiple_of(start, 16), block), :]
        if with_stats:
            row_stats(h_ref, refs[9])
            for layer in range(2):
                for d in range(4):
                    start = (d * 2 + (k ^ layer)) * stride + half
                    lines = flat[pl.ds(pl.multiple_of(start, 16), extra), :piece].astype(F32)
                    refs[11][layer, d, :, :] = lines
                    if d % 2 == 0:
                        refs[10][layer, :, (d // 2) * piece : (d // 2 + 1) * piece] = lines

    outs = [shape((rows, width))]
    if with_stats:
        outs += [shape((8, rows), F32), shape((2, extra, width), F32), shape((2, 4, extra, piece), F32)]
    return run(
        kernel,
        outs,
        [scalar(place.k, place.c, place.t), *pieces],
        scalars=1,
        in_specs=[pl.BlockSpec(memory_space=pl.ANY)] * 8,
        out_specs=[pl.BlockSpec(memory_space=pltpu.VMEM)] * len(outs),
        scratch=[pltpu.VMEM((8 * stride, width), BF), pltpu.SemaphoreType.DMA((8,))],
        grid=(1,),
        vmem=60,
    )


def norm_inputs(h, stat, stat_x, vec):
    rows, width = h.shape
    own = rows // 2

    def kernel(h_ref, stat_ref, stat_x_ref, vec_ref, attn_ref, mlp_ref, cols_ref):
        there = stat_x_ref[...]
        there = jnp.concatenate([there[:, own:], there[:, :own]], axis=1)
        here = stat_ref[...]
        delta = there[0:1] - here[0:1]
        mean = here[0:1] + 0.5 * delta
        spread = here[1:2] + there[1:2] + delta * delta * (width * 0.5)
        inv = lax.rsqrt(spread / (2 * width) + EPS)
        columns = as_columns(jnp.concatenate([mean, inv, jnp.zeros((6, rows), F32)], axis=0))
        cols_ref[...] = columns
        vec = vec_ref[...]

        @pl.loop(0, rows // 64)
        def _(r):
            part = pl.ds(pl.multiple_of(r * 64, 64), 64)
            normed = (h_ref[part, :].astype(F32) - cols_ref[part, 0:1]) * cols_ref[part, 1:2]
            attn_ref[part, :] = (normed * vec[0:1] + vec[1:2]).astype(BF)
            mlp_ref[part, :] = (normed * vec[2:3] + vec[3:4]).astype(BF)

    return run(
        kernel,
        [shape((rows, width)), shape((rows, width)), shape((rows, 128), F32)],
        [h, stat, stat_x, vec],
    )


def product_qkv(attn_in, w_qkv):
    rows, width = attn_in.shape
    own, piece = rows // 2, width // 2
    hd = w_qkv[0].shape[1] // 3

    def kernel(a_ref, w0, w1, q_ref, send_ref):
        first, second = a_ref[:, :piece], a_ref[:, piece:]
        kv = dot(first, w0[:, hd:]) + dot(second, w1[:, hd:])
        send_ref[:, : 2 * hd] = kv.astype(BF)
        q = dot(first, w0[:, :hd]) + dot(second, w1[:, :hd])
        q_ref[...] = q[:own].astype(BF)
        send_ref[:own, 2 * hd :] = q[own:, :128].astype(BF)
        send_ref[own:, 2 * hd :] = q[own:, 128:].astype(BF)

    return run(
        kernel,
        [shape((own, hd)), shape((rows, 2 * hd + 128))],
        [attn_in, *w_qkv],
        flops=6 * rows * width * hd,
    )


def product_up(mlp_in, w_up):
    rows, width = mlp_in.shape
    own, piece = rows // 2, width // 2
    ff = w_up[0].shape[1]

    def kernel(m_ref, w0, w1, own_ref, send_ref):
        for r, ref in ((slice(own, rows), send_ref), (slice(0, own), own_ref)):
            ref[...] = (dot(m_ref[r, :piece], w0[...]) + dot(m_ref[r, piece:], w1[...])).astype(BF)

    return run(kernel, [shape((own, ff))] * 2, [mlp_in, *w_up], flops=2 * rows * width * ff)


def unfold(ref, hd):
    own = ref.shape[0] // 2
    return jnp.concatenate([ref[:own, 2 * hd :], ref[own:, 2 * hd :]], axis=1)


def turn_in(z, tables, inverse):
    cosine, low, high = tables
    lead = z[:, :128]
    left = pltpu.roll(lead, 128 - SHIFT, axis=1)
    right = pltpu.roll(lead, SHIFT, axis=1)
    mixed = left * low + right * high
    lead = lead * cosine - mixed if inverse else lead * cosine + mixed
    return jnp.concatenate([lead, z[:, 128:]], axis=1)


def attention(q_own, kv_own, kv_got, bias, tables, pos_row):
    rows = kv_own.shape[0]
    own, hd = q_own.shape
    scaling = hd**-0.5

    def kernel(qo, kvo, kvg, b_ref, cos_ref, low_ref, high_ref, pos_ref, q_ref, k_ref, v_ref, p_ref, o_ref):
        b = b_ref[0:1, :]
        tab = (cos_ref[...], low_ref[...], high_ref[...])
        q = qo[...].astype(F32) + unfold(kvg, hd).astype(F32) + b[:, :hd]
        q = turn_in(q, tuple(a[:own] for a in tab), False).astype(BF)
        kv = jnp.concatenate(
            [
                kvo[:own, : 2 * hd].astype(F32) + kvg[own:, : 2 * hd].astype(F32),
                kvo[own:, : 2 * hd].astype(F32) + kvg[:own, : 2 * hd].astype(F32),
            ],
            axis=0,
        ) + b[:, hd:]
        k = turn_in(kv[:, :hd], tab, False).astype(BF)
        v = kv[:, hd:].astype(BF)
        q_ref[...], k_ref[...], v_ref[...] = q, k, v
        pos = pos_ref[...]
        column = as_columns(pos)[:own, 0:1]
        scores = dot(q, k, ((1,), (1,))) * scaling
        allowed = column >= pos[0:1, :]
        scores = jnp.where(allowed, scores, MASKED_SCORE)
        top = jnp.max(scores, axis=-1, keepdims=True)
        exps = jnp.where(allowed, jnp.exp(scores - top), 0.0)
        total = jnp.sum(exps, axis=-1, keepdims=True)
        o_ref[...] = (dot(exps.astype(BF), v) / total).astype(BF)
        p_ref[...] = exps / total

    return run(
        kernel,
        [shape((own, hd)), shape((rows, hd)), shape((rows, hd)), shape((own, rows), F32), shape((own, hd))],
        [q_own, kv_own, kv_got, bias, *tables, pos_row],
        flops=4 * own * rows * hd,
    )


def second_products(acts, attns, w_cat):
    own, ff = acts[0].shape
    hd = attns[0].shape[1]
    piece = w_cat[0].shape[1]
    block = own // 8

    half = piece // 2

    def kernel(a0, a1, t0, t1, w0, w1, keep_ref, send_ref):
        @pl.loop(0, 2)
        def _(c):
            cut = pl.ds(pl.multiple_of(c * half, half), half)
            for r, (a, t) in enumerate(((a0, t0), (a1, t1))):
                for j, w in enumerate((w0, w1)):
                    to = pl.ds(pl.multiple_of(j * piece + c * half, half), half)
                    value = (dot(a[...], w[:ff, cut]) + dot(t[...], w[ff:, cut])).astype(BF)
                    for s in range(4):
                        at = (r * 4 + s) * block
                        keep_ref[at : at + block, to] = value[2 * s * block : (2 * s + 1) * block]
                        send_ref[at : at + block, to] = value[(2 * s + 1) * block : (2 * s + 2) * block]

    return run(
        kernel,
        [shape((own, 2 * piece))] * 2,
        [*acts, *attns, *w_cat],
        flops=8 * own * piece * (ff + hd),
    )


def cut_tensor(keep, got, small, small_got):
    rows, width = keep.shape
    block = rows // 8
    extra = 2 * SMALL if small is not None else 0

    def kernel(keep_ref, got_ref, *refs):
        own_ref, *sends = refs[-4:]
        for r in range(2):
            for s in range(4):
                at = slice((r * 4 + s) * block, (r * 4 + s + 1) * block)
                value = keep_ref[at, :].astype(F32) + got_ref[at, :].astype(F32)
                to = slice(r * block, (r + 1) * block)
                if s == 0:
                    own_ref[to, :] = value
                else:
                    sends[s - 1][to, :] = value.astype(BF)
        if extra:
            both = refs[0][...] + refs[1][...]
            own_ref[2 * block : 2 * block + SMALL, :] = both
            both = jnp.concatenate([both, jnp.zeros_like(both)], axis=0).astype(BF)
            for send in sends:
                send[2 * block :, :] = both

    sent = shape((2 * block + extra, width))
    kept = shape((2 * block + extra // 2, width), F32)
    return run(kernel, [kept, sent, sent, sent], [keep, got] + ([small, small_got] if extra else []))


def sum_tensor(place, keep, send, small):
    got = place.over_k(send)
    small_got = None
    if small is not None:
        small_got = place.over_k(small)
    own, *sends = cut_tensor(keep, got, small, small_got)
    parts = []
    for s, v in enumerate(sends):
        parts.append(place.over_z(v, s + 1))
    return own, parts, small_got


def spread_tensor(place, v):
    got = [v]
    for s in (1, 2, 3):
        got.append(place.over_z(v, s))
    out = []
    for g in got:
        out += [g, place.over_k(g)]
    return out


def own_rows(ref, block):
    half = ref.shape[0] // 2
    return jnp.concatenate([ref[:block, :], ref[half : half + block, :]], axis=0)


def residual(own, parts, h, vec, dtype):
    rows, width = own.shape
    block = rows // 2

    def kernel(own_ref, p1, p2, p3, h_ref, vec_ref, out_ref):
        total = own_ref[...] + p1[...].astype(F32) + p2[...].astype(F32) + p3[...].astype(F32)
        out_ref[...] = (own_rows(h_ref, block).astype(F32) + total + vec_ref[4:5, :] + vec_ref[5:6, :]).astype(dtype)

    return run(kernel, [shape((rows, width), dtype)], [own, *parts, h, vec])[0]


def first_grads(grad, w_cat, hd):
    rows, width = grad.shape
    own, piece = rows // 2, width // 2
    total = w_cat[0].shape[0]
    tiles = total // hd
    last = ((1,), (1,))

    def kernel(g_ref, w0, w1, own_ref, send_ref):
        @pl.loop(0, tiles)
        def _(i):
            lines = pl.ds(pl.multiple_of(lax.rem(i + tiles - 1, tiles) * hd, hd), hd)
            at = pl.ds(pl.multiple_of(i * hd, hd), hd)
            value = dot(g_ref[:, :piece], w0[lines, :], last) + dot(g_ref[:, piece:], w1[lines, :], last)
            own_ref[:, at] = value[:own].astype(BF)
            send_ref[:, at] = value[own:].astype(BF)

    return run(kernel, [shape((own, total))] * 2, [grad, *w_cat], flops=2 * rows * width * total)


def attention_grads(d_own, d_got, attn_out, probs, queries, keys, values, tables):
    own, hd = queries.shape
    rows = keys.shape[0]
    scaling = hd**-0.5

    def kernel(do, dg, o_ref, p_ref, q_ref, k_ref, v_ref, cos_ref, low_ref, high_ref, out_ref):
        grad = (do[...].astype(F32) + dg[...].astype(F32)).astype(BF)
        row_dot = jnp.sum(grad.astype(F32) * o_ref[...].astype(F32), axis=-1, keepdims=True)
        d_prob = dot(grad, v_ref[...], ((1,), (1,)))
        probs = p_ref[...]
        d_score = (probs * (d_prob - row_dot)).astype(BF)
        tab = (cos_ref[...], low_ref[...], high_ref[...])
        dq = dot(d_score, k_ref[...]) * scaling
        dq = turn_in(dq, tuple(a[:own] for a in tab), True).astype(BF)
        out_ref[:own, 2 * hd :] = dq[:, :128]
        out_ref[own:, 2 * hd :] = dq[:, 128:]
        dk = dot(d_score, q_ref[...], ((0,), (0,))) * scaling
        out_ref[:, :hd] = turn_in(dk, tab, True).astype(BF)
        out_ref[:, hd : 2 * hd] = dot(probs.astype(BF), grad, ((0,), (0,))).astype(BF)

    part = pl.BlockSpec((own, hd), lambda i: (0, 0))
    args = [d_own, d_got, attn_out, probs, queries, keys, values, *tables]
    return run(
        kernel,
        [shape((rows, 2 * hd + 128))],
        args,
        flops=8 * own * rows * hd,
        grid=(1,),
        in_specs=[part, part] + [pl.BlockSpec(a.shape, lambda i: (0, 0)) for a in args[2:]],
        out_specs=[pl.BlockSpec((rows, 2 * hd + 128), lambda i: (0, 0))],
    )[0]


SMALL = 8


def second_grads(pres, dkv_own, dkv_got, w_qkv, w_up, h, cols, grad, vec):
    rows, width = h.shape
    own = rows // 2
    piece = width // 2
    block = own // 8
    hd, ff = w_qkv[0].shape[1] // 3, pres[0].shape[1]
    last = ((1,), (1,))

    def kernel(p0, p1, kvo, kvg, wq0, wq1, wu0, wu1, h_ref, c_ref, g_ref, vec_ref, *refs):
        keep_ref, send_ref, gain_ref, dqkv_ref, pre_ref = refs
        fill_qkv(dqkv_ref, kvo, kvg, hd)
        pre_ref[:own, :] = p0[...]
        pre_ref[own:, :] = p1[...]
        gain_ref[...] = jnp.zeros((SMALL, width), F32)

        @pl.loop(0, 2)
        def _(r):
            at = pl.ds(pl.multiple_of(r * own, own), own)
            p, qkv = pre_ref[at, :], dqkv_ref[at, :]
            for j in range(2):
                cut = slice(j * piece, (j + 1) * piece)
                d_mlp = dot(p, (wu0, wu1)[j][...], last)
                d_attn = dot(qkv, (wq0, wq1)[j][...], last)
                normed = (h_ref[at, cut].astype(F32) - c_ref[at, 0:1]) * c_ref[at, 1:2]
                both = (d_attn * vec_ref[0:1, cut] + d_mlp * vec_ref[2:3, cut]).astype(BF)
                for s in range(4):
                    to = pl.ds(pl.multiple_of((r * 4 + s) * block, block), block)
                    keep_ref[to, cut] = both[2 * s * block : (2 * s + 1) * block]
                    send_ref[to, cut] = both[(2 * s + 1) * block : (2 * s + 2) * block]
                add = (d_attn * normed, d_attn, d_mlp * normed, d_mlp, g_ref[at, cut].astype(F32))
                for i, v in enumerate(add):
                    gain_ref[i : i + 1, cut] += jnp.sum(v, axis=0, keepdims=True)

        bq = jnp.sum(dqkv_ref[...].astype(F32), axis=0, keepdims=True)
        bf = jnp.sum(p0[...].astype(F32), axis=0, keepdims=True) + jnp.sum(p1[...].astype(F32), axis=0, keepdims=True)
        gain_ref[5:6, :ff] = bf
        gain_ref[6:7, : 3 * hd] = bq

    return run(
        kernel,
        [
            shape((own, width)),
            shape((own, width)),
            shape((SMALL, width), F32),
        ],
        [*pres, dkv_own, dkv_got, *w_qkv, *w_up, h, cols, grad, vec],
        flops=2 * rows * width * (3 * hd + ff),
        scratch=[pltpu.VMEM((rows, 3 * hd), BF), pltpu.VMEM((rows, ff), BF)],
    )


def own_stats(own, parts, small, small_got, h, cols):
    rows, width = own.shape
    rows -= SMALL
    block = rows // 2

    def kernel(own_ref, p1, p2, p3, s_ref, sg_ref, h_ref, c_ref, comb_ref, sums_ref, small_ref):
        comb = own_ref[:rows, :] + p1[:rows, :].astype(F32) + p2[:rows, :].astype(F32) + p3[:rows, :].astype(F32)
        comb_ref[...] = comb
        c = own_rows(c_ref, block)
        normed = (own_rows(h_ref, block).astype(F32) - c[:, 0:1]) * c[:, 1:2]
        lane = lax.broadcasted_iota(jnp.int32, (rows, 128), 1)
        first = jnp.sum(comb, axis=-1, keepdims=True)
        second = jnp.sum(comb * normed, axis=-1, keepdims=True)
        sums_ref[...] = jnp.where(lane == 0, first, second)
        total = own_ref[rows:, :]
        for p in (p1, p2, p3):
            total = total + p[rows:, :].astype(F32)[:SMALL]
        line = lax.broadcasted_iota(jnp.int32, (SMALL, width), 0)
        small_ref[:SMALL, :] = jnp.where(line < 4, total, s_ref[...])
        small_ref[SMALL:, :] = sg_ref[...]

    return run(
        kernel,
        [shape((rows, width), F32), shape((rows, 128), F32), shape((2 * SMALL, width), F32)],
        [own, *parts, small, small_got, h, cols],
    )


def input_grad(comb, sums, got, h, cols, grad):
    rows, width = comb.shape
    block = rows // 2

    def kernel(comb_ref, s_ref, g_ref, h_ref, c_ref, grad_ref, out_ref):
        c = own_rows(c_ref, block)
        normed = (own_rows(h_ref, block).astype(F32) - c[:, 0:1]) * c[:, 1:2]
        there = g_ref[...]
        total = (s_ref[...] + jnp.concatenate([there[block:], there[:block]], axis=0)) / (2 * width)
        change = comb_ref[...] - total[:, 0:1] - normed * total[:, 1:2]
        out_ref[...] = (own_rows(grad_ref, block).astype(F32) + c[:, 1:2] * change).astype(BF)

    return run(kernel, [shape((rows, width))], [comb, sums, got, h, cols, grad])[0]


def grads_cat(acts, attns, grad):
    own, ff = acts[0].shape
    hd = attns[0].shape[1]
    width = grad.shape[1]
    piece = width // 2
    first = ((0,), (0,))

    def kernel(a0, a1, t0, t1, g_ref, own_ref, send_ref):
        def emit(lines, left, right):
            value = dot(left, g_ref[:own, :], first) + dot(right, g_ref[own:, :], first)
            own_ref[lines, :] = value[:, :piece].astype(BF)
            send_ref[lines, :] = value[:, piece:].astype(BF)

        @pl.loop(0, ff // hd)
        def _(i):
            lines = pl.ds(pl.multiple_of(i * hd, hd), hd)
            emit(lines, a0[:, lines], a1[:, lines])

        emit(pl.ds(ff, hd), t0[...], t1[...])

    return run(
        kernel,
        [shape((ff + hd, piece))] * 2,
        [*acts, *attns, grad],
        flops=4 * own * width * (ff + hd),
    )


def grads_up(mlp_in, pres):
    rows, width = mlp_in.shape
    own, piece = rows // 2, width // 2
    ff = pres[0].shape[1]
    tile = 256
    first = ((0,), (0,))

    def kernel(m_ref, p0, p1, own_ref, send_ref):
        def product(start):
            cut = pl.ds(pl.multiple_of(start, tile), tile)
            return (dot(m_ref[:own, cut], p0[...], first) + dot(m_ref[own:, cut], p1[...], first)).astype(BF)

        @pl.loop(0, 2 * piece // tile)
        def _(i):
            value = product(i * tile)

            @pl.when(i < piece // tile)
            def _():
                own_ref[pl.ds(pl.multiple_of(i * tile, tile), tile), :] = value

            @pl.when(i >= piece // tile)
            def _():
                send_ref[pl.ds(pl.multiple_of(i * tile - piece, tile), tile), :] = value

    return run(kernel, [shape((piece, ff))] * 2, [mlp_in, *pres], flops=2 * rows * width * ff)


def fill_qkv(out_ref, own_ref, got_ref, hd):
    half = out_ref.shape[0] // 2
    for r in range(2):
        at = slice(r * half, (r + 1) * half)
        cross = slice((1 - r) * half, (2 - r) * half)
        out_ref[at, :hd] = unfold((own_ref, got_ref)[r], hd)
        both = own_ref[at, : 2 * hd].astype(F32) + got_ref[cross, : 2 * hd].astype(F32)
        out_ref[at, hd:] = both.astype(BF)


def grads_qkv(attn_in, dkvq_own, dkvq_got, hd):
    rows, width = attn_in.shape
    piece = width // 2

    def kernel(a_ref, do_ref, dg_ref, own_ref, send_ref, full):
        fill_qkv(full, do_ref, dg_ref, hd)
        for j, ref in ((1, send_ref), (0, own_ref)):
            value = dot(a_ref[:, j * piece : (j + 1) * piece], full[...], ((0,), (0,)))
            ref[...] = value.astype(BF)

    return run(
        kernel,
        [shape((piece, 3 * hd))] * 2,
        [attn_in, dkvq_own, dkvq_got],
        flops=6 * rows * width * hd,
        scratch=[pltpu.VMEM((rows, 3 * hd), BF)],
    )


def move(place, outs, arrays, plan, parts):
    count = len(arrays)

    def kernel(at, *refs):
        ins, results = refs[:count], refs[count : count + len(outs)]
        buffers, into, outof = refs[count + len(outs) : -2], refs[-2], refs[-1]
        steps = plan(at[0], ins, results)
        for i, (choices, target) in enumerate(steps):
            for condition, source in choices:
                @pl.when(condition)
                def _():
                    pltpu.make_async_copy(source, buffers[i], into.at[i]).start()

        for i, (choices, target) in enumerate(steps):
            pltpu.make_async_copy(choices[0][1], buffers[i], into.at[i]).wait()
            pltpu.make_async_copy(buffers[i], target, outof.at[i]).start()
        for i, (choices, target) in enumerate(steps):
            pltpu.make_async_copy(buffers[i], target, outof.at[i]).wait()

    anywhere = pl.BlockSpec(memory_space=pl.ANY)
    return run(
        kernel,
        outs,
        [scalar(place.k), *arrays],
        scalars=1,
        in_specs=[anywhere] * count,
        out_specs=[anywhere] * len(outs),
        scratch=[pltpu.VMEM(p, BF) for p in parts]
        + [pltpu.SemaphoreType.DMA((len(parts),)), pltpu.SemaphoreType.DMA((len(parts),))],
        grid=(1,),
        vmem=60,
    )


def pick_up(place, fc1, got, layer):
    piece, full = fc1.shape
    half, part = full // 2, piece // 4

    def plan(k, refs, outs):
        steps = []
        for i in range(4):
            lines = pl.ds(i * part, part)
            source = lambda ref, j: ref.at[lines, pl.ds(j * half, half)]
            choices = ((k == layer, source(refs[0], layer)), (k != layer, source(refs[1], 1 - layer)))
            steps.append((choices, outs[0].at[lines, :]))
        return steps

    return move(place, [shape((piece, half))], [fc1, got], plan, [(part, half)] * 4)[0]


def pick_qkv(place, keep, got, layer):
    piece, width = keep.shape
    part = piece // 4

    def plan(k, refs, outs):
        steps = []
        for i in range(4):
            lines = pl.ds(i * part, part)
            choices = ((k == layer, refs[0].at[lines, :]), (k != layer, refs[1].at[lines, :]))
            steps.append((choices, outs[0].at[lines, :]))
        return steps

    return move(place, [shape((piece, width))], [keep, got], plan, [(part, width)] * 4)[0]


def pick_cat(place, fc2, dense, down_got, dense_got, layer):
    full, piece = fc2.shape
    ff, hd = full // 2, dense.shape[0] // 2
    tiles = ff // hd

    def plan(k, refs, outs):
        steps = []
        for i in range(tiles + 1):
            mine, other = (refs[0], refs[2]) if i < tiles else (refs[1], refs[3])
            source = lambda ref, j: ref.at[pl.ds(j * ff + i * hd if i < tiles else j * hd, hd), :]
            choices = ((k == layer, source(mine, layer)), (k != layer, source(other, 1 - layer)))
            steps.append((choices, outs[0].at[pl.ds(i * hd, hd), :]))
        return steps

    return move(place, [shape((ff + hd, piece))], [fc2, dense, down_got, dense_got], plan, [(hd, piece)] * (tiles + 1))[0]


def stream(place, arrays, chunk, count, outs, buffers, emit, wanted):
    flat = [a for pair in arrays for a in pair]
    lanes = [pair[0].shape[1] for pair in arrays]
    kinds = [pair[0].dtype for pair in arrays]
    per = max(len(emit_views) for emit_views in [wanted])

    def kernel(at, *refs):
        ins = refs[: len(flat)]
        results = refs[len(flat) : len(flat) + len(outs)]
        rest = refs[len(flat) + len(outs) :]
        held, made, into, outof = rest[: len(arrays)], rest[len(arrays)], rest[-2], rest[-1]
        k = at[0]
        where = [0]
        for pair in arrays:
            where.append(where[-1] + len(pair))

        def fetch(n, i, layer):
            source = ins[where[n] + (layer if len(arrays[n]) == 2 else 0)]
            return pltpu.make_async_copy(source.at[pl.ds(i * chunk, chunk), :], held[n].at[i], into.at[n, i])

        for i in range(count):
            for n, pair in enumerate(arrays):
                if len(pair) == 1:
                    fetch(n, i, 0).start()
                    continue
                for layer in range(2):
                    @pl.when(k == layer)
                    def _():
                        fetch(n, i, layer).start()

        for i in range(count):
            for n in range(len(arrays)):
                fetch(n, i, 0).wait()
            for layer in range(2):
                @pl.when(k == layer)
                def _():
                    emit(layer, i, [h.at[i] for h in held], made.at[i])

            for j, view in enumerate(wanted):
                source, target = view(i, made.at[i], results)
                pltpu.make_async_copy(source, target, outof.at[i, j]).start()
        for i in range(count):
            for j, view in enumerate(wanted):
                source, target = view(i, made.at[i], results)
                pltpu.make_async_copy(source, target, outof.at[i, j]).wait()

    anywhere = pl.BlockSpec(memory_space=pl.ANY)
    return run(
        kernel,
        outs,
        [scalar(place.k), *flat],
        scalars=1,
        grid=(1,),
        in_specs=[anywhere] * len(flat),
        out_specs=[anywhere] * len(outs),
        scratch=[pltpu.VMEM((count, chunk, w), d) for w, d in zip(lanes, kinds)]
        + [pltpu.VMEM((count, *buffers[0]), buffers[1])]
        + [pltpu.SemaphoreType.DMA((len(arrays), count)), pltpu.SemaphoreType.DMA((count, per))],
        vmem=60,
    )


def sum_for_owner(place, ours, theirs):
    rows, width = ours[0].shape
    chunk = 256
    swapped = [ours[::-1], theirs[::-1]]

    def emit(layer, i, refs, buffer):
        buffer[...] = (refs[0][...].astype(F32) + refs[1][...].astype(F32)).astype(BF)

    view = lambda i, buffer, outs: (buffer, outs[0].at[pl.ds(i * chunk, chunk), :])
    return stream(place, swapped, chunk, rows // chunk, [shape((rows, width))], ((chunk, width), BF), emit, [view])[0]


def finish_up(place, ours, theirs, arrived):
    rows, width = arrived.shape
    chunk = rows // 4

    def emit(layer, i, refs, buffer):
        buffer[:, layer * width : (layer + 1) * width] = refs[0][...].astype(F32) + refs[1][...].astype(F32)
        buffer[:, (1 - layer) * width : (2 - layer) * width] = refs[2][...].astype(F32)

    view = lambda i, buffer, outs: (buffer, outs[0].at[pl.ds(i * chunk, chunk), :])
    return stream(
        place,
        [ours, theirs, [arrived]],
        chunk,
        4,
        [shape((rows, 2 * width), F32)],
        ((chunk, 2 * width), F32),
        emit,
        [view],
    )[0]


def finish_cat(place, ours, theirs, arrived, hd):
    rows, width = arrived.shape
    tiles = rows // hd - 1

    def emit(layer, i, refs, buffer):
        buffer[layer, :, :] = refs[0][...].astype(F32) + refs[1][...].astype(F32)
        buffer[1 - layer, :, :] = refs[2][...].astype(F32)

    def view(half):
        def pick(i, buffer, outs):
            lines = pl.ds(i * hd if i < tiles else 0, hd)
            return buffer.at[half], outs[0 if i < tiles else 1].at[half, lines, :]

        return pick

    return stream(
        place,
        [ours, theirs, [arrived]],
        hd,
        tiles + 1,
        [shape((2, tiles * hd, width), F32), shape((2, hd, width), F32)],
        ((2, hd, width), F32),
        emit,
        [view(0), view(1)],
    )


def finish_qkv(place, ours, theirs, arrived):
    rows, width = arrived.shape
    chunk = rows // 4
    lines = 2 * width // 128

    def emit(layer, i, refs, buffer):
        for c in range(width // 128):
            cut = slice(c * 128, (c + 1) * 128)
            mine = refs[0][:, cut].astype(F32) + refs[1][:, cut].astype(F32)
            buffer[pl.ds(2 * c + layer, chunk, stride=lines), :] = mine
            buffer[pl.ds(2 * c + 1 - layer, chunk, stride=lines), :] = refs[2][:, cut].astype(F32)

    view = lambda i, buffer, outs: (buffer, outs[0].at[pl.ds(i * chunk * lines, chunk * lines), :])
    out = stream(
        place,
        [ours, theirs, [arrived]],
        chunk,
        4,
        [shape((rows * lines, 128), F32)],
        ((chunk * lines, 128), F32),
        emit,
        [view],
    )[0]
    hd = width // 3
    out = out.reshape(rows, 3, hd // 128, 2, 128)
    return jnp.transpose(out, (0, 1, 3, 2, 4)).reshape(1, rows, 3, 2, hd)


def deliver_two(place, out, out_got, grad_in, grad_got):
    rows, width = out.shape
    block, half = rows // 2, width // 2
    n, m, nt = place.n, place.m, place.nt

    def split(at, o_ref, og_ref, g_ref, gg_ref, *sends):
        k, c, t = at[0], at[1], at[2]
        for core, (mine, other) in enumerate(((g_ref, gg_ref), (o_ref, og_ref))):
            @pl.when(k == core)
            def _():
                low, high = (mine, other) if core == 0 else (other, mine)
                for a in range(2):
                    rel = (t % 2) ^ a ^ (c % 2)
                    lines = pl.ds(pl.multiple_of(rel * block, block), block)
                    for b in range(2):
                        cut = slice(b * half, (b + 1) * half)
                        sends[a * 2 + b][:block, :] = low[lines, cut]
                        sends[a * 2 + b][block:, :] = high[lines, cut]

    spot = scalar(place.k, place.c, place.t)
    sends = run(split, [shape((2 * block, half))] * 4, [spot, out, out_got, grad_in, grad_got], scalars=1)
    arrived = []
    for a in range(2):
        for b in range(2):
            pairs = []
            for c in range(n):
                for t in range(nt):
                    y, cl = c // m, c % m
                    pairs.append((c * nt + t, (((t % 2) ^ a) * 2 + t // 2) * nt + (y ^ b) * 2 + cl))
            arrived.append(lax.ppermute(sends[a * 2 + b], (CTX, TENSOR), pairs))

    def join(at, *refs):
        got, out_ref = refs[:4], refs[4]
        c, t = at[1], at[2]
        for a in range(2):
            for b in range(2):
                first, micro = (c // 2) ^ a, (t // 2) ^ b
                lines = pl.ds(pl.multiple_of(first * 2 * block, 2 * block), 2 * block)
                out_ref[micro, lines, :] = got[a * 2 + b][...].astype(F32)

    return run(join, [shape((2, 4 * block, half), F32)], [spot, *arrived], scalars=1)[0][None]


def split_heads(place, qkv_weight):
    piece, _, _, hd = qkv_weight.shape
    lines = qkv_weight.reshape(piece, 3, 2, hd // 128, 128)
    lines = jnp.transpose(lines, (0, 1, 3, 2, 4)).reshape(-1, 128)
    count = 6 * hd // 128

    def kernel(at, in_ref, keep_ref, send_ref, wide):
        wide[...] = in_ref[...].astype(F32)
        for chunk in range(count // 2):
            columns = pl.ds(chunk * 128, 128)
            keep_ref[:, columns] = wide[pl.ds(2 * chunk + at[0], piece, stride=count), :].astype(BF)
            send_ref[:, columns] = wide[pl.ds(2 * chunk + 1 - at[0], piece, stride=count), :].astype(BF)

    return run(
        kernel,
        [shape((piece, 3 * hd))] * 2,
        [scalar(place.k), lines],
        scalars=1,
        scratch=[pltpu.VMEM(lines.shape, F32)],
    )


def body_two(
    x_in,
    cotangent,
    block_pos,
    norm1_gain,
    norm1_bias,
    norm2_gain,
    norm2_bias,
    qkv_weight,
    qkv_bias,
    dense_weight,
    dense_bias,
    fc1_weight,
    fc1_bias,
    fc2_weight,
    fc2_bias,
):
    place = Place()
    k, n, nt = place.k, place.n, place.nt
    is_first = k == 0
    tokens = x_in.shape[1]
    seq = tokens * n
    block = tokens // nt
    piece = fc1_weight.shape[1]
    hd = dense_weight.shape[2]
    ff = fc1_weight.shape[2] // 2

    def x_swap(v):
        return place.over_x(v, 0)

    def y_swap(v):
        return place.over_y(v)

    heads_bias = jnp.pad(qkv_bias.reshape(1, -1), ((0, 0), (0, piece - qkv_bias.size)))
    vectors = [norm1_gain, norm1_bias, norm2_gain, norm2_bias, dense_bias, fc2_bias, fc1_bias[0], heads_bias]
    x_pieces = send_tokens(place, x_in, vectors)

    fc1, fc2 = fc1_weight[0], fc2_weight[0]
    dense = dense_weight.reshape(2 * hd, piece)

    def k_swap(v):
        return place.over_k(v)

    up_got = k_swap(fc1)
    head_keep, head_send = split_heads(place, qkv_weight[0])
    head_got = k_swap(head_send)
    down_got, dense_got = k_swap(fc2), k_swap(dense)
    layers = []
    for layer in range(2):
        mine_q = pick_qkv(place, head_keep, head_got, layer)
        mine_u = pick_up(place, fc1, up_got, layer)
        mine_c = pick_cat(place, fc2, dense, down_got, dense_got, layer)
        layers.append(((mine_q, y_swap(mine_q)), (mine_u, y_swap(mine_u)), (mine_c, y_swap(mine_c))))

    code = (place.cl * nt + place.t) * 2 + k
    absolute = jnp.arange(seq // block, dtype=jnp.int32) ^ code
    slot = (absolute[:, None] * block + jnp.arange(block, dtype=jnp.int32)[None]).reshape(-1)
    per_block = seq // block_pos.shape[1]
    order = jnp.where(place.y == 0, block_pos[0], block_pos[1])
    hit = (slot // per_block)[:, None] == jnp.arange(block_pos.shape[1], dtype=jnp.int32)[None]
    pos = jnp.sum(jnp.where(hit, order[None], 0), axis=1) * per_block + slot % per_block
    pos_row = jnp.broadcast_to(pos.astype(F32)[None], (8, seq))
    cosine, sine = rotary_tables(pos)
    blank = jnp.zeros((seq, 128 - ROT), F32)
    empty = jnp.zeros((seq, SHIFT), F32)
    tables = (
        jnp.concatenate([cosine, blank + 1.0], axis=1),
        jnp.concatenate([-sine[:, :SHIFT], empty, blank], axis=1),
        jnp.concatenate([empty, sine[:, SHIFT:], blank], axis=1),
    )

    h, stat, vecs, lines = unpack_tokens(place, x_pieces, True)
    by_place = jnp.take(lines[:, :, 6:8], jnp.arange(n, dtype=jnp.int32) ^ place.c, axis=1, mode="clip")
    qkv_biases, fc1_biases = [], []
    for layer in range(2):
        fc1_b = by_place[layer, :, 0].reshape(2, ff)
        qkv_b = by_place[layer, :, 1, : qkv_bias.size].reshape(n, 3, 2, hd // n)
        qkv_b = jnp.where(is_first, qkv_b[:, :, 0], qkv_b[:, :, 1])
        qkv_b = jnp.transpose(qkv_b, (1, 0, 2)).reshape(1, 3 * hd)
        qkv_biases.append(jnp.broadcast_to(qkv_b, (8, 3 * hd)))
        fc1_biases.append(jnp.where(is_first, fc1_b[0], fc1_b[1]))

    cot_pieces = send_tokens(place, cotangent, [])
    saved = []
    for layer in range(2):
        w_qkv, w_up, w_cat = layers[layer]
        stat_x = x_swap(stat)
        attn_in, mlp_in, cols = norm_inputs(h, stat, stat_x, vecs[layer])
        q_own, kvq = product_qkv(attn_in, w_qkv)
        f_own, f_send = product_up(mlp_in, w_up)
        kvq_got, f_got = x_swap(kvq), x_swap(f_send)
        queries, keys, values, probs, attn_out = attention(
            q_own, kvq, kvq_got, qkv_biases[layer], tables, pos_row
        )
        pre = f_own.astype(F32) + f_got.astype(F32) + fc1_biases[layer]
        cdf = 0.5 * (1.0 + lax.erf(pre * 0.7071067811865476))
        act = (pre * cdf).astype(BF)
        slope = cdf + pre * jnp.exp(-0.5 * pre * pre) * 0.3989422804014327
        acts = (act, x_swap(act))
        attns = (attn_out, x_swap(attn_out))
        keep, send = second_products(acts, attns, w_cat)
        own, parts, _ = sum_tensor(place, keep, send, None)
        out = residual(own, parts, h, vecs[layer], BF)
        saved.append((h, cols, attn_in, mlp_in, queries, keys, values, probs, attn_out, attns, acts, slope))
        if layer == 0:
            pieces = spread_tensor(place, out)
            h, stat = assemble(pieces, True)
    grad = unpack_tokens(place, cot_pieces, False)[0]

    results = [None, None]
    for layer in (1, 0):
        w_qkv, w_up, w_cat = layers[layer]
        h, cols, attn_in, mlp_in, queries, keys, values, probs, attn_out, attns, acts, slope = saved[layer]
        ta_own, ta_send = first_grads(grad, w_cat, hd)
        ta_got = x_swap(ta_send)
        dkvq = attention_grads(ta_own, ta_got, attn_out, probs, queries, keys, values, tables)
        dkvq_got = x_swap(dkvq)
        d_pre = ((ta_own[:, hd:].astype(F32) + ta_got[:, hd:].astype(F32)) * slope).astype(BF)
        pres = (d_pre, x_swap(d_pre))
        keep, send, small = second_grads(
            pres, dkvq, dkvq_got, w_qkv, w_up, h, cols, grad, vecs[layer]
        )
        own, parts, small_got = sum_tensor(place, keep, send, small)
        comb, sums, small = own_stats(own, parts, small, small_got, h, cols)
        sums_got = x_swap(sums)
        grad_in = input_grad(comb, sums, sums_got, h, cols, grad)
        cat_own, cat_out = grads_cat(acts, attns, grad)
        up_own, up_out = grads_up(mlp_in, pres)
        qkv_own, qkv_out = grads_qkv(attn_in, dkvq, dkvq_got, hd)
        results[layer] = ((cat_own, y_swap(cat_out)), (up_own, y_swap(up_out)), (qkv_own, y_swap(qkv_out)), small)
        if layer == 1:
            pieces = spread_tensor(place, grad_in)
            grad = assemble(pieces, False)[0]

    boundary = deliver_two(place, out, k_swap(out), grad_in, k_swap(grad_in))

    def to_owner(which):
        ours = [results[layer][which][0] for layer in range(2)]
        theirs = [results[layer][which][1] for layer in range(2)]
        sent = sum_for_owner(place, ours, theirs)
        return ours, theirs, k_swap(sent)

    cat, up, heads = to_owner(0), to_owner(1), to_owner(2)
    g_down, g_out = finish_cat(place, *cat, hd)
    g_down, g_out = g_down.reshape(1, 2 * ff, piece), g_out[None]
    g_up = finish_up(place, *up)[None]
    g_qkv = finish_qkv(place, *heads)

    ours = jnp.where(is_first, results[0][3], results[1][3])
    across = y_swap(ours)
    gains = ours[:5, :piece] + across[:5, piece:]
    total = gains[:4].reshape(4, 1, piece)
    token_sum = gains[4:5]
    mine, other = ours[5:7] + across[5:7], ours[13:15] + across[13:15]
    low, high = jnp.where(is_first, mine, other), jnp.where(is_first, other, mine)
    tails = jnp.stack([low, high])
    qkv_b = tails[:, 1, : 3 * hd].reshape(2, 3, hd)
    qkv_b = jnp.transpose(lax.dynamic_slice_in_dim(qkv_b, place.c * (hd // n), hd // n, axis=2), (1, 0, 2))[None]
    fc1_b = lax.dynamic_slice_in_dim(tails[:, 0].reshape(-1), place.c * (2 * ff // n), 2 * ff // n)[None, None]
    return (
        boundary,
        total[0],
        total[1],
        total[2],
        total[3],
        g_qkv,
        qkv_b,
        g_out,
        token_sum,
        g_up,
        fc1_b,
        g_down,
        token_sum,
    )


def body(*args):
    two = lax.axis_size(CTX) == 4 and lax.axis_size(TENSOR) == 4
    if not two:
        return body_any(*args)
    return body_two(*args)


def solution(mesh):
    in_specs = (
        P(None, CTX, None),
        P(None, CTX, None),
        P(),
        P(SECTION, CTX),
        P(SECTION, CTX),
        P(SECTION, CTX),
        P(SECTION, CTX),
        P(SECTION, CTX, None, TENSOR, None),
        P(SECTION, None, TENSOR, CTX),
        P(SECTION, TENSOR, None, CTX),
        P(SECTION, CTX),
        P(SECTION, CTX, TENSOR),
        P(SECTION, TENSOR, CTX),
        P(SECTION, TENSOR, CTX),
        P(SECTION, CTX),
    )
    out_specs = (
        P(SECTION, None, CTX, TENSOR),
        P(SECTION, CTX),
        P(SECTION, CTX),
        P(SECTION, CTX),
        P(SECTION, CTX),
        P(SECTION, CTX, None, TENSOR, None),
        P(SECTION, None, TENSOR, CTX),
        P(SECTION, TENSOR, None, CTX),
        P(SECTION, CTX),
        P(SECTION, CTX, TENSOR),
        P(SECTION, TENSOR, CTX),
        P(SECTION, TENSOR, CTX),
        P(SECTION, CTX),
    )
    return jax.shard_map(body, mesh=mesh, in_specs=in_specs, out_specs=out_specs, check_vma=False)
```

```python
import jax
import jax.numpy as jnp
from jax import lax
from jax.experimental import pallas as pl
from jax.experimental.pallas import tpu as pltpu
from jax.sharding import PartitionSpec as P


ROT = 64
EPS = 1e-05
MASKED_SCORE = -1e30
BF = jnp.bfloat16
F32 = jnp.float32

CTX, TENSOR, SECTION = "ctx", "tensor", "section"


def dot(a, b, dims=((1,), (0,))):
    return lax.dot_general(a, b, (dims, ((), ())), preferred_element_type=F32)


def swap(v, axis, distance):
    size = lax.axis_size(axis)
    return lax.ppermute(v, axis, [(i, i ^ distance) for i in range(size)])


def rotary_tables(positions):
    inverse = 10000.0 ** (-(jnp.arange(ROT // 2, dtype=F32) * 2.0 / ROT))
    angles = positions.astype(F32)[:, None] * inverse[None, :]
    angles = jnp.concatenate([angles, angles], axis=-1)
    return (jnp.cos(angles), jnp.sin(angles))


def rotate(z, cosine, sine):
    half = ROT // 2
    lead = z[:, :ROT]
    turned = jnp.concatenate([-lead[:, half:], lead[:, :half]], axis=-1)
    return jnp.concatenate([lead * cosine + turned * sine, z[:, ROT:]], axis=-1)


def unrotate(g, cosine, sine):
    half = ROT // 2
    lead = g[:, :ROT]
    scaled = lead * sine
    turned = jnp.concatenate([scaled[:, half:], -scaled[:, :half]], axis=-1)
    return jnp.concatenate([lead * cosine + turned, g[:, ROT:]], axis=-1)


class Place:
    def __init__(self):
        self.k = lax.axis_index(SECTION)
        self.c = lax.axis_index(CTX)
        self.t = lax.axis_index(TENSOR)
        self.n = lax.axis_size(CTX)
        self.nt = lax.axis_size(TENSOR)
        self.m = self.n // 2
        self.bits = self.m.bit_length() - 1
        self.y = self.c // self.m
        self.cl = self.c % self.m

    def over_k(self, v):
        return swap(v, SECTION, 1)

    def over_y(self, v):
        return swap(v, CTX, self.m)

    def over_x(self, v, bit):
        return swap(v, CTX, 1 << bit)

    def over_z(self, v, distance):
        return swap(v, TENSOR, distance)

    def reduce_rows(self, v):
        cur = v
        for bit in reversed(range(self.bits)):
            half = cur.shape[0] // 2
            got = self.over_x(cur[half:].astype(BF), bit)
            cur = cur[:half].astype(F32) + got.astype(F32)
        return cur[0].astype(F32)

    def sum_rows(self, v):
        cur = v
        for bit in range(self.bits):
            got = self.over_x(cur.astype(BF), bit)
            shape = got.shape
            got = got.reshape(shape[0] >> (bit + 1), 2, 1 << bit, *shape[1:])
            got = jnp.concatenate([got[:, 1:], got[:, :1]], axis=1).reshape(shape)
            cur = cur.astype(F32) + got.astype(F32)
        return cur

    def gather_rows(self, v):
        cur = v[None]
        for bit in range(self.bits):
            cur = jnp.concatenate([cur, self.over_x(cur, bit)], axis=0)
        return cur.reshape(-1, v.shape[-1])

    def reduce_tensor(self, v):
        got = self.over_k(v[:, :, 1])
        cur = v[:, :, 0].astype(F32) + got.astype(F32)
        sent = cur.astype(BF)
        total = cur[:, 0]
        for s in range(1, self.nt):
            total = total + self.over_z(sent[:, s], s).astype(F32)
        return total

    def gather_tensor(self, v):
        parts = [v] + [self.over_z(v, s) for s in range(1, self.nt)]
        mine = jnp.stack(parts, axis=1)
        other = self.over_k(mine)
        return jnp.stack([mine, other], axis=2).reshape(-1, v.shape[-1])


def merge_stats(place, mean, spread, count):
    for bit in range(place.bits):
        got = place.over_x(jnp.stack([mean, spread]), bit)
        shape = mean.shape
        if mean.ndim == 2:
            pairs = got.reshape(2, shape[0] >> (bit + 1), 2, 1 << bit, shape[1])
            pairs = jnp.concatenate([pairs[:, :, 1:], pairs[:, :, :1]], axis=2)
            got = pairs.reshape(2, *shape)
        delta = got[0] - mean
        spread = spread + got[1] + delta * delta * (count * 0.5)
        mean = 0.5 * (mean + got[0])
        count = count * 2
    return mean, spread, count


def norm_stats(place, h):
    rows, width = h.shape
    wide = h.astype(F32)
    mean = jnp.mean(wide, axis=-1)
    centre = wide - mean[:, None]
    spread = jnp.sum(centre * centre, axis=-1)
    shape = (place.m, rows // place.m)
    mean, spread, count = merge_stats(place, mean.reshape(shape), spread.reshape(shape), float(width))
    inv = lax.rsqrt(spread / count + EPS)
    return mean.reshape(rows, 1), inv.reshape(rows, 1)


def layer_forward(place, h, w, small, tables):
    w_qkv, w_out, w_up, w_down = w
    rows = h.shape[0]
    m = place.m
    own = rows // m
    hd = w_out[0].shape[0]
    cosine, sine, pos = tables
    mean, inv = norm_stats(place, h)
    normed = (h.astype(F32) - mean) * inv
    attn_in = (normed * small["g1"] + small["b1"]).astype(BF)
    mlp_in = (normed * small["g2"] + small["b2"]).astype(BF)
    mixed = dot(attn_in, w_qkv).astype(BF).reshape(m, own, 3 * hd)
    hidden = dot(mlp_in, w_up).astype(BF).reshape(m, own, -1)
    kv = place.sum_rows(mixed[..., hd:]).reshape(rows, 2 * hd) + small["qkv_bias"][hd:]
    q = place.reduce_rows(mixed[..., :hd]) + small["qkv_bias"][:hd]
    queries = rotate(q, cosine[:own], sine[:own]).astype(BF)
    keys = rotate(kv[:, :hd], cosine, sine).astype(BF)
    values = kv[:, hd:].astype(BF)
    scores = dot(queries, keys, ((1,), (1,))) * (hd**-0.5)
    allowed = pos[:own, None] >= pos[None, :]
    scores = jnp.where(allowed, scores, MASKED_SCORE)
    top = jnp.max(scores, axis=-1, keepdims=True)
    exps = jnp.where(allowed, jnp.exp(scores - top), 0.0)
    total = jnp.sum(exps, axis=-1, keepdims=True)
    attn_out = (dot(exps.astype(BF), values) / total).astype(BF)
    probs = exps / total
    pre = place.reduce_rows(hidden) + small["fc1_bias"]
    cdf = 0.5 * (1.0 + lax.erf(pre * 0.7071067811865476))
    act = (pre * cdf).astype(BF)
    slope = cdf + pre * jnp.exp(-0.5 * pre * pre) * 0.3989422804014327
    attn_all = place.gather_rows(attn_out)
    act_all = place.gather_rows(act)
    part = jnp.concatenate(
        [dot(attn_all, w_out[j]) + dot(act_all, w_down[j]) for j in range(2)], axis=1
    ).astype(BF)
    branch = place.reduce_tensor(part.reshape(m, place.nt, 2, -1, part.shape[-1]))
    h_own = h.reshape(m, place.nt, 2, -1, h.shape[-1])[:, 0, 0].astype(F32)
    out = h_own + branch + small["out_bias"]
    saved = (h, mean, inv, attn_in, mlp_in, queries, keys, values, probs, attn_out, attn_all, act_all, slope)
    return out, saved


def layer_backward(place, grad, w, small, tables, saved):
    w_qkv, w_out, w_up, w_down = w
    h, mean, inv, attn_in, mlp_in, queries, keys, values, probs, attn_out, attn_all, act_all, slope = saved
    rows = h.shape[0]
    m = place.m
    own = rows // m
    hd = w_out[0].shape[0]
    width = h.shape[1] // 2
    scaling = hd**-0.5
    cosine, sine, _ = tables
    halves = (grad[:, :width], grad[:, width:])
    d_attn = sum(dot(halves[j], w_out[j], ((1,), (1,))) for j in range(2)).astype(BF)
    d_act = sum(dot(halves[j], w_down[j], ((1,), (1,))) for j in range(2)).astype(BF)
    grad_attn = place.reduce_rows(d_attn.reshape(m, own, hd)).astype(BF)
    row_dot = jnp.sum(grad_attn.astype(F32) * attn_out.astype(F32), axis=-1, keepdims=True)
    d_prob = dot(grad_attn, values, ((1,), (1,)))
    d_score = (probs * (d_prob - row_dot)).astype(BF)
    dq = unrotate(dot(d_score, keys) * scaling, cosine[:own], sine[:own]).astype(BF)
    dk = unrotate(dot(d_score, queries, ((0,), (0,))) * scaling, cosine, sine).astype(BF)
    dv = dot(probs.astype(BF), grad_attn, ((0,), (0,))).astype(BF)
    dkv = place.sum_rows(jnp.concatenate([dk, dv], axis=1).reshape(m, own, 2 * hd)).astype(BF)
    d_qkv = jnp.concatenate([place.gather_rows(dq), dkv.reshape(rows, 2 * hd)], axis=1)
    d_pre = (place.reduce_rows(d_act.reshape(m, own, -1)) * slope).astype(BF)
    d_pre_all = place.gather_rows(d_pre)
    d_mlp_in = dot(d_pre_all, w_up, ((1,), (1,)))
    d_attn_in = dot(d_qkv, w_qkv, ((1,), (1,)))
    normed = (h.astype(F32) - mean) * inv
    combined = (d_attn_in * small["g1"] + d_mlp_in * small["g2"]).astype(BF)
    gains = jnp.stack(
        [
            jnp.sum(d_attn_in * normed, axis=0),
            jnp.sum(d_attn_in, axis=0),
            jnp.sum(d_mlp_in * normed, axis=0),
            jnp.sum(d_mlp_in, axis=0),
            jnp.sum(grad.astype(F32), axis=0),
        ]
    )
    biases = jnp.concatenate(
        [jnp.sum(d_qkv.astype(F32), axis=0), jnp.sum(d_pre_all.astype(F32), axis=0)]
    )
    comb = place.reduce_tensor(combined.reshape(m, place.nt, 2, -1, combined.shape[-1]))
    pick = lambda v: v.reshape(m, place.nt, 2, -1, v.shape[-1])[:, 0, 0]
    own_normed = pick(normed)
    sums = jnp.stack([jnp.sum(comb, axis=-1), jnp.sum(comb * own_normed, axis=-1)])
    for bit in range(place.bits):
        got = place.over_x(sums, bit)
        shape = got.shape
        got = got.reshape(2, shape[1] >> (bit + 1), 2, 1 << bit, shape[2])
        got = jnp.concatenate([got[:, :, 1:], got[:, :, :1]], axis=2).reshape(shape)
        sums = sums + got
    sums = sums / (comb.shape[-1] * m)
    grad_in = pick(grad).astype(F32) + pick(inv) * (
        comb - sums[0][..., None] - own_normed * sums[1][..., None]
    )

    def both(make):
        mine, other = make(0), make(1).astype(BF)
        return mine + place.over_y(other).astype(F32)

    cut = lambda v, j: v[:, j * width : (j + 1) * width]
    g_down = both(lambda j: dot(act_all, halves[j], ((0,), (0,))))
    g_out = both(lambda j: dot(attn_all, halves[j], ((0,), (0,))))
    g_up = both(lambda j: dot(cut(mlp_in, j), d_pre_all, ((0,), (0,))))
    g_qkv = both(lambda j: dot(cut(attn_in, j), d_qkv, ((0,), (0,))))
    return grad_in, (g_qkv, g_out, g_up, g_down), gains, biases


def spread_tokens(place, v, index):
    _, tokens, width = v.shape
    n, m = place.n, place.m
    half = tokens // 2
    rows = lax.dynamic_slice_in_dim(v.astype(BF), place.k * half, half, axis=1)
    rows = rows.reshape(2, half, 2, m, width // n)
    rows = jnp.stack([rows[0], jnp.flip(rows[1], axis=1)])
    rows = jnp.transpose(rows, (0, 3, 1, 2, 4)).reshape(n, half, 2 * width // n)
    got = lax.all_to_all(rows, CTX, 0, 0)
    both = jnp.stack([got, place.over_k(got)])
    block = tokens // place.nt
    blocks = both.reshape(-1, block, 2 * width // n)
    return jnp.take(blocks, index, axis=0, mode="clip").reshape(-1, 2 * width // n)


def deliver(place, out, grad_in):
    is_first = place.k == 0
    n, m, nt = place.n, place.m, place.nt
    mine = jnp.where(is_first, grad_in, out).astype(BF)
    other = jnp.where(is_first, out, grad_in).astype(BF)
    got = place.over_k(other)
    low = jnp.where(is_first, mine, got)
    high = jnp.where(is_first, got, mine)
    block = mine.shape[1]
    width = mine.shape[2] // 2
    pieces = jnp.stack([low, high], axis=1).reshape(m, 2 * block, 2, width)
    quarter = m // 2
    t0 = place.t % 2
    rest = place.cl % quarter
    arrived = {}
    for a in range(m):
        dest_cl = (t0 * quarter + rest) ^ a
        rel = dest_cl ^ place.cl
        chosen = lax.dynamic_index_in_dim(pieces, rel, axis=0, keepdims=False)
        for b in range(2):
            pairs = []
            for c in range(n):
                for t in range(nt):
                    y, cl = c // m, c % m
                    s0, s1 = t % 2, t // 2
                    dc = ((s0 * quarter + cl % quarter) ^ a) * 2 + s1
                    dt = (y ^ b) * 2 + cl // quarter
                    pairs.append((c * nt + t, dc * nt + dt))
            arrived[a, b] = lax.ppermute(chosen[:, b], (CTX, TENSOR), pairs)
    own_cl = place.c // 2
    j = place.t // 2
    stacked = jnp.stack([jnp.stack([arrived[a, b] for b in range(2)]) for a in range(m)])
    result = []
    for micro in range(2):
        halves = []
        for s0 in range(2):
            columns = []
            for r in range(quarter):
                a = own_cl ^ (s0 * quarter + r)
                b = j ^ micro
                columns.append(lax.dynamic_slice(stacked, (a, b, 0, 0), (1, 1, 2 * block, width))[0, 0])
            halves.append(jnp.concatenate(columns, axis=1))
        result.append(jnp.concatenate(halves, axis=0))
    return jnp.stack(result)[None].astype(F32)


def body_any(
    x_in,
    cotangent,
    block_pos,
    norm1_gain,
    norm1_bias,
    norm2_gain,
    norm2_bias,
    qkv_weight,
    qkv_bias,
    dense_weight,
    dense_bias,
    fc1_weight,
    fc1_bias,
    fc2_weight,
    fc2_bias,
):
    place = Place()
    k, n, m, nt = place.k, place.n, place.m, place.nt
    is_first = k == 0
    tokens = x_in.shape[1]
    seq = tokens * n
    block = tokens // nt
    piece = fc1_weight.shape[1]
    hd = dense_weight.shape[2]
    ff = fc1_weight.shape[2]

    stacks = (
        jnp.transpose(qkv_weight[0], (2, 0, 1, 3)).reshape(2, piece, 3 * hd),
        dense_weight[0],
        jnp.transpose(fc1_weight[0].reshape(piece, 2, ff // 2), (1, 0, 2)),
        fc2_weight[0].reshape(2, ff // 2, piece),
    )
    keep = [lax.dynamic_index_in_dim(s, k, 0, keepdims=False) for s in stacks]
    send = [lax.dynamic_index_in_dim(s, 1 - k, 0, keepdims=False) for s in stacks]
    got = [place.over_k(s) for s in send]
    layers = []
    for layer in range(2):
        mine = [jnp.where(k == layer, a, b) for a, b in zip(keep, got)]
        theirs = [place.over_y(s) for s in mine]
        layers.append(
            (
                jnp.concatenate([mine[0], theirs[0]], axis=0),
                (mine[1], theirs[1]),
                jnp.concatenate([mine[2], theirs[2]], axis=0),
                (mine[3], theirs[3]),
            )
        )

    vector = jnp.concatenate(
        [
            norm1_gain[0],
            norm1_bias[0],
            norm2_gain[0],
            norm2_bias[0],
            dense_bias[0],
            fc2_bias[0],
            qkv_bias.reshape(-1),
            fc1_bias.reshape(-1),
        ]
    )
    everything = lax.all_gather(vector, (SECTION, CTX), axis=0).reshape(2, n, -1).astype(F32)
    pair = [
        lax.dynamic_index_in_dim(everything, place.c, 1, keepdims=False),
        lax.dynamic_index_in_dim(everything, place.c ^ m, 1, keepdims=False),
    ]
    smalls = []
    for layer in range(2):
        rows = [jnp.concatenate([p[layer, i * piece : (i + 1) * piece] for p in pair]) for i in range(6)]
        rest = everything[layer, :, 6 * piece :]
        size = 6 * (hd // n)
        qkv_b = rest[:, :size].reshape(n, 3, 2, hd // n)
        qkv_b = jnp.transpose(qkv_b, (2, 1, 0, 3)).reshape(2, 3 * hd)
        fc1_b = rest[:, size:].reshape(2, ff // 2)
        smalls.append(
            {
                "g1": rows[0],
                "b1": rows[1],
                "g2": rows[2],
                "b2": rows[3],
                "out_bias": rows[4] + rows[5],
                "qkv_bias": lax.dynamic_index_in_dim(qkv_b, k, 0, keepdims=False),
                "fc1_bias": lax.dynamic_index_in_dim(fc1_b, k, 0, keepdims=False),
            }
        )

    code = (place.cl * nt + place.t) * 2 + k
    count = seq // block
    absolute = jnp.arange(count, dtype=jnp.int32) ^ code
    half_rows = nt // 2
    source = absolute // nt
    part = (absolute // half_rows) % 2
    index = ((part ^ k) * n + source) * half_rows + absolute % half_rows
    slot = (absolute[:, None] * block + jnp.arange(block, dtype=jnp.int32)[None]).reshape(-1)
    per_block = seq // block_pos.shape[1]
    order = lax.dynamic_index_in_dim(block_pos, place.y, 0, keepdims=False)
    hit = (slot // per_block)[:, None] == jnp.arange(block_pos.shape[1], dtype=jnp.int32)[None]
    pos = jnp.sum(jnp.where(hit, order[None], 0), axis=1) * per_block + slot % per_block
    tables = rotary_tables(pos) + (pos,)

    h = spread_tokens(place, x_in, index)
    grad = spread_tokens(place, cotangent, index)
    saved = []
    for layer in range(2):
        out, kept = layer_forward(place, h, layers[layer], smalls[layer], tables)
        saved.append(kept)
        if layer == 0:
            h = place.gather_tensor(out.astype(BF))
    results = [None, None]
    for layer in (1, 0):
        grad_in, weights, gains, biases = layer_backward(
            place, grad, layers[layer], smalls[layer], tables, saved[layer]
        )
        results[layer] = (weights, gains, biases)
        if layer == 1:
            grad = place.gather_tensor(grad_in.astype(BF))

    boundary = deliver(place, out, grad_in)

    finals = []
    for i in range(4):
        first, second = results[0][0][i], results[1][0][i]
        to_second = lax.ppermute(second.astype(BF), SECTION, [(0, 1)])
        to_first = lax.ppermute(first.astype(BF), SECTION, [(1, 0)])
        mine = jnp.where(is_first, first, second)
        other = jnp.where(is_first, to_first, to_second).astype(F32)
        finals.append((jnp.where(is_first, mine, other), jnp.where(is_first, other, mine)))
    g_qkv = jnp.stack([v.reshape(piece, 3, hd) for v in finals[0]], axis=2)[None]
    g_out = jnp.stack(finals[1])[None]
    g_up = jnp.concatenate(finals[2], axis=1)[None]
    g_down = jnp.concatenate(finals[3], axis=0)[None]

    def flat(layer):
        _, gains, biases = results[layer]
        return gains.reshape(5, 2, piece), biases

    packed = [jnp.concatenate([flat(layer)[0][:, 1].reshape(-1), flat(layer)[1]]) for layer in range(2)]
    packed = place.over_y(jnp.stack(packed))
    sums = []
    for layer in range(2):
        gains, biases = flat(layer)
        sums.append(jnp.concatenate([gains[:, 0].reshape(-1), biases]) + packed[layer])
    mine = jnp.where(is_first, sums[0], sums[1])
    other = place.over_k(jnp.where(is_first, sums[1], sums[0]))
    norms = mine[: 4 * piece] + other[: 4 * piece]
    total = norms
    for s in range(1, nt):
        total = total + place.over_z(norms, s)
    total = total.reshape(4, 1, piece)
    token_sum = mine[4 * piece : 5 * piece][None]
    tail_mine, tail_other = mine[5 * piece :], other[5 * piece :]
    low = jnp.where(is_first, tail_mine, tail_other)
    high = jnp.where(is_first, tail_other, tail_mine)
    tails = jnp.stack([low, high])
    qkv_b = jnp.transpose(tails[:, : 3 * hd].reshape(2, 3, hd), (1, 0, 2))
    qkv_b = lax.dynamic_slice_in_dim(qkv_b, place.c * (hd // n), hd // n, axis=2)[None]
    fc1_b = lax.dynamic_slice_in_dim(tails[:, 3 * hd :].reshape(-1), place.c * (ff // n), ff // n)[None, None]
    return (
        boundary,
        total[0],
        total[1],
        total[2],
        total[3],
        g_qkv,
        qkv_b,
        g_out,
        token_sum,
        g_up,
        fc1_b,
        g_down,
        token_sum,
    )


SHIFT = ROT // 2


def run(kernel, outs, args, flops=0, grid=None, in_specs=None, out_specs=None, scratch=(), scalars=0, vmem=None):
    moved = sum(a.size * a.dtype.itemsize for a in args) + sum(
        int(jnp.dtype(o.dtype).itemsize) * o.size for o in outs
    )
    params = {"vmem_limit_bytes": (vmem or 40) << 20}
    extra = {}
    if in_specs is not None:
        extra["in_specs"], extra["out_specs"] = in_specs, out_specs
    spec = pltpu.PrefetchScalarGridSpec(
        num_scalar_prefetch=scalars, grid=grid or (), scratch_shapes=list(scratch), **extra
    ) if (grid or scalars or scratch) else None
    keywords = {"grid_spec": spec} if spec is not None else {}
    return pl.pallas_call(
        kernel,
        out_shape=outs,
        compiler_params=pltpu.CompilerParams(**params),
        cost_estimate=pl.CostEstimate(flops=flops, bytes_accessed=moved, transcendentals=0),
        **keywords,
    )(*args)


def scalar(*values):
    return jnp.stack([v.astype(jnp.int32) for v in values])


def shape(dims, dtype=BF):
    return jax.ShapeDtypeStruct(dims, dtype)


def as_columns(rows):
    wide = jnp.concatenate([rows, jnp.zeros((120, rows.shape[1]), F32)], axis=0)
    return wide.T


def row_stats(h_ref, stat_ref, columns):
    @pl.loop(0, h_ref.shape[0] // 64)
    def _(i):
        part = pl.ds(pl.multiple_of(i * 64, 64), 64)
        wide = h_ref[part, :].astype(F32)
        mean = jnp.mean(wide, axis=-1, keepdims=True)
        centre = wide - mean
        spread = jnp.sum(centre * centre, axis=-1, keepdims=True)
        lane = lax.broadcasted_iota(jnp.int32, (64, 128), 1)
        columns[part, :] = jnp.where(lane == 0, mean, spread)

    stat_ref[...] = columns[...].T[:8]


def assemble_kernel(with_stats, *refs):
    pieces, h_ref = refs[:8], refs[8]
    block = pieces[0].shape[0] // 2
    for s in range(4):
        for u in range(2):
            piece = pieces[s * 2 + u]
            for r in range(2):
                start = r * 8 * block + s * 2 * block + u * block
                h_ref[start : start + block, :] = piece[r * block : (r + 1) * block, :]
    if with_stats:
        row_stats(h_ref, refs[9], refs[10])


def assemble(pieces, with_stats):
    rows, width = pieces[0].shape
    outs = [shape((8 * rows, width))]
    if with_stats:
        outs.append(shape((8, 8 * rows), F32))

    def kernel(*refs):
        assemble_kernel(with_stats, *refs)

    return run(kernel, outs, pieces, scratch=[pltpu.VMEM((8 * rows, 128), F32)] if with_stats else ())


EXTRA = 16
ROWS = 32


def pack_tokens(place, v, vectors):
    _, tokens, full = v.shape
    half = tokens // 2
    width = full // 4
    extra = EXTRA if vectors else 0
    count = len(vectors)

    def kernel(at, v_ref, *refs):
        k, c = at[0], at[1]
        lines, outs = refs[:count], refs[count : count + 4]
        rows_ref, line_refs, sem = refs[count + 4], refs[count + 5 : -1], refs[-1]
        rows = pl.ds(pl.multiple_of(k * half, half), half)
        copies = [pltpu.make_async_copy(v_ref.at[:, rows, :], rows_ref, sem.at[0])]
        for i in range(count):
            copies.append(pltpu.make_async_copy(lines[i], line_refs[i], sem.at[i + 1]))
        for copy in copies:
            copy.start()
        for copy in copies:
            copy.wait()
        for d in range(4):
            there = c ^ d
            micro = there // 2
            first = pl.ds(pl.multiple_of(there * width, width), width)
            second = pl.ds(pl.multiple_of((there ^ 2) * width, width), width)
            outs[d][:half, :width] = rows_ref[micro, :, first].astype(BF)
            outs[d][:half, width:] = rows_ref[micro, :, second].astype(BF)
            if extra:
                block = [r[...].astype(F32) for r in line_refs]
                block = jnp.concatenate(block + [jnp.zeros((extra - count, width), F32)], axis=0)
                outs[d][half:, :width] = block.astype(BF)
                outs[d][half:, width:] = jnp.zeros((extra, width), BF)

    return run(
        kernel,
        [shape((half + extra, 2 * width))] * 4,
        [scalar(place.k, place.c), v, *vectors],
        scalars=1,
        in_specs=[pl.BlockSpec(memory_space=pl.ANY)] * (1 + count),
        out_specs=[pl.BlockSpec(memory_space=pltpu.VMEM)] * 4,
        scratch=[pltpu.VMEM((2, half, full), v.dtype)]
        + [pltpu.VMEM(a.shape, a.dtype) for a in vectors]
        + [pltpu.SemaphoreType.DMA((1 + count,))],
        grid=(1,),
        vmem=60,
    )


def send_tokens(place, v, vectors):
    parts = pack_tokens(place, v, vectors)
    got = [parts[0]]
    for d in (1, 2, 3):
        got.append(swap(parts[d], CTX, d))
    out = []
    for g in got:
        out += [g, place.over_k(g)]
    return out


def unpack_tokens(place, pieces, with_stats):
    extra = EXTRA if with_stats else 0
    stride, width = pieces[0].shape
    half = stride - extra
    block = half // 2
    rows = 8 * half
    piece = width // 2

    def kernel(at, *refs):
        got, h_ref, flat, sem = refs[:8], refs[8], refs[-2], refs[-1]
        k, c, t = at[0], at[1], at[2]
        copies = [
            pltpu.make_async_copy(got[i], flat.at[pl.ds(i * stride, stride), :], sem.at[i]) for i in range(8)
        ]
        for copy in copies:
            copy.start()
        for copy in copies:
            copy.wait()
        code = ((c % 2) * 4 + t) * 2 + k
        for j in range(16):
            a = code ^ j
            d = (a // 4) ^ c
            u = ((a // 2) % 2) ^ k
            start = (d * 2 + u) * stride + (a % 2) * block
            h_ref[j * block : (j + 1) * block, :] = flat[pl.ds(pl.multiple_of(start, 16), block), :]
        if with_stats:
            row_stats(h_ref, refs[9], refs[-3])
            for layer in range(2):
                for d in range(4):
                    start = (d * 2 + (k ^ layer)) * stride + half
                    lines = flat[pl.ds(pl.multiple_of(start, 16), extra), :piece].astype(F32)
                    refs[11][layer, d, :, :] = lines
                    if d % 2 == 0:
                        refs[10][layer, :, (d // 2) * piece : (d // 2 + 1) * piece] = lines

    outs = [shape((rows, width))]
    if with_stats:
        outs += [shape((8, rows), F32), shape((2, extra, width), F32), shape((2, 4, extra, piece), F32)]
    return run(
        kernel,
        outs,
        [scalar(place.k, place.c, place.t), *pieces],
        scalars=1,
        in_specs=[pl.BlockSpec(memory_space=pl.ANY)] * 8,
        out_specs=[pl.BlockSpec(memory_space=pltpu.VMEM)] * len(outs),
        scratch=[pltpu.VMEM((rows, 128), F32)] * with_stats
        + [pltpu.VMEM((8 * stride, width), BF), pltpu.SemaphoreType.DMA((8,))],
        grid=(1,),
        vmem=60,
    )


def norm_inputs(h, stat, stat_x, vec):
    rows, width = h.shape
    own = rows // 2

    def kernel(h_ref, stat_ref, stat_x_ref, vec_ref, attn_ref, mlp_ref, cols_ref):
        there = stat_x_ref[...]
        there = jnp.concatenate([there[:, own:], there[:, :own]], axis=1)
        here = stat_ref[...]
        delta = there[0:1] - here[0:1]
        mean = here[0:1] + 0.5 * delta
        spread = here[1:2] + there[1:2] + delta * delta * (width * 0.5)
        inv = lax.rsqrt(spread / (2 * width) + EPS)
        columns = as_columns(jnp.concatenate([mean, inv, jnp.zeros((6, rows), F32)], axis=0))
        cols_ref[...] = columns
        vec = vec_ref[...]

        @pl.loop(0, rows // 64)
        def _(r):
            part = pl.ds(pl.multiple_of(r * 64, 64), 64)
            normed = (h_ref[part, :].astype(F32) - cols_ref[part, 0:1]) * cols_ref[part, 1:2]
            attn_ref[part, :] = (normed * vec[0:1] + vec[1:2]).astype(BF)
            mlp_ref[part, :] = (normed * vec[2:3] + vec[3:4]).astype(BF)

    return run(
        kernel,
        [shape((rows, width)), shape((rows, width)), shape((rows, 128), F32)],
        [h, stat, stat_x, vec],
    )


def product_qkv(attn_in, w_qkv):
    rows, width = attn_in.shape
    own, piece = rows // 2, width // 2
    hd = w_qkv[0].shape[1] // 3

    def kernel(a_ref, w0, w1, q_ref, send_ref):
        first, second = a_ref[:, :piece], a_ref[:, piece:]
        kv = dot(first, w0[:, hd:]) + dot(second, w1[:, hd:])
        send_ref[:, : 2 * hd] = kv.astype(BF)
        q = dot(first, w0[:, :hd]) + dot(second, w1[:, :hd])
        q_ref[...] = q[:own].astype(BF)
        send_ref[:own, 2 * hd :] = q[own:, :128].astype(BF)
        send_ref[own:, 2 * hd :] = q[own:, 128:].astype(BF)

    return run(
        kernel,
        [shape((own, hd)), shape((rows, 2 * hd + 128))],
        [attn_in, *w_qkv],
        flops=6 * rows * width * hd,
    )


def product_up(mlp_in, w_up):
    rows, width = mlp_in.shape
    own, piece = rows // 2, width // 2
    ff = w_up[0].shape[1]

    def kernel(m_ref, w0, w1, own_ref, send_ref):
        for r, ref in ((slice(own, rows), send_ref), (slice(0, own), own_ref)):
            ref[...] = (dot(m_ref[r, :piece], w0[...]) + dot(m_ref[r, piece:], w1[...])).astype(BF)

    return run(kernel, [shape((own, ff))] * 2, [mlp_in, *w_up], flops=2 * rows * width * ff)


def unfold(ref, hd):
    own = ref.shape[0] // 2
    return jnp.concatenate([ref[:own, 2 * hd :], ref[own:, 2 * hd :]], axis=1)


def turn_in(z, tables, inverse):
    cosine, low, high = tables
    lead = z[:, :128]
    left = pltpu.roll(lead, 128 - SHIFT, axis=1)
    right = pltpu.roll(lead, SHIFT, axis=1)
    mixed = left * low + right * high
    lead = lead * cosine - mixed if inverse else lead * cosine + mixed
    return jnp.concatenate([lead, z[:, 128:]], axis=1)


def attention(q_own, kv_own, kv_got, bias, tables, pos_row):
    rows = kv_own.shape[0]
    own, hd = q_own.shape
    scaling = hd**-0.5

    def kernel(qo, kvo, kvg, b_ref, cos_ref, low_ref, high_ref, pos_ref, q_ref, k_ref, v_ref, p_ref, o_ref):
        b = b_ref[0:1, :]
        tab = (cos_ref[...], low_ref[...], high_ref[...])
        q = qo[...].astype(F32) + unfold(kvg, hd).astype(F32) + b[:, :hd]
        q = turn_in(q, tuple(a[:own] for a in tab), False).astype(BF)
        kv = jnp.concatenate(
            [
                kvo[:own, : 2 * hd].astype(F32) + kvg[own:, : 2 * hd].astype(F32),
                kvo[own:, : 2 * hd].astype(F32) + kvg[:own, : 2 * hd].astype(F32),
            ],
            axis=0,
        ) + b[:, hd:]
        k = turn_in(kv[:, :hd], tab, False).astype(BF)
        v = kv[:, hd:].astype(BF)
        q_ref[...], k_ref[...], v_ref[...] = q, k, v
        pos = pos_ref[...]
        column = as_columns(pos)[:own, 0:1]
        scores = dot(q, k, ((1,), (1,))) * scaling
        allowed = column >= pos[0:1, :]
        scores = jnp.where(allowed, scores, MASKED_SCORE)
        top = jnp.max(scores, axis=-1, keepdims=True)
        exps = jnp.where(allowed, jnp.exp(scores - top), 0.0)
        total = jnp.sum(exps, axis=-1, keepdims=True)
        o_ref[...] = (dot(exps.astype(BF), v) / total).astype(BF)
        p_ref[...] = exps / total

    return run(
        kernel,
        [shape((own, hd)), shape((rows, hd)), shape((rows, hd)), shape((own, rows), F32), shape((own, hd))],
        [q_own, kv_own, kv_got, bias, *tables, pos_row],
        flops=4 * own * rows * hd,
    )


def second_products(acts, attns, w_cat):
    own, ff = acts[0].shape
    hd = attns[0].shape[1]
    piece = w_cat[0].shape[1]
    block = own // 8

    half = piece // 2

    def kernel(a0, a1, t0, t1, w0, w1, keep_ref, send_ref):
        @pl.loop(0, 2)
        def _(c):
            cut = pl.ds(pl.multiple_of(c * half, half), half)
            for r, (a, t) in enumerate(((a0, t0), (a1, t1))):
                for j, w in enumerate((w0, w1)):
                    to = pl.ds(pl.multiple_of(j * piece + c * half, half), half)
                    value = (dot(a[...], w[:ff, cut]) + dot(t[...], w[ff:, cut])).astype(BF)
                    for s in range(4):
                        at = (r * 4 + s) * block
                        keep_ref[at : at + block, to] = value[2 * s * block : (2 * s + 1) * block]
                        send_ref[at : at + block, to] = value[(2 * s + 1) * block : (2 * s + 2) * block]

    return run(
        kernel,
        [shape((own, 2 * piece))] * 2,
        [*acts, *attns, *w_cat],
        flops=8 * own * piece * (ff + hd),
    )


def cut_tensor(keeps, gots, small, small_got):
    width = keeps[0].shape[1]
    block = ROWS
    groups = sum(v.shape[0] for v in keeps) // (4 * block)
    lines = groups * block
    extra = 2 * SMALL if small is not None else 0
    count = len(keeps)

    def kernel(*refs):
        own_ref, *sends = refs[-4:]
        at = 0
        for keep_ref, got_ref in zip(refs[:count], refs[count : 2 * count]):
            for first in range(0, keep_ref.shape[0], 4 * block):
                to = slice(at, at + block)
                at += block
                for s in range(4):
                    cut = slice(first + s * block, first + (s + 1) * block)
                    value = keep_ref[cut, :].astype(F32) + got_ref[cut, :].astype(F32)
                    if s == 0:
                        own_ref[to, :] = value
                    else:
                        sends[s - 1][to, :] = value.astype(BF)
        if extra:
            both = refs[2 * count][...] + refs[2 * count + 1][...]
            own_ref[lines : lines + SMALL, :] = both
            both = jnp.concatenate([both, jnp.zeros_like(both)], axis=0).astype(BF)
            for send in sends:
                send[lines:, :] = both

    sent = shape((lines + extra, width))
    kept = shape((lines + extra // 2, width), F32)
    return run(kernel, [kept, sent, sent, sent], [*keeps, *gots] + ([small, small_got] if extra else []))


def sum_tensor(place, keeps, gots, small, small_got):
    own, *sends = cut_tensor(keeps, gots, small, small_got)
    parts = []
    for s, v in enumerate(sends):
        parts.append(place.over_z(v, s + 1))
    return (own, *parts)


def spread_tensor(place, v):
    got = [v]
    for s in (1, 2, 3):
        got.append(place.over_z(v, s))
    out = []
    for g in got:
        out += [g, place.over_k(g)]
    return out


def own_rows(ref, block):
    half = ref.shape[0] // 2
    return jnp.concatenate([ref[:block, :], ref[half : half + block, :]], axis=0)


def residual(own, parts, h, vec, dtype):
    rows, width = own.shape
    block = rows // 2

    def kernel(own_ref, p1, p2, p3, h_ref, vec_ref, out_ref):
        total = own_ref[...] + p1[...].astype(F32) + p2[...].astype(F32) + p3[...].astype(F32)
        out_ref[...] = (own_rows(h_ref, block).astype(F32) + total + vec_ref[4:5, :] + vec_ref[5:6, :]).astype(dtype)

    return run(kernel, [shape((rows, width), dtype)], [own, *parts, h, vec])[0]


def first_grads_attn(grad, w_cat, hd):
    rows, width = grad.shape
    own, piece = rows // 2, width // 2
    total = w_cat[0].shape[0]
    last = ((1,), (1,))

    def kernel(g_ref, w0, w1, own_ref, send_ref):
        lines = pl.ds(total - hd, hd)
        value = dot(g_ref[:, :piece], w0[lines, :], last) + dot(g_ref[:, piece:], w1[lines, :], last)
        own_ref[...] = value[:own].astype(BF)
        send_ref[...] = value[own:].astype(BF)

    return run(kernel, [shape((own, hd))] * 2, [grad, *w_cat], flops=2 * rows * width * hd)


def first_grads_act(grad, w_cat, hd):
    rows, width = grad.shape
    own, piece = rows // 2, width // 2
    ff = w_cat[0].shape[0] - hd
    tile = ff // 4
    last = ((1,), (1,))

    def kernel(g_ref, w0, w1, own_ref, first_ref, second_ref):
        @pl.loop(0, 4)
        def _(i):
            lines = pl.ds(pl.multiple_of(i * tile, tile), tile)
            value = dot(g_ref[:, :piece], w0[lines, :], last) + dot(g_ref[:, piece:], w1[lines, :], last)
            own_ref[:, lines] = value[:own].astype(BF)
            to = pl.ds(pl.multiple_of(lax.rem(i, 2) * tile, tile), tile)

            @pl.when(i < 2)
            def _():
                first_ref[:, to] = value[own:].astype(BF)

            @pl.when(i >= 2)
            def _():
                second_ref[:, to] = value[own:].astype(BF)

    outs = [shape((own, ff)), shape((own, ff // 2)), shape((own, ff // 2))]
    return run(kernel, outs, [grad, *w_cat], flops=2 * rows * width * ff)


def hidden_grads(own, first, second, slope):
    rows, ff = own.shape
    half = ff // 2

    def kernel(own_ref, first_ref, second_ref, slope_ref, out_ref):
        for i, got in enumerate((first_ref, second_ref)):
            cut = slice(i * half, (i + 1) * half)
            value = own_ref[:, cut].astype(F32) + got[...].astype(F32)
            out_ref[:, cut] = (value * slope_ref[:, cut]).astype(BF)

    return run(kernel, [shape((rows, ff))], [own, first, second, slope])[0]


def attention_grads(d_own, d_got, attn_out, probs, queries, keys, values, tables):
    own, hd = queries.shape
    rows = keys.shape[0]
    scaling = hd**-0.5

    def kernel(do, dg, o_ref, p_ref, q_ref, k_ref, v_ref, cos_ref, low_ref, high_ref, out_ref):
        grad = (do[...].astype(F32) + dg[...].astype(F32)).astype(BF)
        row_dot = jnp.sum(grad.astype(F32) * o_ref[...].astype(F32), axis=-1, keepdims=True)
        d_prob = dot(grad, v_ref[...], ((1,), (1,)))
        probs = p_ref[...]
        d_score = (probs * (d_prob - row_dot)).astype(BF)
        tab = (cos_ref[...], low_ref[...], high_ref[...])
        dq = dot(d_score, k_ref[...]) * scaling
        dq = turn_in(dq, tuple(a[:own] for a in tab), True).astype(BF)
        out_ref[:own, 2 * hd :] = dq[:, :128]
        out_ref[own:, 2 * hd :] = dq[:, 128:]
        dk = dot(d_score, q_ref[...], ((0,), (0,))) * scaling
        out_ref[:, :hd] = turn_in(dk, tab, True).astype(BF)
        out_ref[:, hd : 2 * hd] = dot(probs.astype(BF), grad, ((0,), (0,))).astype(BF)

    return run(
        kernel,
        [shape((rows, 2 * hd + 128))],
        [d_own, d_got, attn_out, probs, queries, keys, values, *tables],
        flops=8 * own * rows * hd,
    )[0]


SMALL = 8


def second_grads(r, pre, dkv_own, dkv_got, w_qkv, w_up, h, cols, grad, vec, before):
    rows, width = h.shape
    own = rows // 2
    piece = width // 2
    tile = piece // 2
    block = own // 8
    hd, ff = w_qkv[0].shape[1] // 3, pre.shape[1]
    last = ((1,), (1,))
    at, cross = slice(r * own, (r + 1) * own), slice((1 - r) * own, (2 - r) * own)

    def kernel(p_ref, kvo, kvg, wq0, wq1, wu0, wu1, h_ref, c_ref, g_ref, vec_ref, *refs):
        keep_ref, send_ref, gain_ref, qkv_ref = refs[-4:]
        qkv_ref[:, :hd] = unfold((kvo, kvg)[r], hd)
        both = kvo[at, : 2 * hd].astype(F32) + kvg[cross, : 2 * hd].astype(F32)
        qkv_ref[:, hd:] = both.astype(BF)
        gain_ref[...] = jnp.zeros((SMALL, width), F32) if before is None else refs[0][...]

        @pl.loop(0, 2)
        def _(n):
            lines = pl.ds(pl.multiple_of(n * tile, tile), tile)
            for j in range(2):
                cut = pl.ds(pl.multiple_of(j * piece + n * tile, tile), tile)
                d_mlp = dot(p_ref[...], (wu0, wu1)[j][lines, :], last)
                d_attn = dot(qkv_ref[...], (wq0, wq1)[j][lines, :], last)
                normed = (h_ref[at, cut].astype(F32) - c_ref[at, 0:1]) * c_ref[at, 1:2]
                both = (d_attn * vec_ref[0:1, cut] + d_mlp * vec_ref[2:3, cut]).astype(BF)
                for s in range(4):
                    to = slice(s * block, (s + 1) * block)
                    keep_ref[to, cut] = both[2 * s * block : (2 * s + 1) * block]
                    send_ref[to, cut] = both[(2 * s + 1) * block : (2 * s + 2) * block]
                add = (d_attn * normed, d_attn, d_mlp * normed, d_mlp, g_ref[at, cut].astype(F32))
                for i, v in enumerate(add):
                    gain_ref[i : i + 1, cut] += jnp.sum(v, axis=0, keepdims=True)

        gain_ref[5:6, :ff] += jnp.sum(p_ref[...].astype(F32), axis=0, keepdims=True)
        gain_ref[6:7, : 3 * hd] += jnp.sum(qkv_ref[...].astype(F32), axis=0, keepdims=True)

    return run(
        kernel,
        [shape((own // 2, width)), shape((own // 2, width)), shape((SMALL, width), F32)],
        [pre, dkv_own, dkv_got, *w_qkv, *w_up, h, cols, grad, vec] + ([] if before is None else [before]),
        flops=rows * width * (3 * hd + ff),
        scratch=[pltpu.VMEM((own, 3 * hd), BF)],
    )


def own_stats(halves, small, small_got, h, cols):
    width = small.shape[1]
    block, rows = ROWS, 2 * ROWS
    count = 4 * len(halves)

    def kernel(*refs):
        groups = [refs[i : i + 4] for i in range(0, count, 4)]
        s_ref, sg_ref, h_ref, c_ref, comb_ref, sums_ref, small_ref = refs[count:]
        each = rows // len(groups)
        add = lambda parts: sum(p[:each, :].astype(F32) for p in parts)
        comb = jnp.concatenate([add(parts) for parts in groups], axis=0)
        comb_ref[...] = comb
        c = own_rows(c_ref, block)
        normed = (own_rows(h_ref, block).astype(F32) - c[:, 0:1]) * c[:, 1:2]
        lane = lax.broadcasted_iota(jnp.int32, (rows, 128), 1)
        first = jnp.sum(comb, axis=-1, keepdims=True)
        second = jnp.sum(comb * normed, axis=-1, keepdims=True)
        sums_ref[...] = jnp.where(lane == 0, first, second)
        total = groups[-1][0][each:, :]
        for p in groups[-1][1:]:
            total = total + p[each:, :].astype(F32)[:SMALL]
        line = lax.broadcasted_iota(jnp.int32, (SMALL, width), 0)
        small_ref[:SMALL, :] = jnp.where(line < 4, total, s_ref[...])
        small_ref[SMALL:, :] = sg_ref[...]

    return run(
        kernel,
        [shape((rows, width), F32), shape((rows, 128), F32), shape((2 * SMALL, width), F32)],
        [p for parts in halves for p in parts] + [small, small_got, h, cols],
    )


def input_grad(comb, sums, got, h, cols, grad):
    rows, width = comb.shape
    block = rows // 2

    def kernel(comb_ref, s_ref, g_ref, h_ref, c_ref, grad_ref, out_ref):
        c = own_rows(c_ref, block)
        normed = (own_rows(h_ref, block).astype(F32) - c[:, 0:1]) * c[:, 1:2]
        there = g_ref[...]
        total = (s_ref[...] + jnp.concatenate([there[block:], there[:block]], axis=0)) / (2 * width)
        change = comb_ref[...] - total[:, 0:1] - normed * total[:, 1:2]
        out_ref[...] = (own_rows(grad_ref, block).astype(F32) + c[:, 1:2] * change).astype(BF)

    return run(kernel, [shape((rows, width))], [comb, sums, got, h, cols, grad])[0]


def grads_cat(acts, attns, grad):
    own, ff = acts[0].shape
    hd = attns[0].shape[1]
    width = grad.shape[1]
    piece = width // 2
    first = ((0,), (0,))

    def kernel(a0, a1, t0, t1, g_ref, own_ref, send_ref):
        def emit(lines, left, right):
            value = dot(left, g_ref[:own, :], first) + dot(right, g_ref[own:, :], first)
            own_ref[lines, :] = value[:, :piece].astype(BF)
            send_ref[lines, :] = value[:, piece:].astype(BF)

        @pl.loop(0, ff // hd)
        def _(i):
            lines = pl.ds(pl.multiple_of(i * hd, hd), hd)
            emit(lines, a0[:, lines], a1[:, lines])

        emit(pl.ds(ff, hd), t0[...], t1[...])

    return run(
        kernel,
        [shape((ff + hd, piece))] * 2,
        [*acts, *attns, grad],
        flops=4 * own * width * (ff + hd),
    )


def grads_up(mlp_in, pres):
    rows, width = mlp_in.shape
    own, piece = rows // 2, width // 2
    ff = pres[0].shape[1]
    tile = 256
    first = ((0,), (0,))

    def kernel(m_ref, p0, p1, own_ref, send_ref):
        def product(start):
            cut = pl.ds(pl.multiple_of(start, tile), tile)
            return (dot(m_ref[:own, cut], p0[...], first) + dot(m_ref[own:, cut], p1[...], first)).astype(BF)

        @pl.loop(0, 2 * piece // tile)
        def _(i):
            value = product(i * tile)

            @pl.when(i < piece // tile)
            def _():
                own_ref[pl.ds(pl.multiple_of(i * tile, tile), tile), :] = value

            @pl.when(i >= piece // tile)
            def _():
                send_ref[pl.ds(pl.multiple_of(i * tile - piece, tile), tile), :] = value

    return run(kernel, [shape((piece, ff))] * 2, [mlp_in, *pres], flops=2 * rows * width * ff)


def fill_qkv(out_ref, own_ref, got_ref, hd):
    half = out_ref.shape[0] // 2
    for r in range(2):
        at = slice(r * half, (r + 1) * half)
        cross = slice((1 - r) * half, (2 - r) * half)
        out_ref[at, :hd] = unfold((own_ref, got_ref)[r], hd)
        both = own_ref[at, : 2 * hd].astype(F32) + got_ref[cross, : 2 * hd].astype(F32)
        out_ref[at, hd:] = both.astype(BF)


def grads_qkv(attn_in, dkvq_own, dkvq_got, hd):
    rows, width = attn_in.shape
    piece = width // 2

    def kernel(a_ref, do_ref, dg_ref, own_ref, send_ref, full):
        fill_qkv(full, do_ref, dg_ref, hd)
        for j, ref in ((1, send_ref), (0, own_ref)):
            value = dot(a_ref[:, j * piece : (j + 1) * piece], full[...], ((0,), (0,)))
            ref[...] = value.astype(BF)

    return run(
        kernel,
        [shape((piece, 3 * hd))] * 2,
        [attn_in, dkvq_own, dkvq_got],
        flops=6 * rows * width * hd,
        scratch=[pltpu.VMEM((rows, 3 * hd), BF)],
    )


def move(place, outs, arrays, plan, parts):
    count = len(arrays)

    def kernel(at, *refs):
        ins, results = refs[:count], refs[count : count + len(outs)]
        buffers, into, outof = refs[count + len(outs) : -2], refs[-2], refs[-1]
        steps = plan(at[0], ins, results)
        for i, (choices, target) in enumerate(steps):
            for condition, source in choices:
                @pl.when(condition)
                def _():
                    pltpu.make_async_copy(source, buffers[i], into.at[i]).start()

        for i, (choices, target) in enumerate(steps):
            pltpu.make_async_copy(choices[0][1], buffers[i], into.at[i]).wait()
            pltpu.make_async_copy(buffers[i], target, outof.at[i]).start()
        for i, (choices, target) in enumerate(steps):
            pltpu.make_async_copy(buffers[i], target, outof.at[i]).wait()

    anywhere = pl.BlockSpec(memory_space=pl.ANY)
    return run(
        kernel,
        outs,
        [scalar(place.k), *arrays],
        scalars=1,
        in_specs=[anywhere] * count,
        out_specs=[anywhere] * len(outs),
        scratch=[pltpu.VMEM(p, BF) for p in parts]
        + [pltpu.SemaphoreType.DMA((len(parts),)), pltpu.SemaphoreType.DMA((len(parts),))],
        grid=(1,),
        vmem=60,
    )


def pick_up(place, fc1, got, layer):
    piece, full = fc1.shape
    half, part = full // 2, piece // 4

    def plan(k, refs, outs):
        steps = []
        for i in range(4):
            lines = pl.ds(i * part, part)
            source = lambda ref, j: ref.at[lines, pl.ds(j * half, half)]
            choices = ((k == layer, source(refs[0], layer)), (k != layer, source(refs[1], 1 - layer)))
            steps.append((choices, outs[0].at[lines, :]))
        return steps

    return move(place, [shape((piece, half))], [fc1, got], plan, [(part, half)] * 4)[0]


def pick_qkv(place, keep, got, layer):
    piece, width = keep.shape
    part = piece // 4

    def plan(k, refs, outs):
        steps = []
        for i in range(4):
            lines = pl.ds(i * part, part)
            choices = ((k == layer, refs[0].at[lines, :]), (k != layer, refs[1].at[lines, :]))
            steps.append((choices, outs[0].at[lines, :]))
        return steps

    return move(place, [shape((piece, width))], [keep, got], plan, [(part, width)] * 4)[0]


def pick_cat(place, fc2, dense, down_got, dense_got, layer):
    full, piece = fc2.shape
    ff, hd = full // 2, dense.shape[0] // 2
    tiles = ff // hd

    def plan(k, refs, outs):
        steps = []
        for i in range(tiles + 1):
            mine, other = (refs[0], refs[2]) if i < tiles else (refs[1], refs[3])
            source = lambda ref, j: ref.at[pl.ds(j * ff + i * hd if i < tiles else j * hd, hd), :]
            choices = ((k == layer, source(mine, layer)), (k != layer, source(other, 1 - layer)))
            steps.append((choices, outs[0].at[pl.ds(i * hd, hd), :]))
        return steps

    return move(place, [shape((ff + hd, piece))], [fc2, dense, down_got, dense_got], plan, [(hd, piece)] * (tiles + 1))[0]


def stream(place, arrays, chunk, count, outs, buffers, emit, wanted):
    flat = [a for pair in arrays for a in pair]
    lanes = [pair[0].shape[1] for pair in arrays]
    kinds = [pair[0].dtype for pair in arrays]
    per = max(len(emit_views) for emit_views in [wanted])

    def kernel(at, *refs):
        ins = refs[: len(flat)]
        results = refs[len(flat) : len(flat) + len(outs)]
        rest = refs[len(flat) + len(outs) :]
        held, made, into, outof = rest[: len(arrays)], rest[len(arrays)], rest[-2], rest[-1]
        k = at[0]
        where = [0]
        for pair in arrays:
            where.append(where[-1] + len(pair))

        def fetch(n, i, layer):
            source = ins[where[n] + (layer if len(arrays[n]) == 2 else 0)]
            return pltpu.make_async_copy(source.at[pl.ds(i * chunk, chunk), :], held[n].at[i], into.at[n, i])

        for i in range(count):
            for n, pair in enumerate(arrays):
                if len(pair) == 1:
                    fetch(n, i, 0).start()
                    continue
                for layer in range(2):
                    @pl.when(k == layer)
                    def _():
                        fetch(n, i, layer).start()

        for i in range(count):
            for n in range(len(arrays)):
                fetch(n, i, 0).wait()
            for layer in range(2):
                @pl.when(k == layer)
                def _():
                    emit(layer, i, [h.at[i] for h in held], made.at[i])

            for j, view in enumerate(wanted):
                source, target = view(i, made.at[i], results)
                pltpu.make_async_copy(source, target, outof.at[i, j]).start()
        for i in range(count):
            for j, view in enumerate(wanted):
                source, target = view(i, made.at[i], results)
                pltpu.make_async_copy(source, target, outof.at[i, j]).wait()

    anywhere = pl.BlockSpec(memory_space=pl.ANY)
    return run(
        kernel,
        outs,
        [scalar(place.k), *flat],
        scalars=1,
        grid=(1,),
        in_specs=[anywhere] * len(flat),
        out_specs=[anywhere] * len(outs),
        scratch=[pltpu.VMEM((count, chunk, w), d) for w, d in zip(lanes, kinds)]
        + [pltpu.VMEM((count, *buffers[0]), buffers[1])]
        + [pltpu.SemaphoreType.DMA((len(arrays), count)), pltpu.SemaphoreType.DMA((count, per))],
        vmem=60,
    )


def sum_for_owner(place, ours, theirs):
    rows, width = ours[0].shape
    chunk = 256
    swapped = [ours[::-1], theirs[::-1]]

    def emit(layer, i, refs, buffer):
        @pl.loop(0, chunk // 32)
        def _(n):
            at = pl.ds(pl.multiple_of(n * 32, 32), 32)
            buffer[at, :] = (refs[0][at, :].astype(F32) + refs[1][at, :].astype(F32)).astype(BF)

    view = lambda i, buffer, outs: (buffer, outs[0].at[pl.ds(i * chunk, chunk), :])
    return stream(place, swapped, chunk, rows // chunk, [shape((rows, width))], ((chunk, width), BF), emit, [view])[0]


def finish_up(place, ours, theirs, arrived):
    rows, width = arrived.shape
    chunk = rows // 4

    def emit(layer, i, refs, buffer):
        mine, other = pl.ds(layer * width, width), pl.ds((1 - layer) * width, width)

        @pl.loop(0, chunk // 32)
        def _(n):
            at = pl.ds(pl.multiple_of(n * 32, 32), 32)
            buffer[at, mine] = refs[0][at, :].astype(F32) + refs[1][at, :].astype(F32)
            buffer[at, other] = refs[2][at, :].astype(F32)

    view = lambda i, buffer, outs: (buffer, outs[0].at[pl.ds(i * chunk, chunk), :])
    return stream(
        place,
        [ours, theirs, [arrived]],
        chunk,
        4,
        [shape((rows, 2 * width), F32)],
        ((chunk, 2 * width), F32),
        emit,
        [view],
    )[0]


def finish_cat(place, ours, theirs, arrived, hd):
    rows, width = arrived.shape
    tiles = rows // hd - 1

    def emit(layer, i, refs, buffer):
        @pl.loop(0, hd // 32)
        def _(n):
            at = pl.ds(pl.multiple_of(n * 32, 32), 32)
            buffer[layer, at, :] = refs[0][at, :].astype(F32) + refs[1][at, :].astype(F32)
            buffer[1 - layer, at, :] = refs[2][at, :].astype(F32)

    def view(half):
        def pick(i, buffer, outs):
            lines = pl.ds(i * hd if i < tiles else 0, hd)
            return buffer.at[half], outs[0 if i < tiles else 1].at[half, lines, :]

        return pick

    return stream(
        place,
        [ours, theirs, [arrived]],
        hd,
        tiles + 1,
        [shape((2, tiles * hd, width), F32), shape((2, hd, width), F32)],
        ((2, hd, width), F32),
        emit,
        [view(0), view(1)],
    )


def finish_qkv(place, ours, theirs, arrived):
    rows, width = arrived.shape
    chunk = rows // 4
    lines = 2 * width // 128

    def emit(layer, i, refs, buffer):
        @pl.loop(0, width // 128)
        def _(c):
            cut = pl.ds(pl.multiple_of(c * 128, 128), 128)
            mine = refs[0][:, cut].astype(F32) + refs[1][:, cut].astype(F32)
            buffer[pl.ds(2 * c + layer, chunk, stride=lines), :] = mine
            buffer[pl.ds(2 * c + 1 - layer, chunk, stride=lines), :] = refs[2][:, cut].astype(F32)

    view = lambda i, buffer, outs: (buffer, outs[0].at[pl.ds(i * chunk * lines, chunk * lines), :])
    out = stream(
        place,
        [ours, theirs, [arrived]],
        chunk,
        4,
        [shape((rows * lines, 128), F32)],
        ((chunk * lines, 128), F32),
        emit,
        [view],
    )[0]
    hd = width // 3
    out = out.reshape(rows, 3, hd // 128, 2, 128)
    return jnp.transpose(out, (0, 1, 3, 2, 4)).reshape(1, rows, 3, 2, hd)


def deliver_two(place, out, out_got, grad_in, grad_got):
    rows, width = out.shape
    block, half = rows // 2, width // 2
    n, m, nt = place.n, place.m, place.nt

    def split(at, o_ref, og_ref, g_ref, gg_ref, *sends):
        k, c, t = at[0], at[1], at[2]
        for core, (mine, other) in enumerate(((g_ref, gg_ref), (o_ref, og_ref))):
            @pl.when(k == core)
            def _():
                low, high = (mine, other) if core == 0 else (other, mine)
                for a in range(2):
                    rel = (t % 2) ^ a ^ (c % 2)
                    lines = pl.ds(pl.multiple_of(rel * block, block), block)
                    for b in range(2):
                        cut = slice(b * half, (b + 1) * half)
                        sends[a * 2 + b][:block, :] = low[lines, cut]
                        sends[a * 2 + b][block:, :] = high[lines, cut]

    spot = scalar(place.k, place.c, place.t)
    sends = run(split, [shape((2 * block, half))] * 4, [spot, out, out_got, grad_in, grad_got], scalars=1)
    arrived = []
    for a in range(2):
        for b in range(2):
            pairs = []
            for c in range(n):
                for t in range(nt):
                    y, cl = c // m, c % m
                    pairs.append((c * nt + t, (((t % 2) ^ a) * 2 + t // 2) * nt + (y ^ b) * 2 + cl))
            arrived.append(lax.ppermute(sends[a * 2 + b], (CTX, TENSOR), pairs))

    def join(at, *refs):
        got, out_ref = refs[:4], refs[4]
        c, t = at[1], at[2]
        for a in range(2):
            for b in range(2):
                first, micro = (c // 2) ^ a, (t // 2) ^ b
                lines = pl.ds(pl.multiple_of(first * 2 * block, 2 * block), 2 * block)
                out_ref[micro, lines, :] = got[a * 2 + b][...].astype(F32)

    return run(join, [shape((2, 4 * block, half), F32)], [spot, *arrived], scalars=1)[0][None]


def split_heads(place, qkv_weight):
    piece, _, _, hd = qkv_weight.shape
    lines = qkv_weight.reshape(piece, 3, 2, hd // 128, 128)
    lines = jnp.transpose(lines, (0, 1, 3, 2, 4)).reshape(-1, 128)
    count = 6 * hd // 128

    def kernel(at, in_ref, keep_ref, send_ref, wide):
        wide[...] = in_ref[...].astype(F32)
        for chunk in range(count // 2):
            columns = pl.ds(chunk * 128, 128)
            keep_ref[:, columns] = wide[pl.ds(2 * chunk + at[0], piece, stride=count), :].astype(BF)
            send_ref[:, columns] = wide[pl.ds(2 * chunk + 1 - at[0], piece, stride=count), :].astype(BF)

    return run(
        kernel,
        [shape((piece, 3 * hd))] * 2,
        [scalar(place.k), lines],
        scalars=1,
        scratch=[pltpu.VMEM(lines.shape, F32)],
    )


def body_two(
    x_in,
    cotangent,
    block_pos,
    norm1_gain,
    norm1_bias,
    norm2_gain,
    norm2_bias,
    qkv_weight,
    qkv_bias,
    dense_weight,
    dense_bias,
    fc1_weight,
    fc1_bias,
    fc2_weight,
    fc2_bias,
):
    place = Place()
    k, n, nt = place.k, place.n, place.nt
    is_first = k == 0
    tokens = x_in.shape[1]
    seq = tokens * n
    block = tokens // nt
    piece = fc1_weight.shape[1]
    hd = dense_weight.shape[2]
    ff = fc1_weight.shape[2] // 2

    def x_swap(v):
        return place.over_x(v, 0)

    def y_swap(v):
        return place.over_y(v)

    heads_bias = jnp.pad(qkv_bias.reshape(1, -1), ((0, 0), (0, piece - qkv_bias.size)))
    vectors = [norm1_gain, norm1_bias, norm2_gain, norm2_bias, dense_bias, fc2_bias, fc1_bias[0], heads_bias]
    x_pieces = send_tokens(place, x_in, vectors)

    fc1, fc2 = fc1_weight[0], fc2_weight[0]
    dense = dense_weight.reshape(2 * hd, piece)

    def k_swap(v):
        return place.over_k(v)

    up_got = k_swap(fc1)
    head_keep, head_send = split_heads(place, qkv_weight[0])
    head_got = k_swap(head_send)
    down_got, dense_got = k_swap(fc2), k_swap(dense)
    layers = []
    for layer in range(2):
        mine_q = pick_qkv(place, head_keep, head_got, layer)
        mine_u = pick_up(place, fc1, up_got, layer)
        mine_c = pick_cat(place, fc2, dense, down_got, dense_got, layer)
        layers.append(((mine_q, y_swap(mine_q)), (mine_u, y_swap(mine_u)), (mine_c, y_swap(mine_c))))

    code = (place.cl * nt + place.t) * 2 + k
    absolute = jnp.arange(seq // block, dtype=jnp.int32) ^ code
    slot = (absolute[:, None] * block + jnp.arange(block, dtype=jnp.int32)[None]).reshape(-1)
    per_block = seq // block_pos.shape[1]
    order = jnp.where(place.y == 0, block_pos[0], block_pos[1])
    hit = (slot // per_block)[:, None] == jnp.arange(block_pos.shape[1], dtype=jnp.int32)[None]
    pos = jnp.sum(jnp.where(hit, order[None], 0), axis=1) * per_block + slot % per_block
    pos_row = jnp.broadcast_to(pos.astype(F32)[None], (8, seq))
    cosine, sine = rotary_tables(pos)
    blank = jnp.zeros((seq, 128 - ROT), F32)
    empty = jnp.zeros((seq, SHIFT), F32)
    tables = (
        jnp.concatenate([cosine, blank + 1.0], axis=1),
        jnp.concatenate([-sine[:, :SHIFT], empty, blank], axis=1),
        jnp.concatenate([empty, sine[:, SHIFT:], blank], axis=1),
    )

    h, stat, vecs, lines = unpack_tokens(place, x_pieces, True)
    by_place = jnp.take(lines[:, :, 6:8], jnp.arange(n, dtype=jnp.int32) ^ place.c, axis=1, mode="clip")
    qkv_biases, fc1_biases = [], []
    for layer in range(2):
        fc1_b = by_place[layer, :, 0].reshape(2, ff)
        qkv_b = by_place[layer, :, 1, : qkv_bias.size].reshape(n, 3, 2, hd // n)
        qkv_b = jnp.where(is_first, qkv_b[:, :, 0], qkv_b[:, :, 1])
        qkv_b = jnp.transpose(qkv_b, (1, 0, 2)).reshape(1, 3 * hd)
        qkv_biases.append(jnp.broadcast_to(qkv_b, (8, 3 * hd)))
        fc1_biases.append(jnp.where(is_first, fc1_b[0], fc1_b[1]))

    cot_pieces = send_tokens(place, cotangent, [])
    saved = []
    for layer in range(2):
        w_qkv, w_up, w_cat = layers[layer]
        stat_x = x_swap(stat)
        attn_in, mlp_in, cols = norm_inputs(h, stat, stat_x, vecs[layer])
        q_own, kvq = product_qkv(attn_in, w_qkv)
        f_own, f_send = product_up(mlp_in, w_up)
        kvq_got, f_got = x_swap(kvq), x_swap(f_send)
        queries, keys, values, probs, attn_out = attention(
            q_own, kvq, kvq_got, qkv_biases[layer], tables, pos_row
        )
        pre = f_own.astype(F32) + f_got.astype(F32) + fc1_biases[layer]
        cdf = 0.5 * (1.0 + lax.erf(pre * 0.7071067811865476))
        act = (pre * cdf).astype(BF)
        slope = cdf + pre * jnp.exp(-0.5 * pre * pre) * 0.3989422804014327
        acts = (act, x_swap(act))
        attns = (attn_out, x_swap(attn_out))
        keep, send = second_products(acts, attns, w_cat)
        own, *parts = sum_tensor(place, [keep], [k_swap(send)], None, None)
        out = residual(own, parts, h, vecs[layer], BF)
        saved.append((h, cols, attn_in, mlp_in, queries, keys, values, probs, attn_out, attns, acts, slope))
        if layer == 0:
            pieces = spread_tensor(place, out)
            h, stat = assemble(pieces, True)
    grad = unpack_tokens(place, cot_pieces, False)[0]

    results = [None, None]
    for layer in (1, 0):
        w_qkv, w_up, w_cat = layers[layer]
        h, cols, attn_in, mlp_in, queries, keys, values, probs, attn_out, attns, acts, slope = saved[layer]
        t_own, t_send = first_grads_attn(grad, w_cat, hd)
        t_got = x_swap(t_send)
        a_own, a_first, a_second = first_grads_act(grad, w_cat, hd)
        a_got = (x_swap(a_first), x_swap(a_second))
        dkvq = attention_grads(t_own, t_got, attn_out, probs, queries, keys, values, tables)
        dkvq_got = x_swap(dkvq)
        d_pre = hidden_grads(a_own, *a_got, slope)
        pres = (d_pre, x_swap(d_pre))
        small, halves, keeps, gots = None, [], [], []
        for r in range(2):
            keep, send, small = second_grads(r, pres[r], dkvq, dkvq_got, w_qkv, w_up, h, cols, grad, vecs[layer], small)
            keeps.append(keep)
            gots.append(k_swap(send))
            if r == 1:
                small_got = k_swap(small)
            if layer == 1:
                behind = (small, small_got) if r else (None, None)
                halves.append(sum_tensor(place, keeps[r:], gots[r:], *behind))
        if layer == 0:
            halves.append(sum_tensor(place, keeps, gots, small, small_got))
        comb, sums, small = own_stats(halves, small, small_got, h, cols)
        sums_got = x_swap(sums)
        grad_in = input_grad(comb, sums, sums_got, h, cols, grad)
        cat_own, cat_out = grads_cat(acts, attns, grad)
        up_own, up_out = grads_up(mlp_in, pres)
        qkv_own, qkv_out = grads_qkv(attn_in, dkvq, dkvq_got, hd)
        results[layer] = ((cat_own, y_swap(cat_out)), (up_own, y_swap(up_out)), (qkv_own, y_swap(qkv_out)), small)
        if layer == 1:
            pieces = spread_tensor(place, grad_in)
            grad = assemble(pieces, False)[0]

    boundary = deliver_two(place, out, k_swap(out), grad_in, k_swap(grad_in))

    def to_owner(which):
        ours = [results[layer][which][0] for layer in range(2)]
        theirs = [results[layer][which][1] for layer in range(2)]
        sent = sum_for_owner(place, ours, theirs)
        return ours, theirs, k_swap(sent)

    cat, up, heads = to_owner(0), to_owner(1), to_owner(2)
    g_down, g_out = finish_cat(place, *cat, hd)
    g_down, g_out = g_down.reshape(1, 2 * ff, piece), g_out[None]
    g_up = finish_up(place, *up)[None]
    g_qkv = finish_qkv(place, *heads)

    ours = jnp.where(is_first, results[0][3], results[1][3])
    across = y_swap(ours)
    gains = ours[:5, :piece] + across[:5, piece:]
    total = gains[:4].reshape(4, 1, piece)
    token_sum = gains[4:5]
    mine, other = ours[5:7] + across[5:7], ours[13:15] + across[13:15]
    low, high = jnp.where(is_first, mine, other), jnp.where(is_first, other, mine)
    tails = jnp.stack([low, high])
    qkv_b = tails[:, 1, : 3 * hd].reshape(2, 3, hd)
    qkv_b = jnp.transpose(lax.dynamic_slice_in_dim(qkv_b, place.c * (hd // n), hd // n, axis=2), (1, 0, 2))[None]
    fc1_b = lax.dynamic_slice_in_dim(tails[:, 0].reshape(-1), place.c * (2 * ff // n), 2 * ff // n)[None, None]
    return (
        boundary,
        total[0],
        total[1],
        total[2],
        total[3],
        g_qkv,
        qkv_b,
        g_out,
        token_sum,
        g_up,
        fc1_b,
        g_down,
        token_sum,
    )


def body(*args):
    two = lax.axis_size(CTX) == 4 and lax.axis_size(TENSOR) == 4
    if not two:
        return body_any(*args)
    return body_two(*args)


def solution(mesh):
    in_specs = (
        P(None, CTX, None),
        P(None, CTX, None),
        P(),
        P(SECTION, CTX),
        P(SECTION, CTX),
        P(SECTION, CTX),
        P(SECTION, CTX),
        P(SECTION, CTX, None, TENSOR, None),
        P(SECTION, None, TENSOR, CTX),
        P(SECTION, TENSOR, None, CTX),
        P(SECTION, CTX),
        P(SECTION, CTX, TENSOR),
        P(SECTION, TENSOR, CTX),
        P(SECTION, TENSOR, CTX),
        P(SECTION, CTX),
    )
    out_specs = (
        P(SECTION, None, CTX, TENSOR),
        P(SECTION, CTX),
        P(SECTION, CTX),
        P(SECTION, CTX),
        P(SECTION, CTX),
        P(SECTION, CTX, None, TENSOR, None),
        P(SECTION, None, TENSOR, CTX),
        P(SECTION, TENSOR, None, CTX),
        P(SECTION, CTX),
        P(SECTION, CTX, TENSOR),
        P(SECTION, TENSOR, CTX),
        P(SECTION, TENSOR, CTX),
        P(SECTION, CTX),
    )
    return jax.shard_map(body, mesh=mesh, in_specs=in_specs, out_specs=out_specs, check_vma=False)
```

```python
import jax
import jax.numpy as jnp
from jax import lax
from jax.experimental import pallas as pl
from jax.experimental.pallas import tpu as pltpu
from jax.sharding import PartitionSpec as P


ROT = 64
EPS = 1e-05
MASKED_SCORE = -1e30
BF = jnp.bfloat16
F32 = jnp.float32

CTX, TENSOR, SECTION = "ctx", "tensor", "section"


def dot(a, b, dims=((1,), (0,))):
    return lax.dot_general(a, b, (dims, ((), ())), preferred_element_type=F32)


def swap(v, axis, distance):
    size = lax.axis_size(axis)
    return lax.ppermute(v, axis, [(i, i ^ distance) for i in range(size)])


def rotary_tables(positions):
    inverse = 10000.0 ** (-(jnp.arange(ROT // 2, dtype=F32) * 2.0 / ROT))
    angles = positions.astype(F32)[:, None] * inverse[None, :]
    angles = jnp.concatenate([angles, angles], axis=-1)
    return (jnp.cos(angles), jnp.sin(angles))


def rotate(z, cosine, sine):
    half = ROT // 2
    lead = z[:, :ROT]
    turned = jnp.concatenate([-lead[:, half:], lead[:, :half]], axis=-1)
    return jnp.concatenate([lead * cosine + turned * sine, z[:, ROT:]], axis=-1)


def unrotate(g, cosine, sine):
    half = ROT // 2
    lead = g[:, :ROT]
    scaled = lead * sine
    turned = jnp.concatenate([scaled[:, half:], -scaled[:, :half]], axis=-1)
    return jnp.concatenate([lead * cosine + turned, g[:, ROT:]], axis=-1)


class Place:
    def __init__(self):
        self.k = lax.axis_index(SECTION)
        self.c = lax.axis_index(CTX)
        self.t = lax.axis_index(TENSOR)
        self.n = lax.axis_size(CTX)
        self.nt = lax.axis_size(TENSOR)
        self.m = self.n // 2
        self.bits = self.m.bit_length() - 1
        self.y = self.c // self.m
        self.cl = self.c % self.m

    def over_k(self, v):
        return swap(v, SECTION, 1)

    def over_y(self, v):
        return swap(v, CTX, self.m)

    def over_x(self, v, bit):
        return swap(v, CTX, 1 << bit)

    def over_z(self, v, distance):
        return swap(v, TENSOR, distance)

    def reduce_rows(self, v):
        cur = v
        for bit in reversed(range(self.bits)):
            half = cur.shape[0] // 2
            got = self.over_x(cur[half:].astype(BF), bit)
            cur = cur[:half].astype(F32) + got.astype(F32)
        return cur[0].astype(F32)

    def sum_rows(self, v):
        cur = v
        for bit in range(self.bits):
            got = self.over_x(cur.astype(BF), bit)
            shape = got.shape
            got = got.reshape(shape[0] >> (bit + 1), 2, 1 << bit, *shape[1:])
            got = jnp.concatenate([got[:, 1:], got[:, :1]], axis=1).reshape(shape)
            cur = cur.astype(F32) + got.astype(F32)
        return cur

    def gather_rows(self, v):
        cur = v[None]
        for bit in range(self.bits):
            cur = jnp.concatenate([cur, self.over_x(cur, bit)], axis=0)
        return cur.reshape(-1, v.shape[-1])

    def reduce_tensor(self, v):
        got = self.over_k(v[:, :, 1])
        cur = v[:, :, 0].astype(F32) + got.astype(F32)
        sent = cur.astype(BF)
        total = cur[:, 0]
        for s in range(1, self.nt):
            total = total + self.over_z(sent[:, s], s).astype(F32)
        return total

    def gather_tensor(self, v):
        parts = [v] + [self.over_z(v, s) for s in range(1, self.nt)]
        mine = jnp.stack(parts, axis=1)
        other = self.over_k(mine)
        return jnp.stack([mine, other], axis=2).reshape(-1, v.shape[-1])


def merge_stats(place, mean, spread, count):
    for bit in range(place.bits):
        got = place.over_x(jnp.stack([mean, spread]), bit)
        shape = mean.shape
        if mean.ndim == 2:
            pairs = got.reshape(2, shape[0] >> (bit + 1), 2, 1 << bit, shape[1])
            pairs = jnp.concatenate([pairs[:, :, 1:], pairs[:, :, :1]], axis=2)
            got = pairs.reshape(2, *shape)
        delta = got[0] - mean
        spread = spread + got[1] + delta * delta * (count * 0.5)
        mean = 0.5 * (mean + got[0])
        count = count * 2
    return mean, spread, count


def norm_stats(place, h):
    rows, width = h.shape
    wide = h.astype(F32)
    mean = jnp.mean(wide, axis=-1)
    centre = wide - mean[:, None]
    spread = jnp.sum(centre * centre, axis=-1)
    shape = (place.m, rows // place.m)
    mean, spread, count = merge_stats(place, mean.reshape(shape), spread.reshape(shape), float(width))
    inv = lax.rsqrt(spread / count + EPS)
    return mean.reshape(rows, 1), inv.reshape(rows, 1)


def layer_forward(place, h, w, small, tables):
    w_qkv, w_out, w_up, w_down = w
    rows = h.shape[0]
    m = place.m
    own = rows // m
    hd = w_out[0].shape[0]
    cosine, sine, pos = tables
    mean, inv = norm_stats(place, h)
    normed = (h.astype(F32) - mean) * inv
    attn_in = (normed * small["g1"] + small["b1"]).astype(BF)
    mlp_in = (normed * small["g2"] + small["b2"]).astype(BF)
    mixed = dot(attn_in, w_qkv).astype(BF).reshape(m, own, 3 * hd)
    hidden = dot(mlp_in, w_up).astype(BF).reshape(m, own, -1)
    kv = place.sum_rows(mixed[..., hd:]).reshape(rows, 2 * hd) + small["qkv_bias"][hd:]
    q = place.reduce_rows(mixed[..., :hd]) + small["qkv_bias"][:hd]
    queries = rotate(q, cosine[:own], sine[:own]).astype(BF)
    keys = rotate(kv[:, :hd], cosine, sine).astype(BF)
    values = kv[:, hd:].astype(BF)
    scores = dot(queries, keys, ((1,), (1,))) * (hd**-0.5)
    allowed = pos[:own, None] >= pos[None, :]
    scores = jnp.where(allowed, scores, MASKED_SCORE)
    top = jnp.max(scores, axis=-1, keepdims=True)
    exps = jnp.where(allowed, jnp.exp(scores - top), 0.0)
    total = jnp.sum(exps, axis=-1, keepdims=True)
    attn_out = (dot(exps.astype(BF), values) / total).astype(BF)
    probs = exps / total
    pre = place.reduce_rows(hidden) + small["fc1_bias"]
    cdf = 0.5 * (1.0 + lax.erf(pre * 0.7071067811865476))
    act = (pre * cdf).astype(BF)
    slope = cdf + pre * jnp.exp(-0.5 * pre * pre) * 0.3989422804014327
    attn_all = place.gather_rows(attn_out)
    act_all = place.gather_rows(act)
    part = jnp.concatenate(
        [dot(attn_all, w_out[j]) + dot(act_all, w_down[j]) for j in range(2)], axis=1
    ).astype(BF)
    branch = place.reduce_tensor(part.reshape(m, place.nt, 2, -1, part.shape[-1]))
    h_own = h.reshape(m, place.nt, 2, -1, h.shape[-1])[:, 0, 0].astype(F32)
    out = h_own + branch + small["out_bias"]
    saved = (h, mean, inv, attn_in, mlp_in, queries, keys, values, probs, attn_out, attn_all, act_all, slope)
    return out, saved


def layer_backward(place, grad, w, small, tables, saved):
    w_qkv, w_out, w_up, w_down = w
    h, mean, inv, attn_in, mlp_in, queries, keys, values, probs, attn_out, attn_all, act_all, slope = saved
    rows = h.shape[0]
    m = place.m
    own = rows // m
    hd = w_out[0].shape[0]
    width = h.shape[1] // 2
    scaling = hd**-0.5
    cosine, sine, _ = tables
    halves = (grad[:, :width], grad[:, width:])
    d_attn = sum(dot(halves[j], w_out[j], ((1,), (1,))) for j in range(2)).astype(BF)
    d_act = sum(dot(halves[j], w_down[j], ((1,), (1,))) for j in range(2)).astype(BF)
    grad_attn = place.reduce_rows(d_attn.reshape(m, own, hd)).astype(BF)
    row_dot = jnp.sum(grad_attn.astype(F32) * attn_out.astype(F32), axis=-1, keepdims=True)
    d_prob = dot(grad_attn, values, ((1,), (1,)))
    d_score = (probs * (d_prob - row_dot)).astype(BF)
    dq = unrotate(dot(d_score, keys) * scaling, cosine[:own], sine[:own]).astype(BF)
    dk = unrotate(dot(d_score, queries, ((0,), (0,))) * scaling, cosine, sine).astype(BF)
    dv = dot(probs.astype(BF), grad_attn, ((0,), (0,))).astype(BF)
    dkv = place.sum_rows(jnp.concatenate([dk, dv], axis=1).reshape(m, own, 2 * hd)).astype(BF)
    d_qkv = jnp.concatenate([place.gather_rows(dq), dkv.reshape(rows, 2 * hd)], axis=1)
    d_pre = (place.reduce_rows(d_act.reshape(m, own, -1)) * slope).astype(BF)
    d_pre_all = place.gather_rows(d_pre)
    d_mlp_in = dot(d_pre_all, w_up, ((1,), (1,)))
    d_attn_in = dot(d_qkv, w_qkv, ((1,), (1,)))
    normed = (h.astype(F32) - mean) * inv
    combined = (d_attn_in * small["g1"] + d_mlp_in * small["g2"]).astype(BF)
    gains = jnp.stack(
        [
            jnp.sum(d_attn_in * normed, axis=0),
            jnp.sum(d_attn_in, axis=0),
            jnp.sum(d_mlp_in * normed, axis=0),
            jnp.sum(d_mlp_in, axis=0),
            jnp.sum(grad.astype(F32), axis=0),
        ]
    )
    biases = jnp.concatenate(
        [jnp.sum(d_qkv.astype(F32), axis=0), jnp.sum(d_pre_all.astype(F32), axis=0)]
    )
    comb = place.reduce_tensor(combined.reshape(m, place.nt, 2, -1, combined.shape[-1]))
    pick = lambda v: v.reshape(m, place.nt, 2, -1, v.shape[-1])[:, 0, 0]
    own_normed = pick(normed)
    sums = jnp.stack([jnp.sum(comb, axis=-1), jnp.sum(comb * own_normed, axis=-1)])
    for bit in range(place.bits):
        got = place.over_x(sums, bit)
        shape = got.shape
        got = got.reshape(2, shape[1] >> (bit + 1), 2, 1 << bit, shape[2])
        got = jnp.concatenate([got[:, :, 1:], got[:, :, :1]], axis=2).reshape(shape)
        sums = sums + got
    sums = sums / (comb.shape[-1] * m)
    grad_in = pick(grad).astype(F32) + pick(inv) * (
        comb - sums[0][..., None] - own_normed * sums[1][..., None]
    )

    def both(make):
        mine, other = make(0), make(1).astype(BF)
        return mine + place.over_y(other).astype(F32)

    cut = lambda v, j: v[:, j * width : (j + 1) * width]
    g_down = both(lambda j: dot(act_all, halves[j], ((0,), (0,))))
    g_out = both(lambda j: dot(attn_all, halves[j], ((0,), (0,))))
    g_up = both(lambda j: dot(cut(mlp_in, j), d_pre_all, ((0,), (0,))))
    g_qkv = both(lambda j: dot(cut(attn_in, j), d_qkv, ((0,), (0,))))
    return grad_in, (g_qkv, g_out, g_up, g_down), gains, biases


def spread_tokens(place, v, index):
    _, tokens, width = v.shape
    n, m = place.n, place.m
    half = tokens // 2
    rows = lax.dynamic_slice_in_dim(v.astype(BF), place.k * half, half, axis=1)
    rows = rows.reshape(2, half, 2, m, width // n)
    rows = jnp.stack([rows[0], jnp.flip(rows[1], axis=1)])
    rows = jnp.transpose(rows, (0, 3, 1, 2, 4)).reshape(n, half, 2 * width // n)
    got = lax.all_to_all(rows, CTX, 0, 0)
    both = jnp.stack([got, place.over_k(got)])
    block = tokens // place.nt
    blocks = both.reshape(-1, block, 2 * width // n)
    return jnp.take(blocks, index, axis=0, mode="clip").reshape(-1, 2 * width // n)


def deliver(place, out, grad_in):
    is_first = place.k == 0
    n, m, nt = place.n, place.m, place.nt
    mine = jnp.where(is_first, grad_in, out).astype(BF)
    other = jnp.where(is_first, out, grad_in).astype(BF)
    got = place.over_k(other)
    low = jnp.where(is_first, mine, got)
    high = jnp.where(is_first, got, mine)
    block = mine.shape[1]
    width = mine.shape[2] // 2
    pieces = jnp.stack([low, high], axis=1).reshape(m, 2 * block, 2, width)
    quarter = m // 2
    t0 = place.t % 2
    rest = place.cl % quarter
    arrived = {}
    for a in range(m):
        dest_cl = (t0 * quarter + rest) ^ a
        rel = dest_cl ^ place.cl
        chosen = lax.dynamic_index_in_dim(pieces, rel, axis=0, keepdims=False)
        for b in range(2):
            pairs = []
            for c in range(n):
                for t in range(nt):
                    y, cl = c // m, c % m
                    s0, s1 = t % 2, t // 2
                    dc = ((s0 * quarter + cl % quarter) ^ a) * 2 + s1
                    dt = (y ^ b) * 2 + cl // quarter
                    pairs.append((c * nt + t, dc * nt + dt))
            arrived[a, b] = lax.ppermute(chosen[:, b], (CTX, TENSOR), pairs)
    own_cl = place.c // 2
    j = place.t // 2
    stacked = jnp.stack([jnp.stack([arrived[a, b] for b in range(2)]) for a in range(m)])
    result = []
    for micro in range(2):
        halves = []
        for s0 in range(2):
            columns = []
            for r in range(quarter):
                a = own_cl ^ (s0 * quarter + r)
                b = j ^ micro
                columns.append(lax.dynamic_slice(stacked, (a, b, 0, 0), (1, 1, 2 * block, width))[0, 0])
            halves.append(jnp.concatenate(columns, axis=1))
        result.append(jnp.concatenate(halves, axis=0))
    return jnp.stack(result)[None].astype(F32)


def body_any(
    x_in,
    cotangent,
    block_pos,
    norm1_gain,
    norm1_bias,
    norm2_gain,
    norm2_bias,
    qkv_weight,
    qkv_bias,
    dense_weight,
    dense_bias,
    fc1_weight,
    fc1_bias,
    fc2_weight,
    fc2_bias,
):
    place = Place()
    k, n, m, nt = place.k, place.n, place.m, place.nt
    is_first = k == 0
    tokens = x_in.shape[1]
    seq = tokens * n
    block = tokens // nt
    piece = fc1_weight.shape[1]
    hd = dense_weight.shape[2]
    ff = fc1_weight.shape[2]

    stacks = (
        jnp.transpose(qkv_weight[0], (2, 0, 1, 3)).reshape(2, piece, 3 * hd),
        dense_weight[0],
        jnp.transpose(fc1_weight[0].reshape(piece, 2, ff // 2), (1, 0, 2)),
        fc2_weight[0].reshape(2, ff // 2, piece),
    )
    keep = [lax.dynamic_index_in_dim(s, k, 0, keepdims=False) for s in stacks]
    send = [lax.dynamic_index_in_dim(s, 1 - k, 0, keepdims=False) for s in stacks]
    got = [place.over_k(s) for s in send]
    layers = []
    for layer in range(2):
        mine = [jnp.where(k == layer, a, b) for a, b in zip(keep, got)]
        theirs = [place.over_y(s) for s in mine]
        layers.append(
            (
                jnp.concatenate([mine[0], theirs[0]], axis=0),
                (mine[1], theirs[1]),
                jnp.concatenate([mine[2], theirs[2]], axis=0),
                (mine[3], theirs[3]),
            )
        )

    vector = jnp.concatenate(
        [
            norm1_gain[0],
            norm1_bias[0],
            norm2_gain[0],
            norm2_bias[0],
            dense_bias[0],
            fc2_bias[0],
            qkv_bias.reshape(-1),
            fc1_bias.reshape(-1),
        ]
    )
    everything = lax.all_gather(vector, (SECTION, CTX), axis=0).reshape(2, n, -1).astype(F32)
    pair = [
        lax.dynamic_index_in_dim(everything, place.c, 1, keepdims=False),
        lax.dynamic_index_in_dim(everything, place.c ^ m, 1, keepdims=False),
    ]
    smalls = []
    for layer in range(2):
        rows = [jnp.concatenate([p[layer, i * piece : (i + 1) * piece] for p in pair]) for i in range(6)]
        rest = everything[layer, :, 6 * piece :]
        size = 6 * (hd // n)
        qkv_b = rest[:, :size].reshape(n, 3, 2, hd // n)
        qkv_b = jnp.transpose(qkv_b, (2, 1, 0, 3)).reshape(2, 3 * hd)
        fc1_b = rest[:, size:].reshape(2, ff // 2)
        smalls.append(
            {
                "g1": rows[0],
                "b1": rows[1],
                "g2": rows[2],
                "b2": rows[3],
                "out_bias": rows[4] + rows[5],
                "qkv_bias": lax.dynamic_index_in_dim(qkv_b, k, 0, keepdims=False),
                "fc1_bias": lax.dynamic_index_in_dim(fc1_b, k, 0, keepdims=False),
            }
        )

    code = (place.cl * nt + place.t) * 2 + k
    count = seq // block
    absolute = jnp.arange(count, dtype=jnp.int32) ^ code
    half_rows = nt // 2
    source = absolute // nt
    part = (absolute // half_rows) % 2
    index = ((part ^ k) * n + source) * half_rows + absolute % half_rows
    slot = (absolute[:, None] * block + jnp.arange(block, dtype=jnp.int32)[None]).reshape(-1)
    per_block = seq // block_pos.shape[1]
    order = lax.dynamic_index_in_dim(block_pos, place.y, 0, keepdims=False)
    hit = (slot // per_block)[:, None] == jnp.arange(block_pos.shape[1], dtype=jnp.int32)[None]
    pos = jnp.sum(jnp.where(hit, order[None], 0), axis=1) * per_block + slot % per_block
    tables = rotary_tables(pos) + (pos,)

    h = spread_tokens(place, x_in, index)
    grad = spread_tokens(place, cotangent, index)
    saved = []
    for layer in range(2):
        out, kept = layer_forward(place, h, layers[layer], smalls[layer], tables)
        saved.append(kept)
        if layer == 0:
            h = place.gather_tensor(out.astype(BF))
    results = [None, None]
    for layer in (1, 0):
        grad_in, weights, gains, biases = layer_backward(
            place, grad, layers[layer], smalls[layer], tables, saved[layer]
        )
        results[layer] = (weights, gains, biases)
        if layer == 1:
            grad = place.gather_tensor(grad_in.astype(BF))

    boundary = deliver(place, out, grad_in)

    finals = []
    for i in range(4):
        first, second = results[0][0][i], results[1][0][i]
        to_second = lax.ppermute(second.astype(BF), SECTION, [(0, 1)])
        to_first = lax.ppermute(first.astype(BF), SECTION, [(1, 0)])
        mine = jnp.where(is_first, first, second)
        other = jnp.where(is_first, to_first, to_second).astype(F32)
        finals.append((jnp.where(is_first, mine, other), jnp.where(is_first, other, mine)))
    g_qkv = jnp.stack([v.reshape(piece, 3, hd) for v in finals[0]], axis=2)[None]
    g_out = jnp.stack(finals[1])[None]
    g_up = jnp.concatenate(finals[2], axis=1)[None]
    g_down = jnp.concatenate(finals[3], axis=0)[None]

    def flat(layer):
        _, gains, biases = results[layer]
        return gains.reshape(5, 2, piece), biases

    packed = [jnp.concatenate([flat(layer)[0][:, 1].reshape(-1), flat(layer)[1]]) for layer in range(2)]
    packed = place.over_y(jnp.stack(packed))
    sums = []
    for layer in range(2):
        gains, biases = flat(layer)
        sums.append(jnp.concatenate([gains[:, 0].reshape(-1), biases]) + packed[layer])
    mine = jnp.where(is_first, sums[0], sums[1])
    other = place.over_k(jnp.where(is_first, sums[1], sums[0]))
    norms = mine[: 4 * piece] + other[: 4 * piece]
    total = norms
    for s in range(1, nt):
        total = total + place.over_z(norms, s)
    total = total.reshape(4, 1, piece)
    token_sum = mine[4 * piece : 5 * piece][None]
    tail_mine, tail_other = mine[5 * piece :], other[5 * piece :]
    low = jnp.where(is_first, tail_mine, tail_other)
    high = jnp.where(is_first, tail_other, tail_mine)
    tails = jnp.stack([low, high])
    qkv_b = jnp.transpose(tails[:, : 3 * hd].reshape(2, 3, hd), (1, 0, 2))
    qkv_b = lax.dynamic_slice_in_dim(qkv_b, place.c * (hd // n), hd // n, axis=2)[None]
    fc1_b = lax.dynamic_slice_in_dim(tails[:, 3 * hd :].reshape(-1), place.c * (ff // n), ff // n)[None, None]
    return (
        boundary,
        total[0],
        total[1],
        total[2],
        total[3],
        g_qkv,
        qkv_b,
        g_out,
        token_sum,
        g_up,
        fc1_b,
        g_down,
        token_sum,
    )


SHIFT = ROT // 2


def run(kernel, outs, args, flops=0, grid=None, in_specs=None, out_specs=None, scratch=(), scalars=0, vmem=None):
    moved = sum(a.size * a.dtype.itemsize for a in args) + sum(
        int(jnp.dtype(o.dtype).itemsize) * o.size for o in outs
    )
    params = {"vmem_limit_bytes": (vmem or 40) << 20}
    extra = {}
    if in_specs is not None:
        extra["in_specs"], extra["out_specs"] = in_specs, out_specs
    spec = pltpu.PrefetchScalarGridSpec(
        num_scalar_prefetch=scalars, grid=grid or (), scratch_shapes=list(scratch), **extra
    ) if (grid or scalars or scratch) else None
    keywords = {"grid_spec": spec} if spec is not None else {}
    return pl.pallas_call(
        kernel,
        out_shape=outs,
        compiler_params=pltpu.CompilerParams(**params),
        cost_estimate=pl.CostEstimate(flops=flops, bytes_accessed=moved, transcendentals=0),
        **keywords,
    )(*args)


def scalar(*values):
    return jnp.stack([v.astype(jnp.int32) for v in values])


def shape(dims, dtype=BF):
    return jax.ShapeDtypeStruct(dims, dtype)


def as_columns(rows):
    wide = jnp.concatenate([rows, jnp.zeros((120, rows.shape[1]), F32)], axis=0)
    return wide.T


def row_stats(h_ref, stat_ref, columns):
    @pl.loop(0, h_ref.shape[0] // 64)
    def _(i):
        part = pl.ds(pl.multiple_of(i * 64, 64), 64)
        wide = h_ref[part, :].astype(F32)
        mean = jnp.mean(wide, axis=-1, keepdims=True)
        centre = wide - mean
        spread = jnp.sum(centre * centre, axis=-1, keepdims=True)
        lane = lax.broadcasted_iota(jnp.int32, (64, 128), 1)
        columns[part, :] = jnp.where(lane == 0, mean, spread)

    stat_ref[...] = columns[...].T[:8]


def assemble_kernel(with_stats, *refs):
    pieces, h_ref = refs[:8], refs[8]
    block = pieces[0].shape[0] // 2
    for s in range(4):
        for u in range(2):
            piece = pieces[s * 2 + u]
            for r in range(2):
                start = r * 8 * block + s * 2 * block + u * block
                h_ref[start : start + block, :] = piece[r * block : (r + 1) * block, :]
    if with_stats:
        row_stats(h_ref, refs[9], refs[10])


def assemble(pieces, with_stats):
    rows, width = pieces[0].shape
    outs = [shape((8 * rows, width))]
    if with_stats:
        outs.append(shape((8, 8 * rows), F32))

    def kernel(*refs):
        assemble_kernel(with_stats, *refs)

    return run(kernel, outs, pieces, scratch=[pltpu.VMEM((8 * rows, 128), F32)] if with_stats else ())


EXTRA = 16
ROWS = 32


def pack_tokens(place, v, vectors):
    _, tokens, full = v.shape
    half = tokens // 2
    width = full // 4
    extra = EXTRA if vectors else 0
    count = len(vectors)

    def kernel(at, v_ref, *refs):
        k, c = at[0], at[1]
        lines, outs = refs[:count], refs[count : count + 4]
        rows_ref, line_refs, sem = refs[count + 4], refs[count + 5 : -1], refs[-1]
        rows = pl.ds(pl.multiple_of(k * half, half), half)
        copies = [pltpu.make_async_copy(v_ref.at[:, rows, :], rows_ref, sem.at[0])]
        for i in range(count):
            copies.append(pltpu.make_async_copy(lines[i], line_refs[i], sem.at[i + 1]))
        for copy in copies:
            copy.start()
        for copy in copies:
            copy.wait()
        for d in range(4):
            there = c ^ d
            micro = there // 2
            first = pl.ds(pl.multiple_of(there * width, width), width)
            second = pl.ds(pl.multiple_of((there ^ 2) * width, width), width)
            outs[d][:half, :width] = rows_ref[micro, :, first].astype(BF)
            outs[d][:half, width:] = rows_ref[micro, :, second].astype(BF)
            if extra:
                block = [r[...].astype(F32) for r in line_refs]
                block = jnp.concatenate(block + [jnp.zeros((extra - count, width), F32)], axis=0)
                outs[d][half:, :width] = block.astype(BF)
                outs[d][half:, width:] = jnp.zeros((extra, width), BF)

    return run(
        kernel,
        [shape((half + extra, 2 * width))] * 4,
        [scalar(place.k, place.c), v, *vectors],
        scalars=1,
        in_specs=[pl.BlockSpec(memory_space=pl.ANY)] * (1 + count),
        out_specs=[pl.BlockSpec(memory_space=pltpu.VMEM)] * 4,
        scratch=[pltpu.VMEM((2, half, full), v.dtype)]
        + [pltpu.VMEM(a.shape, a.dtype) for a in vectors]
        + [pltpu.SemaphoreType.DMA((1 + count,))],
        grid=(1,),
        vmem=60,
    )


def send_tokens(place, v, vectors):
    parts = pack_tokens(place, v, vectors)
    got = [parts[0]]
    for d in (1, 2, 3):
        got.append(swap(parts[d], CTX, d))
    out = []
    for g in got:
        out += [g, place.over_k(g)]
    return out


def unpack_tokens(place, pieces, with_stats):
    extra = EXTRA if with_stats else 0
    stride, width = pieces[0].shape
    half = stride - extra
    block = half // 2
    rows = 8 * half
    piece = width // 2

    def kernel(at, *refs):
        got, h_ref, flat, sem = refs[:8], refs[8], refs[-2], refs[-1]
        k, c, t = at[0], at[1], at[2]
        copies = [
            pltpu.make_async_copy(got[i], flat.at[pl.ds(i * stride, stride), :], sem.at[i]) for i in range(8)
        ]
        for copy in copies:
            copy.start()
        for copy in copies:
            copy.wait()
        code = ((c % 2) * 4 + t) * 2 + k
        for j in range(16):
            a = code ^ j
            d = (a // 4) ^ c
            u = ((a // 2) % 2) ^ k
            start = (d * 2 + u) * stride + (a % 2) * block
            h_ref[j * block : (j + 1) * block, :] = flat[pl.ds(pl.multiple_of(start, 16), block), :]
        if with_stats:
            row_stats(h_ref, refs[9], refs[-3])
            for layer in range(2):
                for d in range(4):
                    start = (d * 2 + (k ^ layer)) * stride + half
                    lines = flat[pl.ds(pl.multiple_of(start, 16), extra), :piece].astype(F32)
                    refs[11][layer, d, :, :] = lines
                    if d % 2 == 0:
                        refs[10][layer, :, (d // 2) * piece : (d // 2 + 1) * piece] = lines

    outs = [shape((rows, width))]
    if with_stats:
        outs += [shape((8, rows), F32), shape((2, extra, width), F32), shape((2, 4, extra, piece), F32)]
    return run(
        kernel,
        outs,
        [scalar(place.k, place.c, place.t), *pieces],
        scalars=1,
        in_specs=[pl.BlockSpec(memory_space=pl.ANY)] * 8,
        out_specs=[pl.BlockSpec(memory_space=pltpu.VMEM)] * len(outs),
        scratch=[pltpu.VMEM((rows, 128), F32)] * with_stats
        + [pltpu.VMEM((8 * stride, width), BF), pltpu.SemaphoreType.DMA((8,))],
        grid=(1,),
        vmem=60,
    )


def norm_inputs(h, stat, stat_x, vec):
    rows, width = h.shape
    own = rows // 2

    def kernel(h_ref, stat_ref, stat_x_ref, vec_ref, attn_ref, mlp_ref, cols_ref):
        there = stat_x_ref[...]
        there = jnp.concatenate([there[:, own:], there[:, :own]], axis=1)
        here = stat_ref[...]
        delta = there[0:1] - here[0:1]
        mean = here[0:1] + 0.5 * delta
        spread = here[1:2] + there[1:2] + delta * delta * (width * 0.5)
        inv = lax.rsqrt(spread / (2 * width) + EPS)
        columns = as_columns(jnp.concatenate([mean, inv, jnp.zeros((6, rows), F32)], axis=0))
        cols_ref[...] = columns
        vec = vec_ref[...]

        @pl.loop(0, rows // 64)
        def _(r):
            part = pl.ds(pl.multiple_of(r * 64, 64), 64)
            normed = (h_ref[part, :].astype(F32) - cols_ref[part, 0:1]) * cols_ref[part, 1:2]
            attn_ref[part, :] = (normed * vec[0:1] + vec[1:2]).astype(BF)
            mlp_ref[part, :] = (normed * vec[2:3] + vec[3:4]).astype(BF)

    return run(
        kernel,
        [shape((rows, width)), shape((rows, width)), shape((rows, 128), F32)],
        [h, stat, stat_x, vec],
    )


def product_qkv(attn_in, w_qkv):
    rows, width = attn_in.shape
    own, piece = rows // 2, width // 2
    hd = w_qkv[0].shape[1] // 3

    def kernel(a_ref, w0, w1, q_ref, send_ref):
        first, second = a_ref[:, :piece], a_ref[:, piece:]
        kv = dot(first, w0[:, hd:]) + dot(second, w1[:, hd:])
        send_ref[:, : 2 * hd] = kv.astype(BF)
        q = dot(first, w0[:, :hd]) + dot(second, w1[:, :hd])
        q_ref[...] = q[:own].astype(BF)
        send_ref[:own, 2 * hd :] = q[own:, :128].astype(BF)
        send_ref[own:, 2 * hd :] = q[own:, 128:].astype(BF)

    return run(
        kernel,
        [shape((own, hd)), shape((rows, 2 * hd + 128))],
        [attn_in, *w_qkv],
        flops=6 * rows * width * hd,
    )


def product_up(mlp_in, w_up):
    rows, width = mlp_in.shape
    own, piece = rows // 2, width // 2
    ff = w_up[0].shape[1]

    def kernel(m_ref, w0, w1, own_ref, send_ref):
        for r, ref in ((slice(own, rows), send_ref), (slice(0, own), own_ref)):
            ref[...] = (dot(m_ref[r, :piece], w0[...]) + dot(m_ref[r, piece:], w1[...])).astype(BF)

    return run(kernel, [shape((own, ff))] * 2, [mlp_in, *w_up], flops=2 * rows * width * ff)


def unfold(ref, hd):
    own = ref.shape[0] // 2
    return jnp.concatenate([ref[:own, 2 * hd :], ref[own:, 2 * hd :]], axis=1)


def turn_in(z, tables, inverse):
    cosine, low, high = tables
    lead = z[:, :128]
    left = pltpu.roll(lead, 128 - SHIFT, axis=1)
    right = pltpu.roll(lead, SHIFT, axis=1)
    mixed = left * low + right * high
    lead = lead * cosine - mixed if inverse else lead * cosine + mixed
    return jnp.concatenate([lead, z[:, 128:]], axis=1)


def attention(q_own, kv_own, kv_got, bias, tables, pos_row):
    rows = kv_own.shape[0]
    own, hd = q_own.shape
    scaling = hd**-0.5

    def kernel(qo, kvo, kvg, b_ref, cos_ref, low_ref, high_ref, pos_ref, q_ref, k_ref, v_ref, p_ref, o_ref):
        b = b_ref[0:1, :]
        tab = (cos_ref[...], low_ref[...], high_ref[...])
        q = qo[...].astype(F32) + unfold(kvg, hd).astype(F32) + b[:, :hd]
        q = turn_in(q, tuple(a[:own] for a in tab), False).astype(BF)
        kv = jnp.concatenate(
            [
                kvo[:own, : 2 * hd].astype(F32) + kvg[own:, : 2 * hd].astype(F32),
                kvo[own:, : 2 * hd].astype(F32) + kvg[:own, : 2 * hd].astype(F32),
            ],
            axis=0,
        ) + b[:, hd:]
        k = turn_in(kv[:, :hd], tab, False).astype(BF)
        v = kv[:, hd:].astype(BF)
        q_ref[...], k_ref[...], v_ref[...] = q, k, v
        pos = pos_ref[...]
        column = as_columns(pos)[:own, 0:1]
        scores = dot(q, k, ((1,), (1,))) * scaling
        allowed = column >= pos[0:1, :]
        scores = jnp.where(allowed, scores, MASKED_SCORE)
        top = jnp.max(scores, axis=-1, keepdims=True)
        exps = jnp.where(allowed, jnp.exp(scores - top), 0.0)
        total = jnp.sum(exps, axis=-1, keepdims=True)
        o_ref[...] = (dot(exps.astype(BF), v) / total).astype(BF)
        p_ref[...] = exps / total

    return run(
        kernel,
        [shape((own, hd)), shape((rows, hd)), shape((rows, hd)), shape((own, rows), F32), shape((own, hd))],
        [q_own, kv_own, kv_got, bias, *tables, pos_row],
        flops=4 * own * rows * hd,
    )


def second_products(acts, attns, w_cat):
    own, ff = acts[0].shape
    hd = attns[0].shape[1]
    piece = w_cat[0].shape[1]
    block = own // 8

    half = piece // 2

    def kernel(a0, a1, t0, t1, w0, w1, keep_ref, send_ref):
        @pl.loop(0, 2)
        def _(c):
            cut = pl.ds(pl.multiple_of(c * half, half), half)
            for r, (a, t) in enumerate(((a0, t0), (a1, t1))):
                for j, w in enumerate((w0, w1)):
                    to = pl.ds(pl.multiple_of(j * piece + c * half, half), half)
                    value = (dot(a[...], w[:ff, cut]) + dot(t[...], w[ff:, cut])).astype(BF)
                    for s in range(4):
                        at = (r * 4 + s) * block
                        keep_ref[at : at + block, to] = value[2 * s * block : (2 * s + 1) * block]
                        send_ref[at : at + block, to] = value[(2 * s + 1) * block : (2 * s + 2) * block]

    return run(
        kernel,
        [shape((own, 2 * piece))] * 2,
        [*acts, *attns, *w_cat],
        flops=8 * own * piece * (ff + hd),
    )


def cut_tensor(keeps, gots, small, small_got):
    width = keeps[0].shape[1]
    block = ROWS
    groups = sum(v.shape[0] for v in keeps) // (4 * block)
    lines = groups * block
    extra = 2 * SMALL if small is not None else 0
    count = len(keeps)

    def kernel(*refs):
        own_ref, *sends = refs[-4:]
        at = 0
        for keep_ref, got_ref in zip(refs[:count], refs[count : 2 * count]):
            for first in range(0, keep_ref.shape[0], 4 * block):
                to = slice(at, at + block)
                at += block
                for s in range(4):
                    cut = slice(first + s * block, first + (s + 1) * block)
                    value = keep_ref[cut, :].astype(F32) + got_ref[cut, :].astype(F32)
                    if s == 0:
                        own_ref[to, :] = value
                    else:
                        sends[s - 1][to, :] = value.astype(BF)
        if extra:
            both = refs[2 * count][...] + refs[2 * count + 1][...]
            own_ref[lines : lines + SMALL, :] = both
            both = jnp.concatenate([both, jnp.zeros_like(both)], axis=0).astype(BF)
            for send in sends:
                send[lines:, :] = both

    sent = shape((lines + extra, width))
    kept = shape((lines + extra // 2, width), F32)
    return run(kernel, [kept, sent, sent, sent], [*keeps, *gots] + ([small, small_got] if extra else []))


def sum_tensor(place, keeps, gots, small, small_got):
    own, *sends = cut_tensor(keeps, gots, small, small_got)
    parts = []
    for s, v in enumerate(sends):
        parts.append(place.over_z(v, s + 1))
    return (own, *parts)


def spread_tensor(place, v):
    got = [v]
    for s in (1, 2, 3):
        got.append(place.over_z(v, s))
    out = []
    for g in got:
        out += [g, place.over_k(g)]
    return out


def own_rows(ref, block):
    half = ref.shape[0] // 2
    return jnp.concatenate([ref[:block, :], ref[half : half + block, :]], axis=0)


def residual(own, parts, h, vec, dtype):
    rows, width = own.shape
    block = rows // 2

    def kernel(own_ref, p1, p2, p3, h_ref, vec_ref, out_ref):
        total = own_ref[...] + p1[...].astype(F32) + p2[...].astype(F32) + p3[...].astype(F32)
        out_ref[...] = (own_rows(h_ref, block).astype(F32) + total + vec_ref[4:5, :] + vec_ref[5:6, :]).astype(dtype)

    return run(kernel, [shape((rows, width), dtype)], [own, *parts, h, vec])[0]


def first_grads_attn(grad, w_cat, hd):
    rows, width = grad.shape
    own, piece = rows // 2, width // 2
    total = w_cat[0].shape[0]
    last = ((1,), (1,))

    def kernel(g_ref, w0, w1, own_ref, send_ref):
        lines = pl.ds(total - hd, hd)
        value = dot(g_ref[:, :piece], w0[lines, :], last) + dot(g_ref[:, piece:], w1[lines, :], last)
        own_ref[...] = value[:own].astype(BF)
        send_ref[...] = value[own:].astype(BF)

    return run(kernel, [shape((own, hd))] * 2, [grad, *w_cat], flops=2 * rows * width * hd)


def first_grads_act(grad, w_cat, hd):
    rows, width = grad.shape
    own, piece = rows // 2, width // 2
    ff = w_cat[0].shape[0] - hd
    tile = ff // 4
    last = ((1,), (1,))

    def kernel(g_ref, w0, w1, own_ref, first_ref, second_ref):
        @pl.loop(0, 4)
        def _(i):
            lines = pl.ds(pl.multiple_of(i * tile, tile), tile)
            value = dot(g_ref[:, :piece], w0[lines, :], last) + dot(g_ref[:, piece:], w1[lines, :], last)
            own_ref[:, lines] = value[:own].astype(BF)
            to = pl.ds(pl.multiple_of(lax.rem(i, 2) * tile, tile), tile)

            @pl.when(i < 2)
            def _():
                first_ref[:, to] = value[own:].astype(BF)

            @pl.when(i >= 2)
            def _():
                second_ref[:, to] = value[own:].astype(BF)

    outs = [shape((own, ff)), shape((own, ff // 2)), shape((own, ff // 2))]
    return run(kernel, outs, [grad, *w_cat], flops=2 * rows * width * ff)


def hidden_grads(own, first, second, slope):
    rows, ff = own.shape
    half = ff // 2

    def kernel(own_ref, first_ref, second_ref, slope_ref, out_ref):
        for i, got in enumerate((first_ref, second_ref)):
            cut = slice(i * half, (i + 1) * half)
            value = own_ref[:, cut].astype(F32) + got[...].astype(F32)
            out_ref[:, cut] = (value * slope_ref[:, cut]).astype(BF)

    return run(kernel, [shape((rows, ff))], [own, first, second, slope])[0]


def attention_grads(d_own, d_got, attn_out, probs, queries, keys, values, tables):
    own, hd = queries.shape
    rows = keys.shape[0]
    scaling = hd**-0.5

    def kernel(do, dg, o_ref, p_ref, q_ref, k_ref, v_ref, cos_ref, low_ref, high_ref, out_ref):
        grad = (do[...].astype(F32) + dg[...].astype(F32)).astype(BF)
        row_dot = jnp.sum(grad.astype(F32) * o_ref[...].astype(F32), axis=-1, keepdims=True)
        d_prob = dot(grad, v_ref[...], ((1,), (1,)))
        probs = p_ref[...]
        d_score = (probs * (d_prob - row_dot)).astype(BF)
        tab = (cos_ref[...], low_ref[...], high_ref[...])
        dq = dot(d_score, k_ref[...]) * scaling
        dq = turn_in(dq, tuple(a[:own] for a in tab), True).astype(BF)
        out_ref[:own, 2 * hd :] = dq[:, :128]
        out_ref[own:, 2 * hd :] = dq[:, 128:]
        dk = dot(d_score, q_ref[...], ((0,), (0,))) * scaling
        out_ref[:, :hd] = turn_in(dk, tab, True).astype(BF)
        out_ref[:, hd : 2 * hd] = dot(probs.astype(BF), grad, ((0,), (0,))).astype(BF)

    return run(
        kernel,
        [shape((rows, 2 * hd + 128))],
        [d_own, d_got, attn_out, probs, queries, keys, values, *tables],
        flops=8 * own * rows * hd,
    )[0]


SMALL = 8


def second_grads(r, pre, dkv_own, dkv_got, w_qkv, w_up, h, cols, grad, vec, before):
    rows, width = h.shape
    own = rows // 2
    piece = width // 2
    tile = piece // 2
    block = own // 8
    hd, ff = w_qkv[0].shape[1] // 3, pre.shape[1]
    last = ((1,), (1,))
    at, cross = slice(r * own, (r + 1) * own), slice((1 - r) * own, (2 - r) * own)

    def kernel(p_ref, kvo, kvg, wq0, wq1, wu0, wu1, h_ref, c_ref, g_ref, vec_ref, *refs):
        keep_ref, send_ref, gain_ref, qkv_ref = refs[-4:]
        qkv_ref[:, :hd] = unfold((kvo, kvg)[r], hd)
        both = kvo[at, : 2 * hd].astype(F32) + kvg[cross, : 2 * hd].astype(F32)
        qkv_ref[:, hd:] = both.astype(BF)
        gain_ref[...] = jnp.zeros((SMALL, width), F32) if before is None else refs[0][...]

        @pl.loop(0, 2)
        def _(n):
            lines = pl.ds(pl.multiple_of(n * tile, tile), tile)
            for j in range(2):
                cut = pl.ds(pl.multiple_of(j * piece + n * tile, tile), tile)
                d_mlp = dot(p_ref[...], (wu0, wu1)[j][lines, :], last)
                d_attn = dot(qkv_ref[...], (wq0, wq1)[j][lines, :], last)
                normed = (h_ref[at, cut].astype(F32) - c_ref[at, 0:1]) * c_ref[at, 1:2]
                both = (d_attn * vec_ref[0:1, cut] + d_mlp * vec_ref[2:3, cut]).astype(BF)
                for s in range(4):
                    to = slice(s * block, (s + 1) * block)
                    keep_ref[to, cut] = both[2 * s * block : (2 * s + 1) * block]
                    send_ref[to, cut] = both[(2 * s + 1) * block : (2 * s + 2) * block]
                add = (d_attn * normed, d_attn, d_mlp * normed, d_mlp, g_ref[at, cut].astype(F32))
                for i, v in enumerate(add):
                    gain_ref[i : i + 1, cut] += jnp.sum(v, axis=0, keepdims=True)

        gain_ref[5:6, :ff] += jnp.sum(p_ref[...].astype(F32), axis=0, keepdims=True)
        gain_ref[6:7, : 3 * hd] += jnp.sum(qkv_ref[...].astype(F32), axis=0, keepdims=True)

    return run(
        kernel,
        [shape((own // 2, width)), shape((own // 2, width)), shape((SMALL, width), F32)],
        [pre, dkv_own, dkv_got, *w_qkv, *w_up, h, cols, grad, vec] + ([] if before is None else [before]),
        flops=rows * width * (3 * hd + ff),
        scratch=[pltpu.VMEM((own, 3 * hd), BF)],
    )


def own_stats(halves, small, small_got, h, cols):
    width = small.shape[1]
    block, rows = ROWS, 2 * ROWS
    count = 4 * len(halves)

    def kernel(*refs):
        groups = [refs[i : i + 4] for i in range(0, count, 4)]
        s_ref, sg_ref, h_ref, c_ref, comb_ref, sums_ref, small_ref = refs[count:]
        each = rows // len(groups)
        add = lambda parts: sum(p[:each, :].astype(F32) for p in parts)
        comb = jnp.concatenate([add(parts) for parts in groups], axis=0)
        comb_ref[...] = comb
        c = own_rows(c_ref, block)
        normed = (own_rows(h_ref, block).astype(F32) - c[:, 0:1]) * c[:, 1:2]
        lane = lax.broadcasted_iota(jnp.int32, (rows, 128), 1)
        first = jnp.sum(comb, axis=-1, keepdims=True)
        second = jnp.sum(comb * normed, axis=-1, keepdims=True)
        sums_ref[...] = jnp.where(lane == 0, first, second)
        total = groups[-1][0][each:, :]
        for p in groups[-1][1:]:
            total = total + p[each:, :].astype(F32)[:SMALL]
        line = lax.broadcasted_iota(jnp.int32, (SMALL, width), 0)
        small_ref[:SMALL, :] = jnp.where(line < 4, total, s_ref[...])
        small_ref[SMALL:, :] = sg_ref[...]

    return run(
        kernel,
        [shape((rows, width), F32), shape((rows, 128), F32), shape((2 * SMALL, width), F32)],
        [p for parts in halves for p in parts] + [small, small_got, h, cols],
    )


def input_grad(comb, sums, got, h, cols, grad):
    rows, width = comb.shape
    block = rows // 2

    def kernel(comb_ref, s_ref, g_ref, h_ref, c_ref, grad_ref, out_ref):
        c = own_rows(c_ref, block)
        normed = (own_rows(h_ref, block).astype(F32) - c[:, 0:1]) * c[:, 1:2]
        there = g_ref[...]
        total = (s_ref[...] + jnp.concatenate([there[block:], there[:block]], axis=0)) / (2 * width)
        change = comb_ref[...] - total[:, 0:1] - normed * total[:, 1:2]
        out_ref[...] = (own_rows(grad_ref, block).astype(F32) + c[:, 1:2] * change).astype(BF)

    return run(kernel, [shape((rows, width))], [comb, sums, got, h, cols, grad])[0]


def sent_out(kernel, outs, args, flops, scratch=()):
    count = len(args)

    def wrapped(*refs):
        results = refs[count : count + len(outs)]
        buffers, rest, sem = refs[count + len(outs) : count + 2 * len(outs)], refs[count + 2 * len(outs) : -1], refs[-1]
        copies = [pltpu.make_async_copy(b, r, sem.at[i]) for i, (b, r) in enumerate(zip(buffers, results))]
        kernel(lambda i: copies[i].start(), *refs[:count], *buffers, *rest)
        for copy in copies:
            copy.wait()

    return run(
        wrapped,
        outs,
        args,
        flops=flops,
        in_specs=[pl.BlockSpec(memory_space=pltpu.VMEM)] * count,
        out_specs=[pl.BlockSpec(memory_space=pl.ANY)] * len(outs),
        scratch=[pltpu.VMEM(o.shape, o.dtype) for o in outs] + list(scratch) + [pltpu.SemaphoreType.DMA((len(outs),))],
        vmem=20,
    )


def grads_cat(acts, attns, grad):
    own, ff = acts[0].shape
    hd = attns[0].shape[1]
    width = grad.shape[1]
    piece = width // 2
    first = ((0,), (0,))

    def kernel(go, a0, a1, t0, t1, g_ref, send_ref, own_ref):
        for n, (j, ref) in enumerate(((1, send_ref), (0, own_ref))):
            cut = slice(j * piece, (j + 1) * piece)
            for lines, left in ((slice(0, ff), (a0, a1)), (slice(ff, ff + hd), (t0, t1))):
                value = dot(left[0][...], g_ref[:own, cut], first) + dot(left[1][...], g_ref[own:, cut], first)
                ref[lines, :] = value.astype(BF)
            go(n)

    outs = [shape((ff + hd, piece))] * 2
    send, mine = sent_out(kernel, outs, [*acts, *attns, grad], 4 * own * width * (ff + hd))
    return mine, send


def grads_up(mlp_in, pres):
    rows, width = mlp_in.shape
    own, piece = rows // 2, width // 2
    ff = pres[0].shape[1]
    first = ((0,), (0,))

    def kernel(go, m_ref, p0, p1, send_ref, own_ref):
        for n, (j, ref) in enumerate(((1, send_ref), (0, own_ref))):
            cut = slice(j * piece, (j + 1) * piece)
            value = dot(m_ref[:own, cut], p0[...], first) + dot(m_ref[own:, cut], p1[...], first)
            ref[...] = value.astype(BF)
            go(n)

    send, mine = sent_out(kernel, [shape((piece, ff))] * 2, [mlp_in, *pres], 2 * rows * width * ff)
    return mine, send


def fill_qkv(out_ref, own_ref, got_ref, hd):
    half = out_ref.shape[0] // 2
    for r in range(2):
        at = slice(r * half, (r + 1) * half)
        cross = slice((1 - r) * half, (2 - r) * half)
        out_ref[at, :hd] = unfold((own_ref, got_ref)[r], hd)
        both = own_ref[at, : 2 * hd].astype(F32) + got_ref[cross, : 2 * hd].astype(F32)
        out_ref[at, hd:] = both.astype(BF)


def grads_qkv(attn_in, dkvq_own, dkvq_got, hd):
    rows, width = attn_in.shape
    piece = width // 2

    def kernel(go, a_ref, do_ref, dg_ref, send_ref, own_ref, full):
        fill_qkv(full, do_ref, dg_ref, hd)
        for n, (j, ref) in enumerate(((1, send_ref), (0, own_ref))):
            value = dot(a_ref[:, j * piece : (j + 1) * piece], full[...], ((0,), (0,)))
            ref[...] = value.astype(BF)
            go(n)

    send, mine = sent_out(
        kernel,
        [shape((piece, 3 * hd))] * 2,
        [attn_in, dkvq_own, dkvq_got],
        6 * rows * width * hd,
        [pltpu.VMEM((rows, 3 * hd), BF)],
    )
    return mine, send


def move(place, outs, arrays, plan, parts):
    count = len(arrays)

    def kernel(at, *refs):
        ins, results = refs[:count], refs[count : count + len(outs)]
        buffers, into, outof = refs[count + len(outs) : -2], refs[-2], refs[-1]
        steps = plan(at[0], ins, results)
        for i, (choices, target) in enumerate(steps):
            for condition, source in choices:
                @pl.when(condition)
                def _():
                    pltpu.make_async_copy(source, buffers[i], into.at[i]).start()

        for i, (choices, target) in enumerate(steps):
            pltpu.make_async_copy(choices[0][1], buffers[i], into.at[i]).wait()
            pltpu.make_async_copy(buffers[i], target, outof.at[i]).start()
        for i, (choices, target) in enumerate(steps):
            pltpu.make_async_copy(buffers[i], target, outof.at[i]).wait()

    anywhere = pl.BlockSpec(memory_space=pl.ANY)
    return run(
        kernel,
        outs,
        [scalar(place.k), *arrays],
        scalars=1,
        in_specs=[anywhere] * count,
        out_specs=[anywhere] * len(outs),
        scratch=[pltpu.VMEM(p, BF) for p in parts]
        + [pltpu.SemaphoreType.DMA((len(parts),)), pltpu.SemaphoreType.DMA((len(parts),))],
        grid=(1,),
        vmem=60,
    )


def pick_up(place, fc1, got, layer):
    piece, full = fc1.shape
    half, part = full // 2, piece // 4

    def plan(k, refs, outs):
        steps = []
        for i in range(4):
            lines = pl.ds(i * part, part)
            source = lambda ref, j: ref.at[lines, pl.ds(j * half, half)]
            choices = ((k == layer, source(refs[0], layer)), (k != layer, source(refs[1], 1 - layer)))
            steps.append((choices, outs[0].at[lines, :]))
        return steps

    return move(place, [shape((piece, half))], [fc1, got], plan, [(part, half)] * 4)[0]


def pick_qkv(place, keep, got, layer):
    piece, width = keep.shape
    part = piece // 4

    def plan(k, refs, outs):
        steps = []
        for i in range(4):
            lines = pl.ds(i * part, part)
            choices = ((k == layer, refs[0].at[lines, :]), (k != layer, refs[1].at[lines, :]))
            steps.append((choices, outs[0].at[lines, :]))
        return steps

    return move(place, [shape((piece, width))], [keep, got], plan, [(part, width)] * 4)[0]


def pick_cat(place, fc2, dense, down_got, dense_got, layer):
    full, piece = fc2.shape
    ff, hd = full // 2, dense.shape[0] // 2
    tiles = ff // hd

    def plan(k, refs, outs):
        steps = []
        for i in range(tiles + 1):
            mine, other = (refs[0], refs[2]) if i < tiles else (refs[1], refs[3])
            source = lambda ref, j: ref.at[pl.ds(j * ff + i * hd if i < tiles else j * hd, hd), :]
            choices = ((k == layer, source(mine, layer)), (k != layer, source(other, 1 - layer)))
            steps.append((choices, outs[0].at[pl.ds(i * hd, hd), :]))
        return steps

    return move(place, [shape((ff + hd, piece))], [fc2, dense, down_got, dense_got], plan, [(hd, piece)] * (tiles + 1))[0]


def stream(place, arrays, chunk, count, outs, buffers, emit, wanted):
    flat = [a for pair in arrays for a in pair]
    lanes = [pair[0].shape[1] for pair in arrays]
    kinds = [pair[0].dtype for pair in arrays]
    per = max(len(emit_views) for emit_views in [wanted])

    def kernel(at, *refs):
        ins = refs[: len(flat)]
        results = refs[len(flat) : len(flat) + len(outs)]
        rest = refs[len(flat) + len(outs) :]
        held, made, into, outof = rest[: len(arrays)], rest[len(arrays)], rest[-2], rest[-1]
        k = at[0]
        where = [0]
        for pair in arrays:
            where.append(where[-1] + len(pair))

        def fetch(n, i, layer):
            source = ins[where[n] + (layer if len(arrays[n]) == 2 else 0)]
            return pltpu.make_async_copy(source.at[pl.ds(i * chunk, chunk), :], held[n].at[i], into.at[n, i])

        for i in range(count):
            for n, pair in enumerate(arrays):
                if len(pair) == 1:
                    fetch(n, i, 0).start()
                    continue
                for layer in range(2):
                    @pl.when(k == layer)
                    def _():
                        fetch(n, i, layer).start()

        for i in range(count):
            for n in range(len(arrays)):
                fetch(n, i, 0).wait()
            for layer in range(2):
                @pl.when(k == layer)
                def _():
                    emit(layer, i, [h.at[i] for h in held], made.at[i])

            for j, view in enumerate(wanted):
                source, target = view(i, made.at[i], results)
                pltpu.make_async_copy(source, target, outof.at[i, j]).start()
        for i in range(count):
            for j, view in enumerate(wanted):
                source, target = view(i, made.at[i], results)
                pltpu.make_async_copy(source, target, outof.at[i, j]).wait()

    anywhere = pl.BlockSpec(memory_space=pl.ANY)
    return run(
        kernel,
        outs,
        [scalar(place.k), *flat],
        scalars=1,
        grid=(1,),
        in_specs=[anywhere] * len(flat),
        out_specs=[anywhere] * len(outs),
        scratch=[pltpu.VMEM((count, chunk, w), d) for w, d in zip(lanes, kinds)]
        + [pltpu.VMEM((count, *buffers[0]), buffers[1])]
        + [pltpu.SemaphoreType.DMA((len(arrays), count)), pltpu.SemaphoreType.DMA((count, per))],
        vmem=60,
    )


def sum_for_owner(place, ours, theirs):
    rows, width = ours[0].shape
    chunk = 256
    swapped = [ours[::-1], theirs[::-1]]

    def emit(layer, i, refs, buffer):
        @pl.loop(0, chunk // 32)
        def _(n):
            at = pl.ds(pl.multiple_of(n * 32, 32), 32)
            buffer[at, :] = (refs[0][at, :].astype(F32) + refs[1][at, :].astype(F32)).astype(BF)

    view = lambda i, buffer, outs: (buffer, outs[0].at[pl.ds(i * chunk, chunk), :])
    return stream(place, swapped, chunk, rows // chunk, [shape((rows, width))], ((chunk, width), BF), emit, [view])[0]


def finish_up(place, ours, theirs, arrived):
    rows, width = arrived.shape
    chunk = rows // 4

    def emit(layer, i, refs, buffer):
        mine, other = pl.ds(layer * width, width), pl.ds((1 - layer) * width, width)

        @pl.loop(0, chunk // 32)
        def _(n):
            at = pl.ds(pl.multiple_of(n * 32, 32), 32)
            buffer[at, mine] = refs[0][at, :].astype(F32) + refs[1][at, :].astype(F32)
            buffer[at, other] = refs[2][at, :].astype(F32)

    view = lambda i, buffer, outs: (buffer, outs[0].at[pl.ds(i * chunk, chunk), :])
    return stream(
        place,
        [ours, theirs, [arrived]],
        chunk,
        4,
        [shape((rows, 2 * width), F32)],
        ((chunk, 2 * width), F32),
        emit,
        [view],
    )[0]


def finish_cat(place, ours, theirs, arrived, hd):
    rows, width = arrived.shape
    tiles = rows // hd - 1

    def emit(layer, i, refs, buffer):
        @pl.loop(0, hd // 32)
        def _(n):
            at = pl.ds(pl.multiple_of(n * 32, 32), 32)
            buffer[layer, at, :] = refs[0][at, :].astype(F32) + refs[1][at, :].astype(F32)
            buffer[1 - layer, at, :] = refs[2][at, :].astype(F32)

    def view(half):
        def pick(i, buffer, outs):
            lines = pl.ds(i * hd if i < tiles else 0, hd)
            return buffer.at[half], outs[0 if i < tiles else 1].at[half, lines, :]

        return pick

    return stream(
        place,
        [ours, theirs, [arrived]],
        hd,
        tiles + 1,
        [shape((2, tiles * hd, width), F32), shape((2, hd, width), F32)],
        ((2, hd, width), F32),
        emit,
        [view(0), view(1)],
    )


def finish_qkv(place, ours, theirs, arrived):
    rows, width = arrived.shape
    chunk = rows // 4
    lines = 2 * width // 128

    def emit(layer, i, refs, buffer):
        @pl.loop(0, width // 128)
        def _(c):
            cut = pl.ds(pl.multiple_of(c * 128, 128), 128)
            mine = refs[0][:, cut].astype(F32) + refs[1][:, cut].astype(F32)
            buffer[pl.ds(2 * c + layer, chunk, stride=lines), :] = mine
            buffer[pl.ds(2 * c + 1 - layer, chunk, stride=lines), :] = refs[2][:, cut].astype(F32)

    view = lambda i, buffer, outs: (buffer, outs[0].at[pl.ds(i * chunk * lines, chunk * lines), :])
    out = stream(
        place,
        [ours, theirs, [arrived]],
        chunk,
        4,
        [shape((rows * lines, 128), F32)],
        ((chunk * lines, 128), F32),
        emit,
        [view],
    )[0]
    hd = width // 3
    out = out.reshape(rows, 3, hd // 128, 2, 128)
    return jnp.transpose(out, (0, 1, 3, 2, 4)).reshape(1, rows, 3, 2, hd)


def deliver_two(place, out, out_got, grad_in, grad_got):
    rows, width = out.shape
    block, half = rows // 2, width // 2
    n, m, nt = place.n, place.m, place.nt

    def split(at, o_ref, og_ref, g_ref, gg_ref, *sends):
        k, c, t = at[0], at[1], at[2]
        for core, (mine, other) in enumerate(((g_ref, gg_ref), (o_ref, og_ref))):
            @pl.when(k == core)
            def _():
                low, high = (mine, other) if core == 0 else (other, mine)
                for a in range(2):
                    rel = (t % 2) ^ a ^ (c % 2)
                    lines = pl.ds(pl.multiple_of(rel * block, block), block)
                    for b in range(2):
                        cut = slice(b * half, (b + 1) * half)
                        sends[a * 2 + b][:block, :] = low[lines, cut]
                        sends[a * 2 + b][block:, :] = high[lines, cut]

    spot = scalar(place.k, place.c, place.t)
    sends = run(split, [shape((2 * block, half))] * 4, [spot, out, out_got, grad_in, grad_got], scalars=1)
    arrived = []
    for a in range(2):
        for b in range(2):
            pairs = []
            for c in range(n):
                for t in range(nt):
                    y, cl = c // m, c % m
                    pairs.append((c * nt + t, (((t % 2) ^ a) * 2 + t // 2) * nt + (y ^ b) * 2 + cl))
            arrived.append(lax.ppermute(sends[a * 2 + b], (CTX, TENSOR), pairs))

    def join(at, *refs):
        got, out_ref = refs[:4], refs[4]
        c, t = at[1], at[2]
        for a in range(2):
            for b in range(2):
                first, micro = (c // 2) ^ a, (t // 2) ^ b
                lines = pl.ds(pl.multiple_of(first * 2 * block, 2 * block), 2 * block)
                out_ref[micro, lines, :] = got[a * 2 + b][...].astype(F32)

    return run(join, [shape((2, 4 * block, half), F32)], [spot, *arrived], scalars=1)[0][None]


def split_heads(place, qkv_weight):
    piece, _, _, hd = qkv_weight.shape
    lines = qkv_weight.reshape(piece, 3, 2, hd // 128, 128)
    lines = jnp.transpose(lines, (0, 1, 3, 2, 4)).reshape(-1, 128)
    count = 6 * hd // 128

    def kernel(at, in_ref, keep_ref, send_ref, wide):
        wide[...] = in_ref[...].astype(F32)
        for chunk in range(count // 2):
            columns = pl.ds(chunk * 128, 128)
            keep_ref[:, columns] = wide[pl.ds(2 * chunk + at[0], piece, stride=count), :].astype(BF)
            send_ref[:, columns] = wide[pl.ds(2 * chunk + 1 - at[0], piece, stride=count), :].astype(BF)

    return run(
        kernel,
        [shape((piece, 3 * hd))] * 2,
        [scalar(place.k), lines],
        scalars=1,
        scratch=[pltpu.VMEM(lines.shape, F32)],
    )


def body_two(
    x_in,
    cotangent,
    block_pos,
    norm1_gain,
    norm1_bias,
    norm2_gain,
    norm2_bias,
    qkv_weight,
    qkv_bias,
    dense_weight,
    dense_bias,
    fc1_weight,
    fc1_bias,
    fc2_weight,
    fc2_bias,
):
    place = Place()
    k, n, nt = place.k, place.n, place.nt
    is_first = k == 0
    tokens = x_in.shape[1]
    seq = tokens * n
    block = tokens // nt
    piece = fc1_weight.shape[1]
    hd = dense_weight.shape[2]
    ff = fc1_weight.shape[2] // 2

    def x_swap(v):
        return place.over_x(v, 0)

    def y_swap(v):
        return place.over_y(v)

    heads_bias = jnp.pad(qkv_bias.reshape(1, -1), ((0, 0), (0, piece - qkv_bias.size)))
    vectors = [norm1_gain, norm1_bias, norm2_gain, norm2_bias, dense_bias, fc2_bias, fc1_bias[0], heads_bias]
    x_pieces = send_tokens(place, x_in, vectors)

    fc1, fc2 = fc1_weight[0], fc2_weight[0]
    dense = dense_weight.reshape(2 * hd, piece)

    def k_swap(v):
        return place.over_k(v)

    up_got = k_swap(fc1)
    head_keep, head_send = split_heads(place, qkv_weight[0])
    head_got = k_swap(head_send)
    down_got, dense_got = k_swap(fc2), k_swap(dense)
    layers = []
    for layer in range(2):
        mine_q = pick_qkv(place, head_keep, head_got, layer)
        mine_u = pick_up(place, fc1, up_got, layer)
        mine_c = pick_cat(place, fc2, dense, down_got, dense_got, layer)
        layers.append(((mine_q, y_swap(mine_q)), (mine_u, y_swap(mine_u)), (mine_c, y_swap(mine_c))))

    code = (place.cl * nt + place.t) * 2 + k
    absolute = jnp.arange(seq // block, dtype=jnp.int32) ^ code
    slot = (absolute[:, None] * block + jnp.arange(block, dtype=jnp.int32)[None]).reshape(-1)
    per_block = seq // block_pos.shape[1]
    order = jnp.where(place.y == 0, block_pos[0], block_pos[1])
    hit = (slot // per_block)[:, None] == jnp.arange(block_pos.shape[1], dtype=jnp.int32)[None]
    pos = jnp.sum(jnp.where(hit, order[None], 0), axis=1) * per_block + slot % per_block
    pos_row = jnp.broadcast_to(pos.astype(F32)[None], (8, seq))
    cosine, sine = rotary_tables(pos)
    blank = jnp.zeros((seq, 128 - ROT), F32)
    empty = jnp.zeros((seq, SHIFT), F32)
    tables = (
        jnp.concatenate([cosine, blank + 1.0], axis=1),
        jnp.concatenate([-sine[:, :SHIFT], empty, blank], axis=1),
        jnp.concatenate([empty, sine[:, SHIFT:], blank], axis=1),
    )

    h, stat, vecs, lines = unpack_tokens(place, x_pieces, True)
    by_place = jnp.take(lines[:, :, 6:8], jnp.arange(n, dtype=jnp.int32) ^ place.c, axis=1, mode="clip")
    qkv_biases, fc1_biases = [], []
    for layer in range(2):
        fc1_b = by_place[layer, :, 0].reshape(2, ff)
        qkv_b = by_place[layer, :, 1, : qkv_bias.size].reshape(n, 3, 2, hd // n)
        qkv_b = jnp.where(is_first, qkv_b[:, :, 0], qkv_b[:, :, 1])
        qkv_b = jnp.transpose(qkv_b, (1, 0, 2)).reshape(1, 3 * hd)
        qkv_biases.append(jnp.broadcast_to(qkv_b, (8, 3 * hd)))
        fc1_biases.append(jnp.where(is_first, fc1_b[0], fc1_b[1]))

    cot_pieces = send_tokens(place, cotangent, [])
    saved = []
    for layer in range(2):
        w_qkv, w_up, w_cat = layers[layer]
        stat_x = x_swap(stat)
        attn_in, mlp_in, cols = norm_inputs(h, stat, stat_x, vecs[layer])
        q_own, kvq = product_qkv(attn_in, w_qkv)
        f_own, f_send = product_up(mlp_in, w_up)
        kvq_got, f_got = x_swap(kvq), x_swap(f_send)
        queries, keys, values, probs, attn_out = attention(
            q_own, kvq, kvq_got, qkv_biases[layer], tables, pos_row
        )
        pre = f_own.astype(F32) + f_got.astype(F32) + fc1_biases[layer]
        cdf = 0.5 * (1.0 + lax.erf(pre * 0.7071067811865476))
        act = (pre * cdf).astype(BF)
        slope = cdf + pre * jnp.exp(-0.5 * pre * pre) * 0.3989422804014327
        acts = (act, x_swap(act))
        attns = (attn_out, x_swap(attn_out))
        keep, send = second_products(acts, attns, w_cat)
        own, *parts = sum_tensor(place, [keep], [k_swap(send)], None, None)
        out = residual(own, parts, h, vecs[layer], BF)
        saved.append((h, cols, attn_in, mlp_in, queries, keys, values, probs, attn_out, attns, acts, slope))
        if layer == 0:
            pieces = spread_tensor(place, out)
            h, stat = assemble(pieces, True)
    grad = unpack_tokens(place, cot_pieces, False)[0]

    results = [None, None]
    for layer in (1, 0):
        w_qkv, w_up, w_cat = layers[layer]
        h, cols, attn_in, mlp_in, queries, keys, values, probs, attn_out, attns, acts, slope = saved[layer]
        t_own, t_send = first_grads_attn(grad, w_cat, hd)
        t_got = x_swap(t_send)
        a_own, a_first, a_second = first_grads_act(grad, w_cat, hd)
        a_got = (x_swap(a_first), x_swap(a_second))
        dkvq = attention_grads(t_own, t_got, attn_out, probs, queries, keys, values, tables)
        dkvq_got = x_swap(dkvq)
        d_pre = hidden_grads(a_own, *a_got, slope)
        pres = (d_pre, x_swap(d_pre))
        small, halves, keeps, gots = None, [], [], []
        for r in range(2):
            keep, send, small = second_grads(r, pres[r], dkvq, dkvq_got, w_qkv, w_up, h, cols, grad, vecs[layer], small)
            keeps.append(keep)
            gots.append(k_swap(send))
            if r == 1:
                small_got = k_swap(small)
            if layer == 1:
                behind = (small, small_got) if r else (None, None)
                halves.append(sum_tensor(place, keeps[r:], gots[r:], *behind))
        if layer == 0:
            halves.append(sum_tensor(place, keeps, gots, small, small_got))
        comb, sums, small = own_stats(halves, small, small_got, h, cols)
        sums_got = x_swap(sums)
        grad_in = input_grad(comb, sums, sums_got, h, cols, grad)
        cat_own, cat_out = grads_cat(acts, attns, grad)
        up_own, up_out = grads_up(mlp_in, pres)
        qkv_own, qkv_out = grads_qkv(attn_in, dkvq, dkvq_got, hd)
        results[layer] = ((cat_own, y_swap(cat_out)), (up_own, y_swap(up_out)), (qkv_own, y_swap(qkv_out)), small)
        if layer == 1:
            pieces = spread_tensor(place, grad_in)
            grad = assemble(pieces, False)[0]

    boundary = deliver_two(place, out, k_swap(out), grad_in, k_swap(grad_in))

    def to_owner(which):
        ours = [results[layer][which][0] for layer in range(2)]
        theirs = [results[layer][which][1] for layer in range(2)]
        sent = sum_for_owner(place, ours, theirs)
        return ours, theirs, k_swap(sent)

    cat, up, heads = to_owner(0), to_owner(1), to_owner(2)
    g_down, g_out = finish_cat(place, *cat, hd)
    g_down, g_out = g_down.reshape(1, 2 * ff, piece), g_out[None]
    g_up = finish_up(place, *up)[None]
    g_qkv = finish_qkv(place, *heads)

    ours = jnp.where(is_first, results[0][3], results[1][3])
    across = y_swap(ours)
    gains = ours[:5, :piece] + across[:5, piece:]
    total = gains[:4].reshape(4, 1, piece)
    token_sum = gains[4:5]
    mine, other = ours[5:7] + across[5:7], ours[13:15] + across[13:15]
    low, high = jnp.where(is_first, mine, other), jnp.where(is_first, other, mine)
    tails = jnp.stack([low, high])
    qkv_b = tails[:, 1, : 3 * hd].reshape(2, 3, hd)
    qkv_b = jnp.transpose(lax.dynamic_slice_in_dim(qkv_b, place.c * (hd // n), hd // n, axis=2), (1, 0, 2))[None]
    fc1_b = lax.dynamic_slice_in_dim(tails[:, 0].reshape(-1), place.c * (2 * ff // n), 2 * ff // n)[None, None]
    return (
        boundary,
        total[0],
        total[1],
        total[2],
        total[3],
        g_qkv,
        qkv_b,
        g_out,
        token_sum,
        g_up,
        fc1_b,
        g_down,
        token_sum,
    )


def body(*args):
    two = lax.axis_size(CTX) == 4 and lax.axis_size(TENSOR) == 4
    if not two:
        return body_any(*args)
    return body_two(*args)


def solution(mesh):
    in_specs = (
        P(None, CTX, None),
        P(None, CTX, None),
        P(),
        P(SECTION, CTX),
        P(SECTION, CTX),
        P(SECTION, CTX),
        P(SECTION, CTX),
        P(SECTION, CTX, None, TENSOR, None),
        P(SECTION, None, TENSOR, CTX),
        P(SECTION, TENSOR, None, CTX),
        P(SECTION, CTX),
        P(SECTION, CTX, TENSOR),
        P(SECTION, TENSOR, CTX),
        P(SECTION, TENSOR, CTX),
        P(SECTION, CTX),
    )
    out_specs = (
        P(SECTION, None, CTX, TENSOR),
        P(SECTION, CTX),
        P(SECTION, CTX),
        P(SECTION, CTX),
        P(SECTION, CTX),
        P(SECTION, CTX, None, TENSOR, None),
        P(SECTION, None, TENSOR, CTX),
        P(SECTION, TENSOR, None, CTX),
        P(SECTION, CTX),
        P(SECTION, CTX, TENSOR),
        P(SECTION, TENSOR, CTX),
        P(SECTION, TENSOR, CTX),
        P(SECTION, CTX),
    )
    return jax.shard_map(body, mesh=mesh, in_specs=in_specs, out_specs=out_specs, check_vma=False)
```
